32 devices in a mesh: row: 4 (over z), col: 8 (over y, x, core).
Axes of the slice: x: 2, y: 2, z: 4, core: 2. Of those that a mesh axis runs over, the one named last changes fastest.
Arguments:
- picture: float32 [3, 256, 1024], P(None, 'row', 'col'), may hold values from -6 to 6
- membrane: float32 [32, 128, 1024], P('row', 'col'), may hold values from -3 to 3
- dictionary: bfloat16 [1024, 3072], replicated, may hold values from -4 to 4
- momentum: float32 [1024, 3072], P(('row', 'col')), may hold values from -5 to 5
Outputs:
- final_codes: float32 [32, 128, 1024], P('row', 'col')
- new_dictionary: float32 [1024, 3072], P(('row', 'col'))
- new_momentum: float32 [1024, 3072], P(('row', 'col'))
The draws below stay inside these ranges and needn't reach their ends.
All inputs are finite; a program needn't handle non-finite values.
Results may differ from the reference program's by a relative error of at most 0.0032.
Values may be sent and summed in bfloat16 or wider, within the bound.
No kernel may reach another device: no remote copies, remote signals or barrier semaphores. Data moves between devices by JAX's collectives and lax.ppermute only.
A program may use at most 64 MiB of HBM per device.

```python
import jax
import jax.numpy as jnp
from jax import lax

K = 1024
CHANNELS = 3
PATCH_SIDE = 32
STRIDE = 8
SWEEPS = 2
PATCH = 3072
SROWS = 32
SCOLS = 128
HEIGHT = 256
WIDTH = 1024


def block_levels(rng, extent, split, least, largest):
    loudness = 1.0
    for axis_at, parts in split:
        steps = jax.random.uniform(jax.random.fold_in(jax.random.fold_in(rng, 6), axis_at), (parts,), jnp.float32, least / len(split), largest / len(split))
        loudness = loudness * jnp.repeat(jnp.exp(steps), extent[axis_at] // parts).reshape((-1,) + (1,) * (len(extent) - 1 - axis_at))
    return loudness


def scatter_about(rng, shape, deviation, bound, shards=(), kind=jnp.bfloat16):
    loudness = block_levels(rng, shape, shards, -0.22, 0.18) if shards else 1.0
    drawn = jax.random.normal(rng, shape, jnp.float32) * deviation * loudness
    return jnp.minimum(jnp.maximum(drawn, -bound), bound).astype(kind)


def setup_inputs(seed: int = 0) -> dict:
    key_of = jax.random.split(jax.random.key(seed), 5)
    return {
        "picture": scatter_about(key_of[0], (CHANNELS, HEIGHT, WIDTH), 1.0, 6.0, ((1, 4), (2, 8)), jnp.float32),
        "membrane": scatter_about(key_of[1], (SROWS, SCOLS, K), 0.5, 3.0, ((0, 4), (1, 8)), jnp.float32),
        "dictionary": scatter_about(key_of[2], (K, PATCH), 1.0, 4.0),
        "momentum": scatter_about(key_of[3], (K, PATCH), 1.0, 5.0, ((0, 32),), jnp.float32),
    }


THRESHOLD = 0.25
RELAXATION = 0.1
DECAY = 0.9
LEARNING = 0.25
EPSILON = 1e-05

def shrink(potential):
    return potential - jnp.clip(potential, -THRESHOLD, THRESHOLD)

def cells_of(picture):
    channels, height, width_px = picture.shape
    blocked = picture.reshape(channels, height // STRIDE, STRIDE, width_px // STRIDE, STRIDE)
    return blocked.transpose(1, 3, 0, 2, 4).reshape(height // STRIDE, width_px // STRIDE, channels * STRIDE * STRIDE)

def reconstruct(coding, dictionary):
    site_rows, site_cols, atom_count = coding.shape
    span_cells = PATCH_SIDE // STRIDE
    cell_size = CHANNELS * STRIDE * STRIDE
    atom_scale = PATCH ** (-0.5)
    flat_codes = coding.reshape(site_rows * site_cols, atom_count)
    canvas = jnp.zeros((site_rows + span_cells - 1, site_cols + span_cells - 1, cell_size), jnp.float32)
    for row_off in range(span_cells):
        for col_off in range(span_cells):
            first_col = (row_off * span_cells + col_off) * cell_size
            placed = jnp.dot(flat_codes, dictionary[:, first_col:first_col + cell_size], preferred_element_type=jnp.float32) * atom_scale
            canvas = canvas.at[row_off:row_off + site_rows, col_off:col_off + site_cols].add(placed.reshape(site_rows, site_cols, cell_size))
    return canvas[:site_rows, :site_cols]

def windows(residual):
    site_rows, site_cols, cell_size = residual.shape
    span_cells = PATCH_SIDE // STRIDE
    padded = jnp.pad(residual, ((0, span_cells - 1), (0, span_cells - 1), (0, 0)))
    return [padded[row_off:row_off + site_rows, col_off:col_off + site_cols].reshape(site_rows * site_cols, cell_size) for row_off in range(span_cells) for col_off in range(span_cells)]

def reference(picture, membrane, dictionary, momentum):
    pixels = cells_of(picture)
    site_rows, site_cols, atom_count = membrane.shape
    cell_size = CHANNELS * STRIDE * STRIDE
    atom_scale = PATCH ** (-0.5)
    potential = membrane
    for repeat in range(SWEEPS):
        active = shrink(potential)
        coding = active.astype(jnp.bfloat16)
        residual = (pixels - reconstruct(coding, dictionary)).astype(jnp.bfloat16)
        drive_term = jnp.zeros((site_rows * site_cols, atom_count), jnp.float32)
        for index_block, window in enumerate(windows(residual)):
            first_col = index_block * cell_size
            drive_term = drive_term + lax.dot_general(window, dictionary[:, first_col:first_col + cell_size], (((1,), (1,)), ((), ())), preferred_element_type=jnp.float32)
        drive_term = drive_term * atom_scale
        potential = potential + RELAXATION * (drive_term.reshape(site_rows, site_cols, atom_count) + active - potential)
    final_codes = shrink(potential)
    coding = final_codes.astype(jnp.bfloat16)
    residual = (pixels - reconstruct(coding, dictionary)).astype(jnp.bfloat16)
    flat_codes = coding.reshape(site_rows * site_cols, atom_count)
    pieces = [lax.dot_general(flat_codes, window, (((0,), (0,)), ((), ())), preferred_element_type=jnp.float32) * atom_scale for window in windows(residual)]
    learning = jnp.concatenate(pieces, axis=1)
    new_momentum = DECAY * momentum + learning
    weights = dictionary.astype(jnp.float32) + LEARNING * new_momentum
    new_dictionary = weights * lax.rsqrt(lax.optimization_barrier(jnp.mean(weights * weights, axis=1, keepdims=True)) + EPSILON)
    return (final_codes, new_dictionary, new_momentum)
```

```python
import functools

import jax
import jax.numpy as jnp
from jax import lax
from jax.experimental import pallas as pl
from jax.experimental.pallas import tpu as pltpu
from jax.sharding import Mesh
from jax.sharding import PartitionSpec as P

PATCH_SIDE = 32
STRIDE = 8
SWEEPS = 2
SPAN = PATCH_SIDE // STRIDE
MARGIN = SPAN - 1

THRESHOLD = 0.25
RELAXATION = 0.1
DECAY = 0.9
LEARNING = 0.25
EPSILON = 1e-05

F32 = jnp.float32
BF16 = jnp.bfloat16
VMEM = pl.BlockSpec(memory_space=pltpu.VMEM)
SMEM = pl.BlockSpec(memory_space=pltpu.SMEM)
HBM = pl.BlockSpec(memory_space=pl.ANY)
PARAMS = pltpu.CompilerParams(vmem_limit_bytes=56 * 1024 * 1024)


def up_to(value, step):
    return -(-value // step) * step


def shrink(potential):
    return potential - jnp.clip(potential, -THRESHOLD, THRESHOLD)


def cells_of(picture):
    channels, height, width_px = picture.shape
    blocked = picture.reshape(channels, height // STRIDE, STRIDE, width_px // STRIDE, STRIDE)
    return blocked.transpose(1, 3, 0, 2, 4).reshape(
        (height // STRIDE) * (width_px // STRIDE), channels * STRIDE * STRIDE
    )


class Sizes:
    def __init__(self, site_rows, site_cols, atoms, patch_len):
        self.rows, self.cols, self.atoms, self.patch = site_rows, site_cols, atoms, patch_len
        self.cell = patch_len // (SPAN * SPAN)
        self.band = SPAN * self.cell
        self.sites = site_rows * site_cols
        self.tall = site_rows + MARGIN
        self.wide = site_cols + MARGIN
        self.wide_pad = up_to(self.wide, 8)
        self.tall_pad = up_to(self.tall, 16)
        self.lanes = up_to(self.cell, 128)
        self.scale = patch_len ** (-0.5)


def dictionary_copies(source, target, sems, z):
    return [
        pltpu.make_async_copy(
            source.at[:, i * z.band : (i + 1) * z.band],
            target.at[:, i * z.band : (i + 1) * z.band],
            sems.at[i],
        )
        for i in range(SPAN)
    ]


def reconstruct(z, coding, dic, pixels, edges, tall_sum, own, left, right, ready=None):
    tall_sum[z.sites :, :] = jnp.zeros((z.tall * z.cols - z.sites, z.band), F32)
    for i in range(SPAN):
        if ready is not None:
            ready(i)
        placed = jnp.dot(
            coding, dic[:, i * z.band : (i + 1) * z.band], preferred_element_type=F32
        )
        start = i * z.cols
        if i == 0:
            tall_sum[0 : z.sites, :] = placed
        else:
            tall_sum[start : start + z.sites, :] += placed
    own[...] = jnp.zeros((z.tall, z.wide_pad, z.lanes), F32)
    own[0 : z.rows, 0 : z.cols, 0 : z.cell] = pixels[...].reshape(z.rows, z.cols, z.cell)
    for j in range(SPAN):
        part = tall_sum[:, j * z.cell : (j + 1) * z.cell].reshape(z.tall, z.cols, z.cell)
        own[:, j : j + z.cols, 0 : z.cell] -= part * z.scale

    @pl.when(edges[0] == 1)
    def _():
        own[z.rows :] = jnp.zeros((MARGIN, z.wide_pad, z.lanes), F32)

    @pl.when(edges[1] == 1)
    def _():
        own[:, z.cols :] = jnp.zeros((z.tall, z.wide_pad - z.cols, z.lanes), F32)

    for c in range(MARGIN):
        left[c, 0 : z.tall, :] = own[:, c, :]
        right[c, 0 : z.tall, :] = own[:, z.cols + c, :]


def first_kernel(z, edges, membrane, pixels, source, own, left, right, dic, tall_sum, sems):
    copies = dictionary_copies(source, dic, sems, z)
    for copy in copies:
        copy.start()
    coding = shrink(membrane[...]).astype(BF16)
    reconstruct(
        z, coding, dic, pixels, edges, tall_sum, own, left, right, lambda i: copies[i].wait()
    )


def side_kernel(z, own, from_left, from_right, joined, up, down):
    joined[...] = own[...]
    for c in range(MARGIN):
        joined[:, c, :] += from_left[c, 0 : z.tall, :]
        joined[:, z.cols + c, :] += from_right[c, 0 : z.tall, :]
    up[...] = joined[0:MARGIN]
    down[...] = joined[z.rows :]


def windows_of(z, whole, wide_part, first_row, row_stride):
    for j in range(SPAN):
        part = whole[:, j : j + z.cols, 0 : z.cell].astype(BF16)
        for p in range(z.tall):
            wide_part[
                pl.ds(p * row_stride + first_row, z.cols), j * z.cell : (j + 1) * z.cell
            ] = part[p]


def sweep_kernel(
    z, last, groups, edges, potential, joined, from_above, from_below, pixels, source, *rest
):
    if last:
        new_potential, own, left, right, shared, dic, tall_sum, whole, wide_part, sems = rest
    else:
        new_potential, own, left, right, dic, tall_sum, whole, wide_part, sems = rest
    copies = dictionary_copies(source, dic, sems, z)
    for copy in copies:
        copy.start()
    whole[...] = joined[...]
    whole[0:MARGIN] += from_above[...]
    whole[z.rows :] += from_below[...]
    windows_of(z, whole, wide_part, 0, z.cols)
    drive = None
    for i in range(SPAN):
        copies[i].wait()
        term = lax.dot_general(
            wide_part[i * z.cols : i * z.cols + z.sites, :],
            dic[:, i * z.band : (i + 1) * z.band],
            (((1,), (1,)), ((), ())),
            preferred_element_type=F32,
        )
        drive = term if drive is None else drive + term
    old = potential[...]
    updated = old + RELAXATION * (drive * z.scale + shrink(old) - old)
    active = shrink(updated)
    coding = active.astype(BF16)
    if last:
        new_potential[...] = active
        rows_n, cores_n, owned = groups
        span = z.atoms // rows_n
        src = lax.broadcasted_iota(jnp.int32, (span, span), 0)
        dst = lax.broadcasted_iota(jnp.int32, (span, span), 1)
        per_core = span // cores_n
        core, rem = dst // per_core, dst % per_core
        wanted = (rem // owned) * (owned * cores_n) + core * owned + rem % owned
        order = (src == wanted).astype(F32).astype(BF16)
        for r in range(rows_n):
            sorted_codes = jnp.dot(
                coding[:, r * span : (r + 1) * span], order, preferred_element_type=F32
            ).astype(BF16)
            for k in range(cores_n):
                shared[r * cores_n + k] = sorted_codes[:, k * per_core : (k + 1) * per_core]
    else:
        new_potential[...] = updated
    reconstruct(z, coding, dic, pixels, edges, tall_sum, own, left, right)


def pack_kernel(z, own, from_left, from_right, packed, joined):
    joined[...] = own[...]
    for c in range(MARGIN):
        joined[:, c, :] += from_left[c, 0 : z.tall, :]
        joined[:, z.cols + c, :] += from_right[c, 0 : z.tall, :]
    for p in range(z.tall):
        packed[p * z.cols : (p + 1) * z.cols, :] = joined[p, 0 : z.cols, :].astype(BF16)
    base = z.tall * z.cols
    packed[base:, :] = jnp.zeros((MARGIN * z.tall_pad, z.lanes), BF16)
    for c in range(MARGIN):
        start = base + c * z.tall_pad
        packed[start : start + z.tall, :] = joined[:, z.cols + c, :].astype(BF16)


def learn_kernel(z, groups, shared, packed, partial, whole, wide_part, codes):
    rows_n, cores_n, _ = groups
    members = rows_n * cores_n
    stride = members * z.cols
    base = z.tall * z.cols

    def unpack(d, low, high):
        main = packed[d, low * z.cols : high * z.cols, :].astype(F32)
        main = main.reshape(high - low, z.cols, z.lanes)
        side = [
            packed[d, base + c * z.tall_pad : base + (c + 1) * z.tall_pad, :].astype(F32)[low:high]
            for c in range(MARGIN)
        ]
        return main, side

    def add(d, low, high, at, first):
        main, side = unpack(d, low, high)
        n = high - low
        if first:
            whole[at : at + n, 0 : z.cols, :] = main
        else:
            whole[at : at + n, 0 : z.cols, :] += main
        for c in range(MARGIN):
            if first:
                whole[at : at + n, z.cols + c, :] = side[c]
            else:
                whole[at : at + n, z.cols + c, :] += side[c]

    for r in range(rows_n):
        for k in range(cores_n):
            d = r * cores_n + k
            add(d, 0, z.tall, 0, True)
            if r > 0:
                add(d - cores_n, z.rows, z.tall, 0, False)
            if r + 1 < rows_n:
                add(d + cores_n, 0, MARGIN, z.rows, False)
            windows_of(z, whole, wide_part, d * z.cols, stride)
            for i in range(z.rows):
                codes[i * stride + d * z.cols : i * stride + (d + 1) * z.cols, :] = shared[
                    d, i * z.cols : (i + 1) * z.cols, :
                ]
    count = z.rows * stride
    across = codes[...].astype(F32).T.astype(BF16)
    for i in range(SPAN):
        term = jnp.dot(
            across, wide_part[i * stride : i * stride + count, :], preferred_element_type=F32
        )
        partial[:, i * z.band : (i + 1) * z.band] = (term * z.scale).astype(BF16)


def finish_kernel(parts, momentum, atoms, new_dictionary, new_momentum):
    learning = parts[0].astype(F32)
    for i in range(1, parts.shape[0]):
        learning = learning + parts[i].astype(F32)
    momentum_out = DECAY * momentum[...] + learning
    new_momentum[...] = momentum_out
    weights = atoms[...].astype(F32) + LEARNING * momentum_out
    power = jnp.mean(weights * weights, axis=1, keepdims=True)
    new_dictionary[...] = weights * lax.rsqrt(power + EPSILON)


def call(kernel, outs, inputs, specs, scratch, name):
    return pl.pallas_call(
        kernel,
        out_shape=[jax.ShapeDtypeStruct(s, d) for s, d in outs],
        in_specs=specs,
        out_specs=[VMEM] * len(outs),
        scratch_shapes=scratch,
        compiler_params=PARAMS,
        name=name,
    )(*inputs)


def shards(picture, membrane, dictionary, momentum):
    site_rows, site_cols, atom_count = membrane.shape
    z = Sizes(site_rows, site_cols, atom_count, dictionary.shape[1])
    rows_n, yx_n, cores_n = (lax.axis_size(a) for a in ("row", "yx", "core"))
    cols_n = yx_n * cores_n
    owned = momentum.shape[0]
    groups = (rows_n, cores_n, owned)
    row_at = lax.axis_index("row")
    col_at = lax.axis_index(("yx", "core"))
    edges = jnp.stack([row_at == rows_n - 1, col_at == cols_n - 1]).astype(jnp.int32)
    pixels = cells_of(picture)

    def along(axis, n, block, distance):
        return lax.ppermute(
            block, axis, [(i - distance, i) for i in range(n) if 0 <= i - distance < n]
        )

    def sideways(left, right):
        return (
            along(("yx", "core"), cols_n, right, 1),
            along(("yx", "core"), cols_n, left, -1),
        )

    own_s = (z.tall, z.wide_pad, z.lanes)
    edge_s = (MARGIN, z.tall_pad, z.lanes)
    rim_s = (MARGIN, z.wide_pad, z.lanes)
    dic_v = pltpu.VMEM((atom_count, z.patch), BF16)
    tall_v = pltpu.VMEM((z.tall * z.cols, z.band), F32)
    whole_v = pltpu.VMEM(own_s, F32)
    wide_v = pltpu.VMEM((z.tall * z.cols, z.band), BF16)
    sems = pltpu.SemaphoreType.DMA((SPAN,))
    sides = [(own_s, F32), (edge_s, F32), (edge_s, F32)]

    potential = membrane.reshape(z.sites, atom_count)
    own, left, right = call(
        functools.partial(first_kernel, z),
        sides,
        (edges, potential, pixels, dictionary),
        [SMEM, VMEM, VMEM, HBM],
        [dic_v, tall_v, sems],
        "first",
    )
    for repeat in range(SWEEPS):
        last = repeat == SWEEPS - 1
        from_left, from_right = sideways(left, right)
        joined, up, down = call(
            functools.partial(side_kernel, z),
            [(own_s, F32), (rim_s, F32), (rim_s, F32)],
            (own, from_left, from_right),
            [VMEM] * 3,
            [],
            "side",
        )
        from_above = along("row", rows_n, down, 1)
        from_below = along("row", rows_n, up, -1)
        outs = [((z.sites, atom_count), F32)] + sides
        if last:
            members = rows_n * cores_n
            outs = outs + [((members, z.sites, atom_count // members), BF16)]
        results = call(
            functools.partial(sweep_kernel, z, last, groups),
            outs,
            (edges, potential, joined, from_above, from_below, pixels, dictionary),
            [SMEM, VMEM, VMEM, VMEM, VMEM, VMEM, HBM],
            [dic_v, tall_v, whole_v, wide_v, sems],
            "sweep",
        )
        potential, own, left, right = results[:4]
    final_codes = potential.reshape(membrane.shape)
    shared = results[4]
    members = rows_n * cores_n
    shared = lax.all_to_all(shared, ("row", "core"), 0, 0, tiled=True)
    from_left, from_right = sideways(left, right)
    packed_rows = z.tall * z.cols + MARGIN * z.tall_pad
    (packed,) = call(
        functools.partial(pack_kernel, z),
        [((packed_rows, z.lanes), BF16)],
        (own, from_left, from_right),
        [VMEM] * 3,
        [whole_v],
        "pack",
    )
    packed = lax.all_gather(packed, ("row", "core"), axis=0, tiled=False)
    (partial,) = call(
        functools.partial(learn_kernel, z, groups),
        [((atom_count // members, z.patch), BF16)],
        (shared, packed),
        [VMEM] * 2,
        [
            whole_v,
            pltpu.VMEM((z.tall * members * z.cols, z.band), BF16),
            pltpu.VMEM((members * z.sites, atom_count // members), BF16),
        ],
        "learn",
    )
    parts = lax.all_to_all(
        partial.reshape(yx_n, owned, z.patch), "yx", 0, 0, tiled=True
    )
    atoms = lax.dynamic_slice_in_dim(dictionary, (row_at * cols_n + col_at) * owned, owned, 0)
    new_dictionary, new_momentum = call(
        finish_kernel,
        [(momentum.shape, F32), (momentum.shape, F32)],
        (parts, momentum, atoms),
        [VMEM] * 3,
        [],
        "finish",
    )
    return (final_codes, new_dictionary, new_momentum)


def solution(mesh):
    rows_n, cols_n = (mesh.shape["row"], mesh.shape["col"])
    cores_n = 2 if cols_n % 2 == 0 else 1
    split = Mesh(
        mesh.devices.reshape(rows_n, cols_n // cores_n, cores_n), ("row", "yx", "core")
    )
    col = ("yx", "core")
    return jax.shard_map(
        shards,
        mesh=split,
        in_specs=(P(None, "row", col), P("row", col, None), P(), P(("row",) + col, None)),
        out_specs=(P("row", col, None), P(("row",) + col, None), P(("row",) + col, None)),
        check_vma=False,
    )
```

```python
import functools

import jax
import jax.numpy as jnp
from jax import lax
from jax.experimental import pallas as pl
from jax.experimental.pallas import tpu as pltpu
from jax.sharding import Mesh
from jax.sharding import PartitionSpec as P

PATCH_SIDE = 32
STRIDE = 8
SWEEPS = 2
SPAN = PATCH_SIDE // STRIDE
MARGIN = SPAN - 1

THRESHOLD = 0.25
RELAXATION = 0.1
DECAY = 0.9
LEARNING = 0.25
EPSILON = 1e-05

F32 = jnp.float32
BF16 = jnp.bfloat16
VMEM = pl.BlockSpec(memory_space=pltpu.VMEM)
SMEM = pl.BlockSpec(memory_space=pltpu.SMEM)
HBM = pl.BlockSpec(memory_space=pl.ANY)
PARAMS = pltpu.CompilerParams(vmem_limit_bytes=24 * 1024 * 1024)


def up_to(value, step):
    return -(-value // step) * step


def shrink(potential):
    return potential - jnp.clip(potential, -THRESHOLD, THRESHOLD)


class Sizes:
    def __init__(self, site_rows, site_cols, atoms, patch_len):
        self.rows, self.cols, self.atoms, self.patch = site_rows, site_cols, atoms, patch_len
        self.cell = patch_len // (SPAN * SPAN)
        self.band = SPAN * self.cell
        self.sites = site_rows * site_cols
        self.tall = site_rows + MARGIN
        self.wide = site_cols + MARGIN
        self.wide_pad = up_to(self.wide, 8)
        self.tall_pad = up_to(self.tall, 16)
        self.lanes = up_to(self.cell, 128)
        self.scale = patch_len ** (-0.5)


def dictionary_copies(source, target, sems, z):
    return [
        pltpu.make_async_copy(
            source.at[:, i * z.band : (i + 1) * z.band],
            target.at[:, i * z.band : (i + 1) * z.band],
            sems.at[i],
        )
        for i in range(SPAN)
    ]


def reconstruct(z, coding, dic, pixels, edges, tall_sum, own, left, right, ready=None):
    tall_sum[z.sites :, :] = jnp.zeros((z.tall * z.cols - z.sites, z.band), F32)
    for i in range(SPAN):
        if ready is not None:
            ready(i)
        placed = jnp.dot(
            coding, dic[:, i * z.band : (i + 1) * z.band], preferred_element_type=F32
        )
        start = i * z.cols
        if i == 0:
            tall_sum[0 : z.sites, :] = placed
        else:
            tall_sum[start : start + z.sites, :] += placed
    own[...] = jnp.zeros((z.tall, z.wide_pad, z.lanes), F32)
    own[0 : z.rows, 0 : z.cols, 0 : z.cell] = pixels[...].reshape(z.rows, z.cols, z.cell)
    for j in range(SPAN):
        part = tall_sum[:, j * z.cell : (j + 1) * z.cell].reshape(z.tall, z.cols, z.cell)
        own[:, j : j + z.cols, 0 : z.cell] -= part * z.scale

    @pl.when(edges[0] == 1)
    def _():
        own[z.rows :] = jnp.zeros((MARGIN, z.wide_pad, z.lanes), F32)

    @pl.when(edges[1] == 1)
    def _():
        own[:, z.cols :] = jnp.zeros((z.tall, z.wide_pad - z.cols, z.lanes), F32)

    for c in range(MARGIN):
        left[c, 0 : z.tall, :] = own[:, c, :]
        right[c, 0 : z.tall, :] = own[:, z.cols + c, :]


def is_equal(a, b):
    return (a == b).astype(F32).astype(BF16)


def cells_of(z, picture, pixels, spread):
    channels, height, width = picture.shape
    flat = picture[...].reshape(channels * height, width)
    high = flat.astype(BF16)
    rest = flat - high.astype(F32)
    middle = rest.astype(BF16)
    low = (rest - middle.astype(F32)).astype(BF16)

    def iota(shape, dim):
        return lax.broadcasted_iota(jnp.int32, shape, dim)

    shape = (channels * height, z.cell)
    line = iota(shape, 0)
    channel, image_row = line // height, line % height
    entry = iota(shape, 1)
    shape = (width, z.cell)
    mine = (iota(shape, 0) % STRIDE == iota(shape, 1) % STRIDE).astype(F32)
    for i in range(z.rows):
        pick = is_equal(
            (channel * STRIDE + image_row - i * STRIDE) * STRIDE + image_row // STRIDE * 65536,
            entry // STRIDE * STRIDE + i * 65536,
        )
        for part, values in enumerate((high, middle, low)):
            moved = lax.dot_general(
                values, pick, (((0,), (0,)), ((), ())), preferred_element_type=F32
            )
            spread[part, i * width : (i + 1) * width, :] = (moved * mine).astype(BF16)
    shape = (z.sites, z.rows * width)
    gather = is_equal(iota(shape, 0), iota(shape, 1) // STRIDE)
    parts = [
        jnp.dot(gather, spread[part], preferred_element_type=F32) for part in range(3)
    ]
    pixels[...] = (parts[0] + parts[1]) + parts[2]


def first_kernel(
    z, edges, membrane, picture, source, own, left, right, pixels, dic, tall_sum, spread, sems
):
    copies = dictionary_copies(source, dic, sems, z)
    for copy in copies:
        copy.start()
    cells_of(z, picture, pixels, spread)
    coding = shrink(membrane[...]).astype(BF16)
    reconstruct(
        z, coding, dic, pixels, edges, tall_sum, own, left, right, lambda i: copies[i].wait()
    )


def side_kernel(z, own, from_left, from_right, joined, up, down):
    joined[...] = own[...]
    for c in range(MARGIN):
        joined[:, c, :] += from_left[c, 0 : z.tall, :]
        joined[:, z.cols + c, :] += from_right[c, 0 : z.tall, :]
    up[...] = joined[0:MARGIN]
    down[...] = joined[z.rows :]


def windows_of(z, whole, wide_part, first_row, row_stride):
    for j in range(SPAN):
        part = whole[:, j : j + z.cols, 0 : z.cell].astype(BF16)
        for p in range(z.tall):
            wide_part[
                pl.ds(p * row_stride + first_row, z.cols), j * z.cell : (j + 1) * z.cell
            ] = part[p]


def sweep_kernel(
    z, last, groups, edges, potential, joined, from_above, from_below, pixels, dic, *rest
):
    if last:
        new_potential, own, left, right, shared, tall_sum, whole, wide_part = rest
    else:
        new_potential, own, left, right, tall_sum, whole, wide_part = rest
    whole[...] = joined[...]
    whole[0:MARGIN] += from_above[...]
    whole[z.rows :] += from_below[...]
    windows_of(z, whole, wide_part, 0, z.cols)
    drive = None
    for i in range(SPAN):
        term = lax.dot_general(
            wide_part[i * z.cols : i * z.cols + z.sites, :],
            dic[:, i * z.band : (i + 1) * z.band],
            (((1,), (1,)), ((), ())),
            preferred_element_type=F32,
        )
        drive = term if drive is None else drive + term
    old = potential[...]
    updated = old + RELAXATION * (drive * z.scale + shrink(old) - old)
    active = shrink(updated)
    coding = active.astype(BF16)
    if last:
        new_potential[...] = active
        rows_n, cores_n, owned = groups
        span = z.atoms // rows_n
        src = lax.broadcasted_iota(jnp.int32, (span, span), 0)
        dst = lax.broadcasted_iota(jnp.int32, (span, span), 1)
        per_core = span // cores_n
        core, rem = dst // per_core, dst % per_core
        wanted = (rem // owned) * (owned * cores_n) + core * owned + rem % owned
        order = is_equal(src, wanted)
        for r in range(rows_n):
            sorted_codes = jnp.dot(
                coding[:, r * span : (r + 1) * span], order, preferred_element_type=F32
            ).astype(BF16)
            for k in range(cores_n):
                shared[r * cores_n + k] = sorted_codes[:, k * per_core : (k + 1) * per_core]
    else:
        new_potential[...] = updated
    reconstruct(z, coding, dic, pixels, edges, tall_sum, own, left, right)


def pack_kernel(z, own, from_left, from_right, packed, joined):
    joined[...] = own[...]
    for c in range(MARGIN):
        joined[:, c, :] += from_left[c, 0 : z.tall, :]
        joined[:, z.cols + c, :] += from_right[c, 0 : z.tall, :]
    for p in range(z.tall):
        packed[p * z.cols : (p + 1) * z.cols, :] = joined[p, 0 : z.cols, :].astype(BF16)
    base = z.tall * z.cols
    packed[base:, :] = jnp.zeros((MARGIN * z.tall_pad, z.lanes), BF16)
    for c in range(MARGIN):
        start = base + c * z.tall_pad
        packed[start : start + z.tall, :] = joined[:, z.cols + c, :].astype(BF16)


def learn_kernel(z, groups, shared, packed, partial, whole, wide_part, codes):
    rows_n, cores_n, _ = groups
    members = rows_n * cores_n
    stride = members * z.cols
    base = z.tall * z.cols

    def unpack(d, low, high):
        main = packed[d, low * z.cols : high * z.cols, :].astype(F32)
        main = main.reshape(high - low, z.cols, z.lanes)
        side = [
            packed[d, base + c * z.tall_pad : base + (c + 1) * z.tall_pad, :].astype(F32)[low:high]
            for c in range(MARGIN)
        ]
        return main, side

    def add(d, low, high, at, first):
        main, side = unpack(d, low, high)
        n = high - low
        if first:
            whole[at : at + n, 0 : z.cols, :] = main
        else:
            whole[at : at + n, 0 : z.cols, :] += main
        for c in range(MARGIN):
            if first:
                whole[at : at + n, z.cols + c, :] = side[c]
            else:
                whole[at : at + n, z.cols + c, :] += side[c]

    for r in range(rows_n):
        for k in range(cores_n):
            d = r * cores_n + k
            add(d, 0, z.tall, 0, True)
            if r > 0:
                add(d - cores_n, z.rows, z.tall, 0, False)
            if r + 1 < rows_n:
                add(d + cores_n, 0, MARGIN, z.rows, False)
            windows_of(z, whole, wide_part, d * z.cols, stride)
            for i in range(z.rows):
                codes[i * stride + d * z.cols : i * stride + (d + 1) * z.cols, :] = shared[
                    d, i * z.cols : (i + 1) * z.cols, :
                ]
    count = z.rows * stride
    across = codes[...].astype(F32).T.astype(BF16)
    for i in range(SPAN):
        term = jnp.dot(
            across, wide_part[i * stride : i * stride + count, :], preferred_element_type=F32
        )
        partial[:, i * z.band : (i + 1) * z.band] = (term * z.scale).astype(BF16)


def finish_kernel(parts, momentum, atoms, new_dictionary, new_momentum):
    learning = parts[0].astype(F32)
    for i in range(1, parts.shape[0]):
        learning = learning + parts[i].astype(F32)
    momentum_out = DECAY * momentum[...] + learning
    new_momentum[...] = momentum_out
    weights = atoms[...].astype(F32) + LEARNING * momentum_out
    power = jnp.mean(weights * weights, axis=1, keepdims=True)
    new_dictionary[...] = weights * lax.rsqrt(power + EPSILON)


def call(kernel, outs, inputs, specs, scratch, name):
    return pl.pallas_call(
        kernel,
        out_shape=[
            pltpu.VMEM(s, d) if kept else jax.ShapeDtypeStruct(s, d) for s, d, kept in outs
        ],
        in_specs=[spec or VMEM for spec in specs],
        out_specs=[VMEM] * len(outs),
        scratch_shapes=scratch,
        compiler_params=PARAMS,
        name=name,
    )(
        *(
            x if spec else pltpu.with_memory_space_constraint(x, pltpu.VMEM)
            for x, spec in zip(inputs, specs)
        )
    )


def shards(picture, membrane, dictionary, momentum):
    site_rows, site_cols, atom_count = membrane.shape
    z = Sizes(site_rows, site_cols, atom_count, dictionary.shape[1])
    rows_n, yx_n, cores_n = (lax.axis_size(a) for a in ("row", "yx", "core"))
    cols_n = yx_n * cores_n
    owned = momentum.shape[0]
    groups = (rows_n, cores_n, owned)
    row_at = lax.axis_index("row")
    col_at = lax.axis_index(("yx", "core"))
    edges = jnp.stack([row_at == rows_n - 1, col_at == cols_n - 1]).astype(jnp.int32)

    def along(axis, n, block, distance):
        return lax.ppermute(
            block, axis, [(i - distance, i) for i in range(n) if 0 <= i - distance < n]
        )

    def sideways(left, right):
        return (
            along(("yx", "core"), cols_n, right, 1),
            along(("yx", "core"), cols_n, left, -1),
        )

    own_s = (z.tall, z.wide_pad, z.lanes)
    edge_s = (MARGIN, z.tall_pad, z.lanes)
    rim_s = (MARGIN, z.wide_pad, z.lanes)
    tall_v = pltpu.VMEM((z.tall * z.cols, z.band), F32)
    whole_v = pltpu.VMEM(own_s, F32)
    wide_v = pltpu.VMEM((z.tall * z.cols, z.band), BF16)
    sems = pltpu.SemaphoreType.DMA((SPAN,))
    sides = [(own_s, F32, True), (edge_s, F32, True), (edge_s, F32, True)]

    potential = membrane.reshape(z.sites, atom_count)
    spread_v = pltpu.VMEM((3, z.rows * picture.shape[2], z.cell), BF16)
    own, left, right, pixels, dic = call(
        functools.partial(first_kernel, z),
        sides + [((z.sites, z.cell), F32, True), (dictionary.shape, BF16, True)],
        (edges, potential, picture, dictionary),
        [SMEM, VMEM, VMEM, HBM],
        [tall_v, spread_v, sems],
        "first",
    )
    for repeat in range(SWEEPS):
        last = repeat == SWEEPS - 1
        from_left, from_right = sideways(left, right)
        joined, up, down = call(
            functools.partial(side_kernel, z),
            [(own_s, F32, True), (rim_s, F32, True), (rim_s, F32, True)],
            (own, from_left, from_right),
            [None] * 3,
            [],
            "side",
        )
        from_above = along("row", rows_n, down, 1)
        from_below = along("row", rows_n, up, -1)
        outs = [((z.sites, atom_count), F32, not last)] + sides
        if last:
            members = rows_n * cores_n
            outs = outs + [((members, z.sites, atom_count // members), BF16, True)]
        results = call(
            functools.partial(sweep_kernel, z, last, groups),
            outs,
            (edges, potential, joined, from_above, from_below, pixels, dic),
            [SMEM, None if repeat else VMEM] + [None] * 5,
            [tall_v, whole_v, wide_v],
            "sweep",
        )
        potential, own, left, right = results[:4]
    final_codes = potential.reshape(membrane.shape)
    shared = results[4]
    members = rows_n * cores_n
    shared = lax.all_to_all(shared, ("row", "core"), 0, 0, tiled=True)
    from_left, from_right = sideways(left, right)
    packed_rows = z.tall * z.cols + MARGIN * z.tall_pad
    (packed,) = call(
        functools.partial(pack_kernel, z),
        [((packed_rows, z.lanes), BF16, True)],
        (own, from_left, from_right),
        [None] * 3,
        [whole_v],
        "pack",
    )
    packed = lax.all_gather(packed, ("row", "core"), axis=0, tiled=False)
    (partial,) = call(
        functools.partial(learn_kernel, z, groups),
        [((atom_count // members, z.patch), BF16, True)],
        (shared, packed),
        [None] * 2,
        [
            whole_v,
            pltpu.VMEM((z.tall * members * z.cols, z.band), BF16),
            pltpu.VMEM((members * z.sites, atom_count // members), BF16),
        ],
        "learn",
    )
    parts = lax.all_to_all(
        partial.reshape(yx_n, owned, z.patch), "yx", 0, 0, tiled=True
    )
    atoms = lax.dynamic_slice_in_dim(dictionary, (row_at * cols_n + col_at) * owned, owned, 0)
    new_dictionary, new_momentum = call(
        finish_kernel,
        [(momentum.shape, F32, False), (momentum.shape, F32, False)],
        (parts, momentum, atoms),
        [None, VMEM, VMEM],
        [],
        "finish",
    )
    return (final_codes, new_dictionary, new_momentum)


def solution(mesh):
    rows_n, cols_n = (mesh.shape["row"], mesh.shape["col"])
    cores_n = 2 if cols_n % 2 == 0 else 1
    split = Mesh(
        mesh.devices.reshape(rows_n, cols_n // cores_n, cores_n), ("row", "yx", "core")
    )
    col = ("yx", "core")
    return jax.shard_map(
        shards,
        mesh=split,
        in_specs=(P(None, "row", col), P("row", col, None), P(), P(("row",) + col, None)),
        out_specs=(P("row", col, None), P(("row",) + col, None), P(("row",) + col, None)),
        check_vma=False,
    )
```

```python
import functools

import jax
import jax.numpy as jnp
from jax import lax
from jax.experimental import pallas as pl
from jax.experimental.pallas import tpu as pltpu
from jax.sharding import Mesh
from jax.sharding import PartitionSpec as P

PATCH_SIDE = 32
STRIDE = 8
SWEEPS = 2
SPAN = PATCH_SIDE // STRIDE
MARGIN = SPAN - 1

THRESHOLD = 0.25
RELAXATION = 0.1
DECAY = 0.9
LEARNING = 0.25
EPSILON = 1e-05

F32 = jnp.float32
BF16 = jnp.bfloat16
VMEM = pl.BlockSpec(memory_space=pltpu.VMEM)
SMEM = pl.BlockSpec(memory_space=pltpu.SMEM)
HBM = pl.BlockSpec(memory_space=pltpu.HBM)
PARAMS = pltpu.CompilerParams(vmem_limit_bytes=24 * 1024 * 1024)


def up_to(value, step):
    return -(-value // step) * step


def shrink(potential):
    return potential - jnp.clip(potential, -THRESHOLD, THRESHOLD)


class Sizes:
    def __init__(self, site_rows, site_cols, atoms, patch_len):
        self.rows, self.cols, self.atoms, self.patch = site_rows, site_cols, atoms, patch_len
        self.cell = patch_len // (SPAN * SPAN)
        self.band = SPAN * self.cell
        self.sites = site_rows * site_cols
        self.tall = site_rows + MARGIN
        self.wide = site_cols + MARGIN
        self.wide_pad = up_to(self.wide, 8)
        self.tall_pad = up_to(self.tall, 16)
        self.lanes = up_to(self.cell, 128)
        self.rim = up_to(MARGIN * self.wide, 16)
        self.packed = up_to(self.tall * self.cols + MARGIN * self.tall_pad, 32)
        self.scale = patch_len ** (-0.5)


class Place:
    def __init__(self, where, rows_n, cols_n):
        self.row, self.col = where[0], where[1]
        self.rows_n, self.cols_n = rows_n, cols_n
        self.owner = self.row * cols_n + self.col

    def pairs(self, axis):
        at, n = (self.row, self.rows_n) if axis == 0 else (self.col, self.cols_n)
        before, after = at > 0, at < n - 1
        odd = at % 2
        return [
            (odd == 0, ((True, after), (False, before))),
            (odd == 1, ((False, before), (True, after))),
        ]


def partners(n):
    even, odd = {}, {}
    for i in range(n):
        even[i] = i ^ 1 if i ^ 1 < n else i
        other = ((i + 1) ^ 1) - 1
        odd[i] = other if 0 <= other < n else (n - 1 if i == 0 and n % 2 == 0 else i)
    if n % 2 == 0:
        odd[n - 1] = 0
    return [sorted(even.items()), sorted(odd.items())]


def reconstruct(z, place, coding, dic, pixels, tall_sum, own, sends, ready=None):
    tall_sum[z.sites :, :] = jnp.zeros((z.tall * z.cols - z.sites, z.band), F32)
    for i in range(SPAN):
        if ready is not None:
            ready(i)
        placed = jnp.dot(
            coding, dic[:, i * z.band : (i + 1) * z.band], preferred_element_type=F32
        )
        start = i * z.cols
        if i == 0:
            tall_sum[0 : z.sites, :] = placed
        else:
            tall_sum[start : start + z.sites, :] += placed
    own[...] = jnp.zeros((z.tall, z.wide_pad, z.lanes), F32)
    own[0 : z.rows, 0 : z.cols, 0 : z.cell] = pixels[...].reshape(z.rows, z.cols, z.cell)
    for j in range(SPAN):
        part = tall_sum[:, j * z.cell : (j + 1) * z.cell].reshape(z.tall, z.cols, z.cell)
        own[:, j : j + z.cols, 0 : z.cell] -= part * z.scale

    @pl.when(place.row == place.rows_n - 1)
    def _():
        own[z.rows :] = jnp.zeros((MARGIN, z.wide_pad, z.lanes), F32)

    @pl.when(place.col == place.cols_n - 1)
    def _():
        own[:, z.cols :] = jnp.zeros((z.tall, z.wide_pad - z.cols, z.lanes), F32)

    for mine, halves in place.pairs(1):

        @pl.when(mine)
        def _(halves=halves):
            for send, (onward, _) in zip(sends, halves):
                first = z.cols if onward else 0
                for c in range(MARGIN):
                    send[c, 0 : z.tall, :] = own[:, first + c, :].astype(BF16)


def add_sides(z, place, whole, received):
    for mine, halves in place.pairs(1):
        for rim, (onward, there) in zip(received, halves):

            @pl.when(mine & there)
            def _(rim=rim, first=z.cols if onward else 0):
                for c in range(MARGIN):
                    whole[:, first + c, :] += rim[c].astype(F32)[0 : z.tall]


def is_equal(a, b):
    return (a == b).astype(F32).astype(BF16)


def cells_of(z, picture, pixels, spread):
    channels, height, width = picture.shape
    flat = picture[...].reshape(channels * height, width)
    high = flat.astype(BF16)
    rest = flat - high.astype(F32)
    middle = rest.astype(BF16)
    low = (rest - middle.astype(F32)).astype(BF16)

    def iota(shape, dim):
        return lax.broadcasted_iota(jnp.int32, shape, dim)

    shape = (channels * height, z.cell)
    line = iota(shape, 0)
    channel, image_row = line // height, line % height
    entry = iota(shape, 1)
    shape = (width, z.cell)
    mine = (iota(shape, 0) % STRIDE == iota(shape, 1) % STRIDE).astype(F32)
    for i in range(z.rows):
        pick = is_equal(
            (channel * STRIDE + image_row - i * STRIDE) * STRIDE + image_row // STRIDE * 65536,
            entry // STRIDE * STRIDE + i * 65536,
        )
        for part, values in enumerate((high, middle, low)):
            moved = lax.dot_general(
                values, pick, (((0,), (0,)), ((), ())), preferred_element_type=F32
            )
            spread[part, i * width : (i + 1) * width, :] = (moved * mine).astype(BF16)
    shape = (z.sites, z.rows * width)
    gather = is_equal(iota(shape, 0), iota(shape, 1) // STRIDE)
    parts = [
        jnp.dot(gather, spread[part], preferred_element_type=F32) for part in range(3)
    ]
    pixels[...] = (parts[0] + parts[1]) + parts[2]


def first_kernel(
    z, grid, where, membrane, picture, source, own, *rest
):
    (*sends, pixels, dic, potential, atoms, tall_sum, spread, drawing, sems) = rest
    place = Place(where, *grid)
    early = [
        pltpu.make_async_copy(picture, drawing, sems.at[SPAN]),
        pltpu.make_async_copy(membrane, potential, sems.at[SPAN + 1]),
    ]
    copies = [
        pltpu.make_async_copy(
            source.at[:, i * z.band : (i + 1) * z.band],
            dic.at[:, i * z.band : (i + 1) * z.band],
            sems.at[i],
        )
        for i in range(SPAN)
    ]
    for copy in early + copies:
        copy.start()
    early[0].wait()
    cells_of(z, drawing, pixels, spread)
    early[1].wait()
    coding = shrink(potential[...]).astype(BF16)
    reconstruct(
        z, place, coding, dic, pixels, tall_sum, own, sends, lambda i: copies[i].wait()
    )
    owned = atoms.shape[0]
    atoms[...] = dic[pl.ds(pl.multiple_of(place.owner * owned, owned), owned), :]


def side_kernel(z, grid, where, own, from_even, from_odd, joined, even, odd, rim):
    place = Place(where, *grid)
    joined[...] = own[...]
    add_sides(z, place, joined, (from_even, from_odd))
    rim[MARGIN * z.wide :, :] = jnp.zeros((z.rim - MARGIN * z.wide, z.lanes), F32)
    for mine, halves in place.pairs(0):

        @pl.when(mine)
        def _(halves=halves):
            for send, (onward, _) in zip((even, odd), halves):
                first = z.rows if onward else 0
                for r in range(MARGIN):
                    start = MARGIN * z.cols + r * MARGIN
                    rim[r * z.cols : (r + 1) * z.cols, :] = joined[first + r, 0 : z.cols, :]
                    rim[start : start + MARGIN, :] = joined[first + r, z.cols : z.wide, :]
                send[...] = rim[...].astype(BF16)


def add_ends(z, place, whole, received, rim):
    for mine, halves in place.pairs(0):
        for block, (onward, there) in zip(received, halves):

            @pl.when(mine & there)
            def _(block=block, first=z.rows if onward else 0):
                rim[...] = block[...].astype(F32)
                for r in range(MARGIN):
                    start = MARGIN * z.cols + r * MARGIN
                    whole[first + r, 0 : z.cols, :] += rim[r * z.cols : (r + 1) * z.cols, :]
                    whole[first + r, z.cols : z.wide, :] += rim[start : start + MARGIN, :]


def windows_of(z, whole, wide_part, first_row, row_stride):
    for j in range(SPAN):
        part = whole[:, j : j + z.cols, 0 : z.cell].astype(BF16)
        for p in range(z.tall):
            wide_part[
                pl.ds(p * row_stride + first_row, z.cols), j * z.cell : (j + 1) * z.cell
            ] = part[p]


def sweep_kernel(
    z, grid, last, groups, where, potential, joined, from_even, from_odd, pixels, dic, *rest
):
    if last:
        new_potential, own, *sends, shared, tall_sum, whole, wide_part, rim = rest
    else:
        new_potential, own, *sends, tall_sum, whole, wide_part, rim = rest
    place = Place(where, *grid)
    whole[...] = joined[...]
    add_ends(z, place, whole, (from_even, from_odd), rim)
    windows_of(z, whole, wide_part, 0, z.cols)
    drive = None
    for i in range(SPAN):
        term = lax.dot_general(
            wide_part[i * z.cols : i * z.cols + z.sites, :],
            dic[:, i * z.band : (i + 1) * z.band],
            (((1,), (1,)), ((), ())),
            preferred_element_type=F32,
        )
        drive = term if drive is None else drive + term
    old = potential[...]
    updated = old + RELAXATION * (drive * z.scale + shrink(old) - old)
    active = shrink(updated)
    coding = active.astype(BF16)
    if last:
        new_potential[...] = active
        rows_n, cores_n, owned = groups
        span = z.atoms // rows_n
        src = lax.broadcasted_iota(jnp.int32, (span, span), 0)
        dst = lax.broadcasted_iota(jnp.int32, (span, span), 1)
        per_core = span // cores_n
        core, rem = dst // per_core, dst % per_core
        wanted = (rem // owned) * (owned * cores_n) + core * owned + rem % owned
        order = is_equal(src, wanted)
        for r in range(rows_n):
            sorted_codes = jnp.dot(
                coding[:, r * span : (r + 1) * span], order, preferred_element_type=F32
            ).astype(BF16)
            for k in range(cores_n):
                shared[r * cores_n + k] = sorted_codes[:, k * per_core : (k + 1) * per_core]
    else:
        new_potential[...] = updated
    reconstruct(z, place, coding, dic, pixels, tall_sum, own, sends)


def pack_kernel(z, grid, where, own, from_even, from_odd, packed, joined, flat):
    joined[...] = own[...]
    add_sides(z, Place(where, *grid), joined, (from_even, from_odd))
    base = z.tall * z.cols
    flat[base:, :] = jnp.zeros((z.packed - base, z.lanes), F32)
    for p in range(z.tall):
        flat[p * z.cols : (p + 1) * z.cols, :] = joined[p, 0 : z.cols, :]
    for c in range(MARGIN):
        start = base + c * z.tall_pad
        flat[start : start + z.tall, :] = joined[:, z.cols + c, :]
    half = z.packed // 2
    packed[0 : z.packed, :] = flat[:, 0:128].astype(BF16)
    tail = z.cell - 128
    ends = jnp.concatenate([flat[0:half, 128 : z.cell], flat[half:, 128 : z.cell]], axis=1)
    packed[z.packed :, 0 : 2 * tail] = ends.astype(BF16)


def learn_kernel(z, groups, where, shared, packed, partial, flat, whole, wide_part, codes):
    rows_n, cores_n, _ = groups
    members = rows_n * cores_n
    stride = members * z.cols
    base = z.tall * z.cols
    half = z.packed // 2
    tail = z.cell - 128
    row = where[0]

    for k in range(cores_n):
        for x in range(rows_n):
            d = (row ^ x) if rows_n & (rows_n - 1) == 0 else (row + x) % rows_n
            block = packed[k, x].astype(F32)
            flat[d, :, 0:128] = block[0 : z.packed]
            flat[d, 0:half, 128 : z.cell] = block[z.packed :, 0:tail]
            flat[d, half:, 128 : z.cell] = block[z.packed :, tail : 2 * tail]
        for r in range(rows_n):
            d = r * cores_n + k
            for source, low, high, at in (
                (r, 0, z.tall, 0),
                (r - 1, z.rows, z.tall, 0),
                (r + 1, 0, MARGIN, z.rows),
            ):
                if not 0 <= source < rows_n:
                    continue
                n = high - low
                main = flat[source, low * z.cols : high * z.cols, :].reshape(n, z.cols, z.lanes)
                side = [
                    flat[source, base + c * z.tall_pad + low : base + c * z.tall_pad + high, :]
                    for c in range(MARGIN)
                ]
                if source == r:
                    whole[at : at + n, 0 : z.cols, :] = main
                    for c in range(MARGIN):
                        whole[at : at + n, z.cols + c, :] = side[c]
                else:
                    whole[at : at + n, 0 : z.cols, :] += main
                    for c in range(MARGIN):
                        whole[at : at + n, z.cols + c, :] += side[c]
            windows_of(z, whole, wide_part, d * z.cols, stride)
            for i in range(z.rows):
                codes[i * stride + d * z.cols : i * stride + (d + 1) * z.cols, :] = shared[
                    d, i * z.cols : (i + 1) * z.cols, :
                ]
    count = z.rows * stride
    across = codes[...].astype(F32).T.astype(BF16)
    for i in range(SPAN):
        term = jnp.dot(
            across, wide_part[i * stride : i * stride + count, :], preferred_element_type=F32
        )
        partial[:, i * z.band : (i + 1) * z.band] = (term * z.scale).astype(BF16)


def finish_kernel(where, parts, momentum, atoms, new_dictionary, new_momentum):
    learning = parts[0].astype(F32)
    for i in range(1, parts.shape[0]):
        learning = learning + parts[i].astype(F32)
    momentum_out = DECAY * momentum[...] + learning
    new_momentum[...] = momentum_out
    weights = atoms[...].astype(F32) + LEARNING * momentum_out
    power = jnp.mean(weights * weights, axis=1, keepdims=True)
    new_dictionary[...] = weights * lax.rsqrt(power + EPSILON)


def kept(x, space=pltpu.VMEM):
    return pltpu.with_memory_space_constraint(x, space)


def call(kernel, outs, inputs, scratch, name, far=0):
    specs = [SMEM] + [HBM] * far + [VMEM] * (len(inputs) - 1 - far)
    where, *others = inputs
    placed = [kept(x, pltpu.HBM) for x in others[:far]] + [kept(x) for x in others[far:]]
    return pl.pallas_call(
        kernel,
        out_shape=outs,
        in_specs=specs,
        out_specs=[VMEM] * len(outs),
        scratch_shapes=scratch,
        compiler_params=PARAMS,
        name=name,
    )(where, *placed)


def shards(picture, membrane, dictionary, momentum):
    site_rows, site_cols, atom_count = membrane.shape
    z = Sizes(site_rows, site_cols, atom_count, dictionary.shape[1])
    rows_n, yx_n, cores_n = (lax.axis_size(a) for a in ("row", "yx", "core"))
    cols_n = yx_n * cores_n
    owned = momentum.shape[0]
    groups = (rows_n, cores_n, owned)
    members = rows_n * cores_n
    grid = (rows_n, cols_n)
    where = jnp.stack([lax.axis_index("row"), lax.axis_index(("yx", "core"))]).astype(jnp.int32)

    def swapped(axis, n, blocks):
        return [lax.ppermute(b, axis, route) for b, route in zip(blocks, partners(n))]

    def sideways(blocks):
        return swapped(("yx", "core"), cols_n, blocks)

    own_v = pltpu.VMEM((z.tall, z.wide_pad, z.lanes), F32)
    side_v = pltpu.VMEM((MARGIN, z.tall_pad, z.lanes), BF16)
    end_v = pltpu.VMEM((z.rim, z.lanes), BF16)
    rim_v = pltpu.VMEM((z.rim, z.lanes), F32)
    tall_v = pltpu.VMEM((z.tall * z.cols, z.band), F32)
    wide_v = pltpu.VMEM((z.tall * z.cols, z.band), BF16)
    site_v = pltpu.VMEM((z.sites, atom_count), F32)
    outs = [own_v, side_v, side_v]

    own, *sides, pixels, dic, potential, atoms = call(
        functools.partial(first_kernel, z, grid),
        outs
        + [
            pltpu.VMEM((z.sites, z.cell), F32),
            pltpu.VMEM(dictionary.shape, BF16),
            site_v,
            pltpu.VMEM(momentum.shape, BF16),
        ],
        (where, membrane.reshape(z.sites, atom_count), picture, dictionary),
        [
            tall_v,
            pltpu.VMEM((3, z.rows * picture.shape[2], z.cell), BF16),
            pltpu.VMEM(picture.shape, F32),
            pltpu.SemaphoreType.DMA((SPAN + 2,)),
        ],
        "first",
        far=3,
    )
    for repeat in range(SWEEPS):
        last = repeat == SWEEPS - 1
        joined, *ends = call(
            functools.partial(side_kernel, z, grid),
            [own_v, end_v, end_v],
            (where, own, *sideways(sides)),
            [rim_v],
            "side",
        )
        ends = swapped("row", rows_n, ends)
        final = [
            jax.ShapeDtypeStruct((z.sites, atom_count), F32),
            *outs,
            pltpu.VMEM((members, z.sites, atom_count // members), BF16),
        ]
        potential, own, *rest = call(
            functools.partial(sweep_kernel, z, grid, last, groups),
            final if last else [site_v] + outs,
            (where, potential, joined, *ends, pixels, dic),
            [tall_v, own_v, wide_v, rim_v],
            "sweep",
        )
        sides = rest[:2]
    final_codes = potential.reshape(membrane.shape)
    shared = lax.all_to_all(rest[2], ("row", "core"), 0, 0, tiled=True)
    (packed,) = call(
        functools.partial(pack_kernel, z, grid),
        [pltpu.VMEM((z.packed * 3 // 2, 128), BF16)],
        (where, own, *sideways(sides)),
        [own_v, pltpu.VMEM((z.packed, z.lanes), F32)],
        "pack",
    )
    blocks = [packed]
    for x in range(1, rows_n):
        power = rows_n & (rows_n - 1) == 0
        route = [(i ^ x if power else (i + x) % rows_n, i) for i in range(rows_n)]
        blocks.append(lax.ppermute(packed, "row", route))
    blocks = lax.all_gather(jnp.stack(blocks), "core", axis=0, tiled=False)
    (partial,) = call(
        functools.partial(learn_kernel, z, groups),
        [pltpu.VMEM((atom_count // members, z.patch), BF16)],
        (where, shared, blocks),
        [
            pltpu.VMEM((rows_n, z.packed, z.lanes), F32),
            own_v,
            pltpu.VMEM((z.tall * members * z.cols, z.band), BF16),
            pltpu.VMEM((members * z.sites, atom_count // members), BF16),
        ],
        "learn",
    )
    parts = lax.all_to_all(partial.reshape(yx_n, owned, z.patch), "yx", 0, 0, tiled=True)
    new_dictionary, new_momentum = call(
        finish_kernel,
        [jax.ShapeDtypeStruct(momentum.shape, F32)] * 2,
        (where, parts, momentum, atoms),
        [],
        "finish",
    )
    return (final_codes, new_dictionary, new_momentum)


def solution(mesh):
    rows_n, cols_n = (mesh.shape["row"], mesh.shape["col"])
    cores_n = 2 if cols_n % 2 == 0 else 1
    split = Mesh(
        mesh.devices.reshape(rows_n, cols_n // cores_n, cores_n), ("row", "yx", "core")
    )
    col = ("yx", "core")
    return jax.shard_map(
        shards,
        mesh=split,
        in_specs=(P(None, "row", col), P("row", col, None), P(), P(("row",) + col, None)),
        out_specs=(P("row", col, None), P(("row",) + col, None), P(("row",) + col, None)),
        check_vma=False,
    )
```

```python
import functools

import jax
import jax.numpy as jnp
from jax import lax
from jax.experimental import pallas as pl
from jax.experimental.pallas import tpu as pltpu
from jax.sharding import Mesh
from jax.sharding import PartitionSpec as P

PATCH_SIDE = 32
STRIDE = 8
SWEEPS = 2
SPAN = PATCH_SIDE // STRIDE
MARGIN = SPAN - 1

THRESHOLD = 0.25
RELAXATION = 0.1
DECAY = 0.9
LEARNING = 0.25
EPSILON = 1e-05

F32 = jnp.float32
BF16 = jnp.bfloat16
VMEM = pl.BlockSpec(memory_space=pltpu.VMEM)
SMEM = pl.BlockSpec(memory_space=pltpu.SMEM)
HBM = pl.BlockSpec(memory_space=pltpu.HBM)
PARAMS = pltpu.CompilerParams(vmem_limit_bytes=24 * 1024 * 1024)


def up_to(value, step):
    return -(-value // step) * step


def shrink(potential):
    return potential - jnp.clip(potential, -THRESHOLD, THRESHOLD)


class Sizes:
    def __init__(self, site_rows, site_cols, atoms, patch_len):
        self.rows, self.cols, self.atoms, self.patch = site_rows, site_cols, atoms, patch_len
        self.cell = patch_len // (SPAN * SPAN)
        self.band = SPAN * self.cell
        self.sites = site_rows * site_cols
        self.tall = site_rows + MARGIN
        self.wide = site_cols + MARGIN
        self.wide_pad = up_to(self.wide, 8)
        self.tall_pad = up_to(self.tall, 16)
        self.lanes = up_to(self.cell, 128)
        self.rim = up_to(MARGIN * self.wide, 16)
        self.packed = up_to(self.tall * self.cols + MARGIN * self.tall_pad, 32)
        self.scale = patch_len ** (-0.5)


class Place:
    def __init__(self, where, rows_n, cols_n):
        self.row, self.col = where[0], where[1]
        self.rows_n, self.cols_n = rows_n, cols_n
        self.owner = self.row * cols_n + self.col

    def pairs(self, axis):
        at, n = (self.row, self.rows_n) if axis == 0 else (self.col, self.cols_n)
        before, after = at > 0, at < n - 1
        odd = at % 2
        return [
            (odd == 0, ((True, after), (False, before))),
            (odd == 1, ((False, before), (True, after))),
        ]


def partners(n):
    even, odd = {}, {}
    for i in range(n):
        even[i] = i ^ 1 if i ^ 1 < n else i
        other = ((i + 1) ^ 1) - 1
        odd[i] = other if 0 <= other < n else (n - 1 if i == 0 and n % 2 == 0 else i)
    if n % 2 == 0:
        odd[n - 1] = 0
    return [sorted(even.items()), sorted(odd.items())]


def reconstruct(z, place, coding, dic, pixels, tall_sum, own, ready=None):
    tall_sum[z.sites :, :] = jnp.zeros((z.tall * z.cols - z.sites, z.band), F32)
    for i in range(SPAN):
        if ready is not None:
            ready(i)
        placed = jnp.dot(
            coding, dic[:, i * z.band : (i + 1) * z.band], preferred_element_type=F32
        )
        start = i * z.cols
        if i == 0:
            tall_sum[0 : z.sites, :] = placed
        else:
            tall_sum[start : start + z.sites, :] += placed
    own[...] = jnp.zeros((z.tall, z.wide_pad, z.lanes), F32)
    own[0 : z.rows, 0 : z.cols, 0 : z.cell] = pixels[...].reshape(z.rows, z.cols, z.cell)
    for j in range(SPAN):
        part = tall_sum[:, j * z.cell : (j + 1) * z.cell].reshape(z.tall, z.cols, z.cell)
        own[:, j : j + z.cols, 0 : z.cell] -= part * z.scale

    @pl.when(place.row == place.rows_n - 1)
    def _():
        own[z.rows :] = jnp.zeros((MARGIN, z.wide_pad, z.lanes), F32)

    @pl.when(place.col == place.cols_n - 1)
    def _():
        own[:, z.cols :] = jnp.zeros((z.tall, z.wide_pad - z.cols, z.lanes), F32)


def send_sides(z, place, own, sends):
    for mine, halves in place.pairs(1):

        @pl.when(mine)
        def _(halves=halves):
            for send, (onward, _) in zip(sends, halves):
                first = z.cols if onward else 0
                for c in range(MARGIN):
                    send[c, 0 : z.tall, :] = own[:, first + c, :].astype(BF16)


def send_all(z, place, own, flat, packed, outer):
    base = z.tall * z.cols
    flat[base:, :] = jnp.zeros((z.packed - base, z.lanes), F32)
    for p in range(z.tall):
        flat[p * z.cols : (p + 1) * z.cols, :] = own[p, 0 : z.cols, :]
    for c in range(MARGIN):
        start = base + c * z.tall_pad
        flat[start : start + z.tall, :] = own[:, z.cols + c, :]
    half = z.packed // 2
    packed[0 : z.packed, :] = flat[:, 0:128].astype(BF16)
    tail = z.cell - 128
    ends = jnp.concatenate([flat[0:half, 128 : z.cell], flat[half:, 128 : z.cell]], axis=1)
    packed[z.packed :, 0 : 2 * tail] = ends.astype(BF16)
    for odd, first in ((0, 0), (1, z.cols)):

        @pl.when(place.col % 2 == odd)
        def _(first=first):
            for c in range(MARGIN):
                start = 2 * c * z.tall_pad
                line = own[:, first + c, :].astype(BF16)
                outer[start : start + z.tall, :] = line[:, 0:128]
                start += z.tall_pad
                outer[start : start + z.tall, 0:tail] = line[:, 128 : z.cell]


def add_sides(z, place, whole, received):
    for mine, halves in place.pairs(1):
        for rim, (onward, there) in zip(received, halves):

            @pl.when(mine & there)
            def _(rim=rim, first=z.cols if onward else 0):
                for c in range(MARGIN):
                    whole[:, first + c, :] += rim[c].astype(F32)[0 : z.tall]


def is_equal(a, b):
    return (a == b).astype(F32).astype(BF16)


def cells_of(z, picture, pixels, spread):
    channels, height, width = picture.shape
    turned = picture[...].reshape(channels * height, width).T
    high = turned.astype(BF16)
    rest = turned - high.astype(F32)
    middle = rest.astype(BF16)
    spread[0:width, :] = high
    spread[width : 2 * width, :] = middle
    spread[2 * width :, :] = (rest - middle.astype(F32)).astype(BF16)

    def iota(shape, dim):
        return lax.broadcasted_iota(jnp.int32, shape, dim)

    shape = (channels * height, z.cell)
    line, entry = iota(shape, 0), iota(shape, 1)
    channel, image_row = line // height, line % height
    away = (
        (channel * STRIDE + image_row % STRIDE) * STRIDE
        + image_row // STRIDE * z.cell
        - entry // STRIDE * STRIDE
    )
    shape = (width, z.cell)
    mine = (iota(shape, 0) % STRIDE == iota(shape, 1) % STRIDE).astype(F32)
    for i in range(z.rows):
        moved = jnp.dot(
            spread[...], is_equal(away, i * z.cell), preferred_element_type=F32
        )
        whole = (moved[0:width] + moved[width : 2 * width]) + moved[2 * width :]
        whole = (whole * mine).reshape(z.cols, STRIDE, z.cell)
        pixels[i * z.cols : (i + 1) * z.cols, :] = jnp.sum(whole, axis=1)


def first_kernel(
    z, grid, where, membrane, picture, source, own, *rest
):
    (*sends, pixels, dic, potential, atoms, tall_sum, spread, drawing, sems) = rest
    place = Place(where, *grid)
    early = [
        pltpu.make_async_copy(picture, drawing, sems.at[SPAN]),
        pltpu.make_async_copy(membrane, potential, sems.at[SPAN + 1]),
    ]
    copies = [
        pltpu.make_async_copy(
            source.at[:, i * z.band : (i + 1) * z.band],
            dic.at[:, i * z.band : (i + 1) * z.band],
            sems.at[i],
        )
        for i in range(SPAN)
    ]
    for copy in early + copies:
        copy.start()
    early[0].wait()
    cells_of(z, drawing, pixels, spread)
    early[1].wait()
    coding = shrink(potential[...]).astype(BF16)
    reconstruct(z, place, coding, dic, pixels, tall_sum, own, lambda i: copies[i].wait())
    send_sides(z, place, own, sends)
    owned = atoms.shape[0]
    atoms[...] = dic[pl.ds(pl.multiple_of(place.owner * owned, owned), owned), :]


def side_kernel(z, grid, where, own, from_even, from_odd, joined, even, odd, rim):
    place = Place(where, *grid)
    joined[...] = own[...]
    add_sides(z, place, joined, (from_even, from_odd))
    rim[MARGIN * z.wide :, :] = jnp.zeros((z.rim - MARGIN * z.wide, z.lanes), F32)
    for mine, halves in place.pairs(0):

        @pl.when(mine)
        def _(halves=halves):
            for send, (onward, _) in zip((even, odd), halves):
                first = z.rows if onward else 0
                for r in range(MARGIN):
                    start = MARGIN * z.cols + r * MARGIN
                    rim[r * z.cols : (r + 1) * z.cols, :] = joined[first + r, 0 : z.cols, :]
                    rim[start : start + MARGIN, :] = joined[first + r, z.cols : z.wide, :]
                send[...] = rim[...].astype(BF16)


def add_ends(z, place, whole, received, rim):
    for mine, halves in place.pairs(0):
        for block, (onward, there) in zip(received, halves):

            @pl.when(mine & there)
            def _(block=block, first=z.rows if onward else 0):
                rim[...] = block[...].astype(F32)
                for r in range(MARGIN):
                    start = MARGIN * z.cols + r * MARGIN
                    whole[first + r, 0 : z.cols, :] += rim[r * z.cols : (r + 1) * z.cols, :]
                    whole[first + r, z.cols : z.wide, :] += rim[start : start + MARGIN, :]


def windows_of(z, whole, wide_part, first_row, row_stride):
    for j in range(SPAN):
        part = whole[:, j : j + z.cols, 0 : z.cell].astype(BF16)
        for p in range(z.tall):
            wide_part[
                pl.ds(p * row_stride + first_row, z.cols), j * z.cell : (j + 1) * z.cell
            ] = part[p]


def sweep_kernel(
    z, grid, last, groups, where, potential, joined, from_even, from_odd, pixels, dic, *rest
):
    if last:
        new_potential, packed, outer, shared, tall_sum, whole, wide_part, rim, own, flat = rest
    else:
        new_potential, own, *sends, tall_sum, whole, wide_part, rim = rest
    place = Place(where, *grid)
    whole[...] = joined[...]
    add_ends(z, place, whole, (from_even, from_odd), rim)
    windows_of(z, whole, wide_part, 0, z.cols)
    drive = None
    for i in range(SPAN):
        term = lax.dot_general(
            wide_part[i * z.cols : i * z.cols + z.sites, :],
            dic[:, i * z.band : (i + 1) * z.band],
            (((1,), (1,)), ((), ())),
            preferred_element_type=F32,
        )
        drive = term if drive is None else drive + term
    old = potential[...]
    updated = old + RELAXATION * (drive * z.scale + shrink(old) - old)
    active = shrink(updated)
    coding = active.astype(BF16)
    if last:
        new_potential[...] = active
        rows_n, cores_n, owned = groups
        span = z.atoms // rows_n
        src = lax.broadcasted_iota(jnp.int32, (span, span), 0)
        dst = lax.broadcasted_iota(jnp.int32, (span, span), 1)
        per_core = span // cores_n
        core, rem = dst // per_core, dst % per_core
        wanted = (rem // owned) * (owned * cores_n) + core * owned + rem % owned
        order = is_equal(src, wanted)
        for r in range(rows_n):
            sorted_codes = jnp.dot(
                coding[:, r * span : (r + 1) * span], order, preferred_element_type=F32
            ).astype(BF16)
            for k in range(cores_n):
                shared[r * cores_n + k] = sorted_codes[:, k * per_core : (k + 1) * per_core]
    else:
        new_potential[...] = updated
    reconstruct(z, place, coding, dic, pixels, tall_sum, own)
    if last:
        send_all(z, place, own, flat, packed, outer)
    else:
        send_sides(z, place, own, sends)


def learn_kernel(
    z, grid, groups, where, shared, packed, partial, flat, joined, whole, wide_part, codes
):
    rows_n, cores_n, _ = groups
    members = rows_n * cores_n
    stride = members * z.cols
    base = z.tall * z.cols
    half = z.packed // 2
    tail = z.cell - 128
    end = z.packed + half
    place = Place(where, *grid)

    for x in range(rows_n):
        d = (place.row ^ x) if rows_n & (rows_n - 1) == 0 else (place.row + x) % rows_n
        for k in range(cores_n):
            flat[:, 0:128] = packed[k, x, 0 : z.packed, :].astype(F32)
            ends = packed[k, x, z.packed : end, :].astype(F32)
            flat[0:half, 128 : z.cell] = ends[:, 0:tail]
            flat[half:, 128 : z.cell] = ends[:, tail : 2 * tail]
            joined[k, d, :, 0 : z.cols, :] = flat[0:base, :].reshape(z.tall, z.cols, z.lanes)
            for c in range(MARGIN):
                start = base + c * z.tall_pad
                joined[k, d, :, z.cols + c, :] = flat[start : start + z.tall, :]
        for c in range(MARGIN):
            both = joined[0, d, :, z.cols + c, :] + joined[1, d, :, c, :]
            joined[0, d, :, z.cols + c, :] = both
            joined[1, d, :, c, :] = both
        for k, first, there in ((0, 0, place.col > 1), (1, z.cols, place.col < place.cols_n - 2)):

            @pl.when(there)
            def _(x=x, d=d, k=k, first=first):
                for c in range(MARGIN):
                    start = end + 2 * c * z.tall_pad
                    low = packed[k, x, start : start + z.tall_pad, :].astype(F32)
                    start += z.tall_pad
                    high = packed[k, x, start : start + z.tall_pad, :].astype(F32)
                    joined[k, d, :, first + c, 0:128] += low[0 : z.tall]
                    joined[k, d, :, first + c, 128 : z.cell] += high[0 : z.tall, 0:tail]

    for r in range(rows_n):
        for k in range(cores_n):
            d = r * cores_n + k
            whole[...] = joined[k, r]
            if r > 0:
                whole[0:MARGIN] += joined[k, r - 1, z.rows :]
            if r + 1 < rows_n:
                whole[z.rows :] += joined[k, r + 1, 0:MARGIN]
            windows_of(z, whole, wide_part, d * z.cols, stride)
            for i in range(z.rows):
                codes[i * stride + d * z.cols : i * stride + (d + 1) * z.cols, :] = shared[
                    d, i * z.cols : (i + 1) * z.cols, :
                ]
    count = z.rows * stride
    across = codes[...].astype(F32).T.astype(BF16)
    for i in range(SPAN):
        term = jnp.dot(
            across, wide_part[i * stride : i * stride + count, :], preferred_element_type=F32
        )
        partial[:, i * z.band : (i + 1) * z.band] = (term * z.scale).astype(BF16)


def finish_kernel(where, parts, momentum, atoms, new_dictionary, new_momentum):
    learning = parts[0].astype(F32)
    for i in range(1, parts.shape[0]):
        learning = learning + parts[i].astype(F32)
    momentum_out = DECAY * momentum[...] + learning
    new_momentum[...] = momentum_out
    weights = atoms[...].astype(F32) + LEARNING * momentum_out
    power = jnp.mean(weights * weights, axis=1, keepdims=True)
    new_dictionary[...] = weights * lax.rsqrt(power + EPSILON)


def kept(x, space=pltpu.VMEM):
    return pltpu.with_memory_space_constraint(x, space)


def call(kernel, outs, inputs, scratch, name, far=0):
    specs = [SMEM] + [HBM] * far + [VMEM] * (len(inputs) - 1 - far)
    where, *others = inputs
    placed = [kept(x, pltpu.HBM) for x in others[:far]] + [kept(x) for x in others[far:]]
    return pl.pallas_call(
        kernel,
        out_shape=outs,
        in_specs=specs,
        out_specs=[VMEM] * len(outs),
        scratch_shapes=scratch,
        compiler_params=PARAMS,
        name=name,
    )(where, *placed)


def shards(picture, membrane, dictionary, momentum):
    site_rows, site_cols, atom_count = membrane.shape
    z = Sizes(site_rows, site_cols, atom_count, dictionary.shape[1])
    rows_n, yx_n, cores_n = (lax.axis_size(a) for a in ("row", "yx", "core"))
    cols_n = yx_n * cores_n
    owned = momentum.shape[0]
    groups = (rows_n, cores_n, owned)
    members = rows_n * cores_n
    grid = (rows_n, cols_n)
    where = jnp.stack([lax.axis_index("row"), lax.axis_index(("yx", "core"))]).astype(jnp.int32)

    def swapped(axis, n, blocks):
        return [lax.ppermute(b, axis, route) for b, route in zip(blocks, partners(n))]

    def sideways(blocks):
        return swapped(("yx", "core"), cols_n, blocks)

    own_v = pltpu.VMEM((z.tall, z.wide_pad, z.lanes), F32)
    side_v = pltpu.VMEM((MARGIN, z.tall_pad, z.lanes), BF16)
    end_v = pltpu.VMEM((z.rim, z.lanes), BF16)
    rim_v = pltpu.VMEM((z.rim, z.lanes), F32)
    tall_v = pltpu.VMEM((z.tall * z.cols, z.band), F32)
    wide_v = pltpu.VMEM((z.tall * z.cols, z.band), BF16)
    flat_v = pltpu.VMEM((z.packed, z.lanes), F32)
    site_v = pltpu.VMEM((z.sites, atom_count), F32)
    outs = [own_v, side_v, side_v]

    own, *sides, pixels, dic, potential, atoms = call(
        functools.partial(first_kernel, z, grid),
        outs
        + [
            pltpu.VMEM((z.sites, z.cell), F32),
            pltpu.VMEM(dictionary.shape, BF16),
            site_v,
            pltpu.VMEM(momentum.shape, BF16),
        ],
        (where, membrane.reshape(z.sites, atom_count), picture, dictionary),
        [
            tall_v,
            pltpu.VMEM((3 * picture.shape[2], z.cell), BF16),
            pltpu.VMEM(picture.shape, F32),
            pltpu.SemaphoreType.DMA((SPAN + 2,)),
        ],
        "first",
        far=3,
    )
    for repeat in range(SWEEPS):
        last = repeat == SWEEPS - 1
        joined, *ends = call(
            functools.partial(side_kernel, z, grid),
            [own_v, end_v, end_v],
            (where, own, *sideways(sides)),
            [rim_v],
            "side",
        )
        ends = swapped("row", rows_n, ends)
        final = [
            jax.ShapeDtypeStruct((z.sites, atom_count), F32),
            pltpu.VMEM((z.packed * 3 // 2, 128), BF16),
            pltpu.VMEM((2 * MARGIN * z.tall_pad, 128), BF16),
            pltpu.VMEM((members, z.sites, atom_count // members), BF16),
        ]
        potential, *rest = call(
            functools.partial(sweep_kernel, z, grid, last, groups),
            final if last else [site_v] + outs,
            (where, potential, joined, *ends, pixels, dic),
            [tall_v, own_v, wide_v, rim_v] + ([own_v, flat_v] if last else []),
            "sweep",
        )
        if not last:
            own, *sides = rest
    final_codes = potential.reshape(membrane.shape)
    packed, outer, shared = rest

    def along_row(block):
        power = rows_n & (rows_n - 1) == 0
        return [block] + [
            lax.ppermute(
                block, "row", [(i ^ x if power else (i + x) % rows_n, i) for i in range(rows_n)]
            )
            for x in range(1, rows_n)
        ]

    outer = lax.ppermute(outer, ("yx", "core"), partners(cols_n)[1])
    packed = along_row(packed)
    shared = lax.all_to_all(shared, ("row", "core"), 0, 0, tiled=True)
    outer = along_row(outer)
    blocks = jnp.stack([jnp.concatenate(b) for b in zip(packed, outer)])
    blocks = lax.all_gather(blocks, "core", axis=0, tiled=False)
    (partial,) = call(
        functools.partial(learn_kernel, z, grid, groups),
        [pltpu.VMEM((atom_count // members, z.patch), BF16)],
        (where, shared, blocks),
        [
            flat_v,
            pltpu.VMEM((cores_n, rows_n, z.tall, z.wide_pad, z.lanes), F32),
            own_v,
            pltpu.VMEM((z.tall * members * z.cols, z.band), BF16),
            pltpu.VMEM((members * z.sites, atom_count // members), BF16),
        ],
        "learn",
    )
    parts = lax.all_to_all(partial.reshape(yx_n, owned, z.patch), "yx", 0, 0, tiled=True)
    new_dictionary, new_momentum = call(
        finish_kernel,
        [jax.ShapeDtypeStruct(momentum.shape, F32)] * 2,
        (where, parts, momentum, atoms),
        [],
        "finish",
    )
    return (final_codes, new_dictionary, new_momentum)


def solution(mesh):
    rows_n, cols_n = (mesh.shape["row"], mesh.shape["col"])
    split = Mesh(mesh.devices.reshape(rows_n, cols_n // 2, 2), ("row", "yx", "core"))
    col = ("yx", "core")
    return jax.shard_map(
        shards,
        mesh=split,
        in_specs=(P(None, "row", col), P("row", col, None), P(), P(("row",) + col, None)),
        out_specs=(P("row", col, None), P(("row",) + col, None), P(("row",) + col, None)),
        check_vma=False,
    )
```

```python
import functools

import jax
import jax.numpy as jnp
from jax import lax
from jax.experimental import pallas as pl
from jax.experimental.pallas import tpu as pltpu
from jax.sharding import Mesh
from jax.sharding import PartitionSpec as P

PATCH_SIDE = 32
STRIDE = 8
SWEEPS = 2
SPAN = PATCH_SIDE // STRIDE
MARGIN = SPAN - 1

THRESHOLD = 0.25
RELAXATION = 0.1
DECAY = 0.9
LEARNING = 0.25
EPSILON = 1e-05


F32 = jnp.float32
BF16 = jnp.bfloat16
VMEM = pl.BlockSpec(memory_space=pltpu.VMEM)
SMEM = pl.BlockSpec(memory_space=pltpu.SMEM)
HBM = pl.BlockSpec(memory_space=pltpu.HBM)
PARAMS = pltpu.CompilerParams(vmem_limit_bytes=24 * 1024 * 1024)


def up_to(value, step):
    return -(-value // step) * step


def shrink(potential):
    return potential - jnp.clip(potential, -THRESHOLD, THRESHOLD)


class Sizes:
    def __init__(self, site_rows, site_cols, atoms, patch_len):
        self.rows, self.cols, self.atoms, self.patch = site_rows, site_cols, atoms, patch_len
        self.cell = patch_len // (SPAN * SPAN)
        self.band = SPAN * self.cell
        self.sites = site_rows * site_cols
        self.tall = site_rows + MARGIN
        self.wide = site_cols + MARGIN
        self.wide_pad = up_to(self.wide, 8)
        self.tall_pad = up_to(self.tall, 16)
        self.lanes = up_to(self.cell, 128)
        self.rim = up_to(MARGIN * self.wide, 16)
        self.packed = up_to(self.tall * self.cols + MARGIN * self.tall_pad, 32)
        self.scale = patch_len ** (-0.5)


class Place:
    def __init__(self, where, rows_n, cols_n):
        self.row, self.col = where[0], where[1]
        self.rows_n, self.cols_n = rows_n, cols_n
        self.owner = self.row * cols_n + self.col

    def pairs(self, axis):
        at, n = (self.row, self.rows_n) if axis == 0 else (self.col, self.cols_n)
        before, after = at > 0, at < n - 1
        odd = at % 2
        return [
            (odd == 0, ((True, after), (False, before))),
            (odd == 1, ((False, before), (True, after))),
        ]


def partners(n):
    even, odd = {}, {}
    for i in range(n):
        even[i] = i ^ 1 if i ^ 1 < n else i
        other = ((i + 1) ^ 1) - 1
        odd[i] = other if 0 <= other < n else (n - 1 if i == 0 and n % 2 == 0 else i)
    if n % 2 == 0:
        odd[n - 1] = 0
    return [sorted(even.items()), sorted(odd.items())]


def reconstruct(z, place, coding, dic, pixels, tall_sum, own, ready=None):
    tall_sum[z.sites :, :] = jnp.zeros((z.tall * z.cols - z.sites, z.band), F32)
    for i in range(SPAN):
        if ready is not None:
            ready(i)
        placed = jnp.dot(
            coding, dic[:, i * z.band : (i + 1) * z.band], preferred_element_type=F32
        )
        start = i * z.cols
        if i == 0:
            tall_sum[0 : z.sites, :] = placed
        else:
            tall_sum[start : start + z.sites, :] += placed
    own[...] = jnp.zeros((z.tall, z.wide_pad, z.lanes), F32)
    own[0 : z.rows, 0 : z.cols, 0 : z.cell] = pixels[...].reshape(z.rows, z.cols, z.cell)
    for j in range(SPAN):
        part = tall_sum[:, j * z.cell : (j + 1) * z.cell].reshape(z.tall, z.cols, z.cell)
        own[:, j : j + z.cols, 0 : z.cell] -= part * z.scale

    @pl.when(place.row == place.rows_n - 1)
    def _():
        own[z.rows :] = jnp.zeros((MARGIN, z.wide_pad, z.lanes), F32)

    @pl.when(place.col == place.cols_n - 1)
    def _():
        own[:, z.cols :] = jnp.zeros((z.tall, z.wide_pad - z.cols, z.lanes), F32)


def send_sides(z, place, own, sends):
    for mine, halves in place.pairs(1):

        @pl.when(mine)
        def _(halves=halves):
            for send, (onward, _) in zip(sends, halves):
                first = z.cols if onward else 0
                for c in range(MARGIN):
                    send[c, 0 : z.tall, :] = own[:, first + c, :].astype(BF16)


def add_sides(z, place, whole, received):
    for mine, halves in place.pairs(1):
        for rim, (onward, there) in zip(received, halves):

            @pl.when(mine & there)
            def _(rim=rim, first=z.cols if onward else 0):
                for c in range(MARGIN):
                    whole[:, first + c, :] += rim[c].astype(F32)[0 : z.tall]


def is_equal(a, b):
    return (a == b).astype(F32).astype(BF16)


def cells_of(z, picture, pixels, spread):
    channels, height, width = picture.shape
    turned = picture[...].reshape(channels * height, width).T
    high = turned.astype(BF16)
    rest = turned - high.astype(F32)
    middle = rest.astype(BF16)
    spread[0:width, :] = high
    spread[width : 2 * width, :] = middle
    spread[2 * width :, :] = (rest - middle.astype(F32)).astype(BF16)

    def iota(shape, dim):
        return lax.broadcasted_iota(jnp.int32, shape, dim)

    shape = (channels * height, z.cell)
    line, entry = iota(shape, 0), iota(shape, 1)
    channel, image_row = line // height, line % height
    away = (
        (channel * STRIDE + image_row % STRIDE) * STRIDE
        + image_row // STRIDE * z.cell
        - entry // STRIDE * STRIDE
    )
    shape = (width, z.cell)
    mine = (iota(shape, 0) % STRIDE == iota(shape, 1) % STRIDE).astype(F32)
    for i in range(z.rows):
        moved = jnp.dot(
            spread[...], is_equal(away, i * z.cell), preferred_element_type=F32
        )
        whole = (moved[0:width] + moved[width : 2 * width]) + moved[2 * width :]
        whole = (whole * mine).reshape(z.cols, STRIDE, z.cell)
        pixels[i * z.cols : (i + 1) * z.cols, :] = jnp.sum(whole, axis=1)


def first_kernel(
    z, grid, where, membrane, picture, source, own, *rest
):
    (*sends, pixels, dic, potential, atoms, tall_sum, spread, drawing, sems) = rest
    place = Place(where, *grid)
    early = [
        pltpu.make_async_copy(picture, drawing, sems.at[SPAN]),
        pltpu.make_async_copy(membrane, potential, sems.at[SPAN + 1]),
    ]
    copies = [
        pltpu.make_async_copy(
            source.at[:, i * z.band : (i + 1) * z.band],
            dic.at[:, i * z.band : (i + 1) * z.band],
            sems.at[i],
        )
        for i in range(SPAN)
    ]
    for copy in early + copies:
        copy.start()
    early[0].wait()
    cells_of(z, drawing, pixels, spread)
    early[1].wait()
    coding = shrink(potential[...]).astype(BF16)
    reconstruct(z, place, coding, dic, pixels, tall_sum, own, lambda i: copies[i].wait())
    send_sides(z, place, own, sends)
    owned = atoms.shape[0]
    atoms[...] = dic[pl.ds(pl.multiple_of(place.owner * owned, owned), owned), :]


def side_kernel(z, grid, where, own, from_even, from_odd, joined, even, odd, rim):
    place = Place(where, *grid)
    joined[...] = own[...]
    add_sides(z, place, joined, (from_even, from_odd))
    rim[MARGIN * z.wide :, :] = jnp.zeros((z.rim - MARGIN * z.wide, z.lanes), F32)
    for mine, halves in place.pairs(0):

        @pl.when(mine)
        def _(halves=halves):
            for send, (onward, _) in zip((even, odd), halves):
                first = z.rows if onward else 0
                for r in range(MARGIN):
                    start = MARGIN * z.cols + r * MARGIN
                    rim[r * z.cols : (r + 1) * z.cols, :] = joined[first + r, 0 : z.cols, :]
                    rim[start : start + MARGIN, :] = joined[first + r, z.cols : z.wide, :]
                send[...] = rim[...].astype(BF16)


def add_ends(z, place, whole, received, rim):
    for mine, halves in place.pairs(0):
        for block, (onward, there) in zip(received, halves):

            @pl.when(mine & there)
            def _(block=block, first=z.rows if onward else 0):
                rim[...] = block[...].astype(F32)
                for r in range(MARGIN):
                    start = MARGIN * z.cols + r * MARGIN
                    whole[first + r, 0 : z.cols, :] += rim[r * z.cols : (r + 1) * z.cols, :]
                    whole[first + r, z.cols : z.wide, :] += rim[start : start + MARGIN, :]


def windows_of(z, whole, wide_part, first_row, row_stride):
    for j in range(SPAN):
        part = whole[:, j : j + z.cols, 0 : z.cell].astype(BF16)
        for p in range(z.tall):
            wide_part[
                pl.ds(p * row_stride + first_row, z.cols), j * z.cell : (j + 1) * z.cell
            ] = part[p]


def sweep_kernel(
    z, grid, last, where, potential, joined, from_even, from_odd, pixels, dic, *rest
):
    if last:
        new_potential, own, *sends, codes, tall_sum, whole, wide_part, rim = rest
    else:
        new_potential, own, *sends, tall_sum, whole, wide_part, rim = rest
    place = Place(where, *grid)
    whole[...] = joined[...]
    add_ends(z, place, whole, (from_even, from_odd), rim)
    windows_of(z, whole, wide_part, 0, z.cols)
    drive = None
    for i in range(SPAN):
        term = lax.dot_general(
            wide_part[i * z.cols : i * z.cols + z.sites, :],
            dic[:, i * z.band : (i + 1) * z.band],
            (((1,), (1,)), ((), ())),
            preferred_element_type=F32,
        )
        drive = term if drive is None else drive + term
    old = potential[...]
    updated = old + RELAXATION * (drive * z.scale + shrink(old) - old)
    active = shrink(updated)
    coding = active.astype(BF16)
    if last:
        new_potential[...] = active
        codes[...] = coding
    else:
        new_potential[...] = updated
    reconstruct(z, place, coding, dic, pixels, tall_sum, own)
    send_sides(z, place, own, sends)


def sort_kernel(z, groups, where, codes, _, shared):
    rows_n, cores_n, owned = groups
    span = z.atoms // rows_n
    src = lax.broadcasted_iota(jnp.int32, (span, span), 0)
    dst = lax.broadcasted_iota(jnp.int32, (span, span), 1)
    per_core = span // cores_n
    core, rem = dst // per_core, dst % per_core
    wanted = (rem // owned) * (owned * cores_n) + core * owned + rem % owned
    order = is_equal(src, wanted)
    for r in range(rows_n):
        line = jnp.dot(codes[:, r * span : (r + 1) * span], order, preferred_element_type=F32)
        for k in range(cores_n):
            shared[r * cores_n + k] = line[:, k * per_core : (k + 1) * per_core].astype(BF16)


def pack_kernel(z, grid, where, own, from_even, from_odd, packed, joined, flat):
    joined[...] = own[...]
    add_sides(z, Place(where, *grid), joined, (from_even, from_odd))
    base = z.tall * z.cols
    flat[base:, :] = jnp.zeros((z.packed - base, z.lanes), F32)
    for p in range(z.tall):
        flat[p * z.cols : (p + 1) * z.cols, :] = joined[p, 0 : z.cols, :]
    for c in range(MARGIN):
        start = base + c * z.tall_pad
        flat[start : start + z.tall, :] = joined[:, z.cols + c, :]
    half = z.packed // 2
    packed[0 : z.packed, :] = flat[:, 0:128].astype(BF16)
    tail = z.cell - 128
    ends = jnp.concatenate([flat[0:half, 128 : z.cell], flat[half:, 128 : z.cell]], axis=1)
    packed[z.packed :, 0 : 2 * tail] = ends.astype(BF16)


def offset(at, step, n):
    return at ^ step if n & (n - 1) == 0 else (at + step) % n


def learn_half(z, grid, where, across, wide_part, stride, bands, outs, partial):
    count = z.rows * stride
    for n, i in enumerate(bands):
        term = jnp.dot(
            across, wide_part[i * stride : i * stride + count, :], preferred_element_type=F32
        )
        partial[:, n * z.band : (n + 1) * z.band] = (term * z.scale).astype(BF16)
    owned = outs[0].shape[0]
    place = Place(where, *grid)
    for step, out in enumerate(outs):
        at = offset(place.col // 2, step, len(outs))
        out[...] = partial[pl.ds(pl.multiple_of(at * owned, owned), owned), :]


def learn_kernel(z, grid, groups, yx_n, where, shared, *rest):
    rows_n, cores_n, _ = groups
    members = rows_n * cores_n
    near, far, outs = rest[:rows_n], rest[rows_n : 2 * rows_n], rest[2 * rows_n :]
    outs, (across, wide_part, partial, flat, whole, codes) = outs[:yx_n], outs[yx_n:]
    stride = members * z.cols
    base = z.tall * z.cols
    half = z.packed // 2
    tail = z.cell - 128
    place = Place(where, *grid)
    mine = place.col % 2

    for x in range(rows_n):
        d = offset(place.row, x, rows_n)
        for k, block in ((mine, near[x]), (1 - mine, far[x])):
            flat[k, d, :, 0:128] = block[0 : z.packed, :].astype(F32)
            ends = block[z.packed :, :].astype(F32)
            flat[k, d, 0:half, 128 : z.cell] = ends[:, 0:tail]
            flat[k, d, half:, 128 : z.cell] = ends[:, tail : 2 * tail]
    for k in range(cores_n):
        for r in range(rows_n):
            d = r * cores_n + k
            for source, low, high, at in (
                (r, 0, z.tall, 0),
                (r - 1, z.rows, z.tall, 0),
                (r + 1, 0, MARGIN, z.rows),
            ):
                if not 0 <= source < rows_n:
                    continue
                n = high - low
                main = flat[k, source, low * z.cols : high * z.cols, :]
                main = main.reshape(n, z.cols, z.lanes)
                side = [
                    flat[k, source, base + c * z.tall_pad + low : base + c * z.tall_pad + high, :]
                    for c in range(MARGIN)
                ]
                if source == r:
                    whole[at : at + n, 0 : z.cols, :] = main
                    for c in range(MARGIN):
                        whole[at : at + n, z.cols + c, :] = side[c]
                else:
                    whole[at : at + n, 0 : z.cols, :] += main
                    for c in range(MARGIN):
                        whole[at : at + n, z.cols + c, :] += side[c]
            windows_of(z, whole, wide_part, d * z.cols, stride)
            for i in range(z.rows):
                codes[i * stride + d * z.cols : i * stride + (d + 1) * z.cols, :] = shared[
                    d, i * z.cols : (i + 1) * z.cols, :
                ]
    across[...] = codes[...].astype(F32).T.astype(BF16)
    learn_half(
        z, grid, where, across[...], wide_part, stride, range(SPAN // 2), outs, partial
    )


def rest_kernel(z, grid, stride, where, across, wide_part, *rest):
    *outs, partial = rest
    learn_half(
        z, grid, where, across[...], wide_part, stride, range(SPAN // 2, SPAN), outs, partial
    )


def finish_kernel(z, yx_n, where, momentum, atoms, *rest):
    *parts, new_dictionary, new_momentum = rest
    width = z.patch // 2
    power = 0.0
    for h in range(2):
        lanes = pl.ds(h * width, width)
        learning = parts[h * yx_n][...].astype(F32)
        for part in parts[h * yx_n + 1 : (h + 1) * yx_n]:
            learning = learning + part[...].astype(F32)
        momentum_out = DECAY * momentum[:, lanes] + learning
        new_momentum[:, lanes] = momentum_out
        weights = atoms[:, lanes].astype(F32) + LEARNING * momentum_out
        new_dictionary[:, lanes] = weights
        power = power + jnp.sum(weights * weights, axis=1, keepdims=True)
    norm = lax.rsqrt(power * (1.0 / z.patch) + EPSILON)
    new_dictionary[...] = new_dictionary[...] * norm


def kept(x, space=pltpu.VMEM):
    return pltpu.with_memory_space_constraint(x, space)


def call(kernel, outs, inputs, scratch, name, far=0):
    specs = [SMEM] + [HBM] * far + [VMEM] * (len(inputs) - 1 - far)
    where, *others = inputs
    placed = [kept(x, pltpu.HBM) for x in others[:far]] + [kept(x) for x in others[far:]]
    return pl.pallas_call(
        kernel,
        out_shape=outs,
        in_specs=specs,
        out_specs=[VMEM] * len(outs),
        scratch_shapes=scratch,
        compiler_params=PARAMS,
        name=name,
    )(where, *placed)


def shards(picture, membrane, dictionary, momentum):
    site_rows, site_cols, atom_count = membrane.shape
    z = Sizes(site_rows, site_cols, atom_count, dictionary.shape[1])
    rows_n, yx_n, cores_n = (lax.axis_size(a) for a in ("row", "yx", "core"))
    cols_n = yx_n * cores_n
    owned = momentum.shape[0]
    groups = (rows_n, cores_n, owned)
    members = rows_n * cores_n
    grid = (rows_n, cols_n)
    where = jnp.stack([lax.axis_index("row"), lax.axis_index(("yx", "core"))]).astype(jnp.int32)

    def swapped(axis, n, blocks):
        return [lax.ppermute(b, axis, route) for b, route in zip(blocks, partners(n))]

    def sideways(blocks):
        return swapped(("yx", "core"), cols_n, blocks)

    own_v = pltpu.VMEM((z.tall, z.wide_pad, z.lanes), F32)
    side_v = pltpu.VMEM((MARGIN, z.tall_pad, z.lanes), BF16)
    end_v = pltpu.VMEM((z.rim, z.lanes), BF16)
    rim_v = pltpu.VMEM((z.rim, z.lanes), F32)
    tall_v = pltpu.VMEM((z.tall * z.cols, z.band), F32)
    wide_v = pltpu.VMEM((z.tall * z.cols, z.band), BF16)
    flat_v = pltpu.VMEM((z.packed, z.lanes), F32)
    site_v = pltpu.VMEM((z.sites, atom_count), F32)
    outs = [own_v, side_v, side_v]

    own, *sides, pixels, dic, potential, atoms = call(
        functools.partial(first_kernel, z, grid),
        outs
        + [
            pltpu.VMEM((z.sites, z.cell), F32),
            pltpu.VMEM(dictionary.shape, BF16),
            site_v,
            pltpu.VMEM(momentum.shape, BF16),
        ],
        (where, membrane.reshape(z.sites, atom_count), picture, dictionary),
        [
            tall_v,
            pltpu.VMEM((3 * picture.shape[2], z.cell), BF16),
            pltpu.VMEM(picture.shape, F32),
            pltpu.SemaphoreType.DMA((SPAN + 2,)),
        ],
        "first",
        far=3,
    )
    for repeat in range(SWEEPS):
        last = repeat == SWEEPS - 1
        joined, *ends = call(
            functools.partial(side_kernel, z, grid),
            [own_v, end_v, end_v],
            (where, own, *sideways(sides)),
            [rim_v],
            "side",
        )
        ends = swapped("row", rows_n, ends)
        final = [
            jax.ShapeDtypeStruct((z.sites, atom_count), F32),
            *outs,
            pltpu.VMEM((z.sites, atom_count), BF16),
        ]
        potential, own, *rest = call(
            functools.partial(sweep_kernel, z, grid, last),
            final if last else [site_v] + outs,
            (where, potential, joined, *ends, pixels, dic),
            [tall_v, own_v, wide_v, rim_v],
            "sweep",
        )
        sides = rest[:2]
    final_codes = potential.reshape(membrane.shape)
    sides = sideways(sides)
    (shared,) = call(
        functools.partial(sort_kernel, z, groups),
        [pltpu.VMEM((members, z.sites, atom_count // members), BF16)],
        (where, rest[2], sides[0]),
        [],
        "sort",
    )
    shared = lax.all_to_all(shared, ("row", "core"), 0, 0, tiled=True)
    (packed,) = call(
        functools.partial(pack_kernel, z, grid),
        [pltpu.VMEM((z.packed * 3 // 2, 128), BF16)],
        (where, own, *sides),
        [own_v, flat_v],
        "pack",
    )

    def met(block, axis, n, step):
        return lax.ppermute(block, axis, [(i, offset(i, step, n)) for i in range(n)])

    power = rows_n & (rows_n - 1) == 0
    near = [packed] + [
        met(packed, "row", rows_n, x if power else rows_n - x) for x in range(1, rows_n)
    ]
    far = [met(block, "core", 2, 1) for block in near]
    stride = members * z.cols
    group_atoms = atom_count // members
    half_v = pltpu.VMEM((owned, z.patch // 2), BF16)
    partial_v = pltpu.VMEM((group_atoms, z.patch // 2), BF16)
    *first_half, across, wide_part = call(
        functools.partial(learn_kernel, z, grid, groups, yx_n),
        [half_v] * yx_n
        + [
            pltpu.VMEM((group_atoms, members * z.sites), BF16),
            pltpu.VMEM((z.tall * stride, z.band), BF16),
        ],
        (where, shared, *near, *far),
        [
            partial_v,
            pltpu.VMEM((cores_n, rows_n, z.packed, z.lanes), F32),
            own_v,
            pltpu.VMEM((members * z.sites, group_atoms), BF16),
        ],
        "learn",
    )
    other_half = call(
        functools.partial(rest_kernel, z, grid, stride),
        [half_v] * yx_n,
        (where, across, wide_part),
        [partial_v],
        "rest",
    )
    parts = [
        block if step == 0 else met(block, "yx", yx_n, step)
        for half in (first_half, other_half)
        for step, block in enumerate(half)
    ]
    new_dictionary, new_momentum = call(
        functools.partial(finish_kernel, z, yx_n),
        [jax.ShapeDtypeStruct(momentum.shape, F32)] * 2,
        (where, momentum, atoms, *parts),
        [],
        "finish",
    )
    return (final_codes, new_dictionary, new_momentum)


def solution(mesh):
    rows_n, cols_n = (mesh.shape["row"], mesh.shape["col"])
    split = Mesh(mesh.devices.reshape(rows_n, cols_n // 2, 2), ("row", "yx", "core"))
    col = ("yx", "core")
    return jax.shard_map(
        shards,
        mesh=split,
        in_specs=(P(None, "row", col), P("row", col, None), P(), P(("row",) + col, None)),
        out_specs=(P("row", col, None), P(("row",) + col, None), P(("row",) + col, None)),
        check_vma=False,
    )
```

```python
import functools

import jax
import jax.numpy as jnp
from jax import lax
from jax.experimental import pallas as pl
from jax.experimental.pallas import tpu as pltpu
from jax.sharding import Mesh
from jax.sharding import PartitionSpec as P


PATCH_SIDE = 32
STRIDE = 8
SWEEPS = 2
SPAN = PATCH_SIDE // STRIDE
MARGIN = SPAN - 1

THRESHOLD = 0.25
RELAXATION = 0.1
DECAY = 0.9
LEARNING = 0.25
EPSILON = 1e-05


F32 = jnp.float32
BF16 = jnp.bfloat16
VMEM = pl.BlockSpec(memory_space=pltpu.VMEM)
SMEM = pl.BlockSpec(memory_space=pltpu.SMEM)
HBM = pl.BlockSpec(memory_space=pltpu.HBM)
PARAMS = pltpu.CompilerParams(vmem_limit_bytes=24 * 1024 * 1024)


def up_to(value, step):
    return -(-value // step) * step


def shrink(potential):
    return potential - jnp.clip(potential, -THRESHOLD, THRESHOLD)


class Sizes:
    def __init__(self, site_rows, site_cols, atoms, patch_len):
        self.rows, self.cols, self.atoms, self.patch = site_rows, site_cols, atoms, patch_len
        self.cell = patch_len // (SPAN * SPAN)
        self.band = SPAN * self.cell
        self.sites = site_rows * site_cols
        self.tall = site_rows + MARGIN
        self.wide = site_cols + MARGIN
        self.wide_pad = up_to(self.wide, 8)
        self.tall_pad = up_to(self.tall, 16)
        self.lanes = up_to(self.cell, 128)
        self.rim = up_to(MARGIN * self.wide, 16)
        self.packed = up_to(self.tall * self.cols + MARGIN * self.tall_pad, 32)
        self.scale = patch_len ** (-0.5)


class Place:
    def __init__(self, where, rows_n, cols_n):
        self.row, self.col = where[0], where[1]
        self.rows_n, self.cols_n = rows_n, cols_n
        self.owner = self.row * cols_n + self.col

    def pairs(self, axis):
        at, n = (self.row, self.rows_n) if axis == 0 else (self.col, self.cols_n)
        before, after = at > 0, at < n - 1
        odd = at % 2
        return [
            (odd == 0, ((True, after), (False, before))),
            (odd == 1, ((False, before), (True, after))),
        ]


def partners(n):
    even, odd = {}, {}
    for i in range(n):
        even[i] = i ^ 1 if i ^ 1 < n else i
        other = ((i + 1) ^ 1) - 1
        odd[i] = other if 0 <= other < n else (n - 1 if i == 0 and n % 2 == 0 else i)
    if n % 2 == 0:
        odd[n - 1] = 0
    return [sorted(even.items()), sorted(odd.items())]


def reconstruct(z, place, coding, dic, pixels, tall_sum, own, ready=None):
    tall_sum[z.sites :, :] = jnp.zeros((z.tall * z.cols - z.sites, z.band), F32)
    for i in range(SPAN):
        if ready is not None:
            ready(i)
        placed = jnp.dot(
            coding, dic[:, i * z.band : (i + 1) * z.band], preferred_element_type=F32
        )
        start = i * z.cols
        if i == 0:
            tall_sum[0 : z.sites, :] = placed
        else:
            tall_sum[start : start + z.sites, :] += placed
    own[...] = jnp.zeros((z.tall, z.wide_pad, z.lanes), F32)
    own[0 : z.rows, 0 : z.cols, 0 : z.cell] = pixels[...].reshape(z.rows, z.cols, z.cell)
    for j in range(SPAN):
        part = tall_sum[:, j * z.cell : (j + 1) * z.cell].reshape(z.tall, z.cols, z.cell)
        own[:, j : j + z.cols, 0 : z.cell] -= part * z.scale

    @pl.when(place.row == place.rows_n - 1)
    def _():
        own[z.rows :] = jnp.zeros((MARGIN, z.wide_pad, z.lanes), F32)

    @pl.when(place.col == place.cols_n - 1)
    def _():
        own[:, z.cols :] = jnp.zeros((z.tall, z.wide_pad - z.cols, z.lanes), F32)


def send_sides(z, place, own, sends):
    for mine, halves in place.pairs(1):

        @pl.when(mine)
        def _(halves=halves):
            for send, (onward, _) in zip(sends, halves):
                first = z.cols if onward else 0
                for c in range(MARGIN):
                    send[c, 0 : z.tall, :] = own[:, first + c, :].astype(BF16)


def add_sides(z, place, whole, received):
    for mine, halves in place.pairs(1):
        for rim, (onward, there) in zip(received, halves):

            @pl.when(mine & there)
            def _(rim=rim, first=z.cols if onward else 0):
                for c in range(MARGIN):
                    whole[:, first + c, :] += rim[c].astype(F32)[0 : z.tall]


def is_equal(a, b):
    return (a == b).astype(F32).astype(BF16)


def cells_of(z, picture, pixels, spread):
    channels, height, width = picture.shape
    turned = picture[...].reshape(channels * height, width).T
    high = turned.astype(BF16)
    rest = turned - high.astype(F32)
    middle = rest.astype(BF16)
    spread[0:width, :] = high
    spread[width : 2 * width, :] = middle
    spread[2 * width :, :] = (rest - middle.astype(F32)).astype(BF16)

    def iota(shape, dim):
        return lax.broadcasted_iota(jnp.int32, shape, dim)

    shape = (channels * height, z.cell)
    line, entry = iota(shape, 0), iota(shape, 1)
    channel, image_row = line // height, line % height
    away = (
        (channel * STRIDE + image_row % STRIDE) * STRIDE
        + image_row // STRIDE * z.cell
        - entry // STRIDE * STRIDE
    )
    shape = (width, z.cell)
    mine = (iota(shape, 0) % STRIDE == iota(shape, 1) % STRIDE).astype(F32)
    for i in range(z.rows):
        moved = jnp.dot(
            spread[...], is_equal(away, i * z.cell), preferred_element_type=F32
        )
        whole = (moved[0:width] + moved[width : 2 * width]) + moved[2 * width :]
        whole = (whole * mine).reshape(z.cols, STRIDE, z.cell)
        pixels[i * z.cols : (i + 1) * z.cols, :] = jnp.sum(whole, axis=1)


def first_kernel(
    z, grid, where, membrane, picture, source, own, *rest
):
    (*sends, pixels, dic, potential, atoms, tall_sum, spread, drawing, sems) = rest
    place = Place(where, *grid)
    early = [
        pltpu.make_async_copy(picture, drawing, sems.at[SPAN]),
        pltpu.make_async_copy(membrane, potential, sems.at[SPAN + 1]),
    ]
    copies = [
        pltpu.make_async_copy(
            source.at[:, i * z.band : (i + 1) * z.band],
            dic.at[:, i * z.band : (i + 1) * z.band],
            sems.at[i],
        )
        for i in range(SPAN)
    ]
    for copy in early + copies:
        copy.start()
    early[0].wait()
    cells_of(z, drawing, pixels, spread)
    early[1].wait()
    coding = shrink(potential[...]).astype(BF16)
    reconstruct(z, place, coding, dic, pixels, tall_sum, own, lambda i: copies[i].wait())
    send_sides(z, place, own, sends)
    owned = atoms.shape[0]
    atoms[...] = dic[pl.ds(pl.multiple_of(place.owner * owned, owned), owned), :]


def side_kernel(z, grid, where, own, from_even, from_odd, joined, even, odd, rim):
    place = Place(where, *grid)
    joined[...] = own[...]
    add_sides(z, place, joined, (from_even, from_odd))
    rim[MARGIN * z.wide :, :] = jnp.zeros((z.rim - MARGIN * z.wide, z.lanes), F32)
    for mine, halves in place.pairs(0):

        @pl.when(mine)
        def _(halves=halves):
            for send, (onward, _) in zip((even, odd), halves):
                first = z.rows if onward else 0
                for r in range(MARGIN):
                    start = MARGIN * z.cols + r * MARGIN
                    rim[r * z.cols : (r + 1) * z.cols, :] = joined[first + r, 0 : z.cols, :]
                    rim[start : start + MARGIN, :] = joined[first + r, z.cols : z.wide, :]
                send[...] = rim[...].astype(BF16)


def add_ends(z, place, whole, received, rim):
    for mine, halves in place.pairs(0):
        for block, (onward, there) in zip(received, halves):

            @pl.when(mine & there)
            def _(block=block, first=z.rows if onward else 0):
                rim[...] = block[...].astype(F32)
                for r in range(MARGIN):
                    start = MARGIN * z.cols + r * MARGIN
                    whole[first + r, 0 : z.cols, :] += rim[r * z.cols : (r + 1) * z.cols, :]
                    whole[first + r, z.cols : z.wide, :] += rim[start : start + MARGIN, :]


def windows_of(z, whole, wide_part, first_row, row_stride):
    for j in range(SPAN):
        part = whole[:, j : j + z.cols, 0 : z.cell].astype(BF16)
        for p in range(z.tall):
            wide_part[
                pl.ds(p * row_stride + first_row, z.cols), j * z.cell : (j + 1) * z.cell
            ] = part[p]


def sweep_kernel(
    z, grid, last, where, potential, joined, from_even, from_odd, pixels, dic, *rest
):
    if last:
        new_potential, own, *sends, codes, tall_sum, whole, wide_part, rim = rest
    else:
        new_potential, own, *sends, tall_sum, whole, wide_part, rim = rest
    place = Place(where, *grid)
    whole[...] = joined[...]
    add_ends(z, place, whole, (from_even, from_odd), rim)
    windows_of(z, whole, wide_part, 0, z.cols)
    drive = None
    for i in range(SPAN):
        term = lax.dot_general(
            wide_part[i * z.cols : i * z.cols + z.sites, :],
            dic[:, i * z.band : (i + 1) * z.band],
            (((1,), (1,)), ((), ())),
            preferred_element_type=F32,
        )
        drive = term if drive is None else drive + term
    old = potential[...]
    updated = old + RELAXATION * (drive * z.scale + shrink(old) - old)
    active = shrink(updated)
    coding = active.astype(BF16)
    if last:
        new_potential[...] = active
        codes[...] = coding
    else:
        new_potential[...] = updated
    reconstruct(z, place, coding, dic, pixels, tall_sum, own)
    send_sides(z, place, own, sends)


def sort_kernel(z, groups, where, codes, _, shared):
    rows_n, cores_n, owned = groups
    span = z.atoms // rows_n
    src = lax.broadcasted_iota(jnp.int32, (span, span), 0)
    dst = lax.broadcasted_iota(jnp.int32, (span, span), 1)
    per_core = span // cores_n
    core, rem = dst // per_core, dst % per_core
    wanted = (rem // owned) * (owned * cores_n) + core * owned + rem % owned
    order = is_equal(src, wanted)
    for r in range(rows_n):
        line = jnp.dot(codes[:, r * span : (r + 1) * span], order, preferred_element_type=F32)
        for k in range(cores_n):
            shared[r * cores_n + k] = line[:, k * per_core : (k + 1) * per_core].astype(BF16)


def pack_kernel(z, grid, where, own, from_even, from_odd, packed, joined, flat):
    joined[...] = own[...]
    add_sides(z, Place(where, *grid), joined, (from_even, from_odd))
    base = z.tall * z.cols
    flat[base:, :] = jnp.zeros((z.packed - base, z.lanes), F32)
    for p in range(z.tall):
        flat[p * z.cols : (p + 1) * z.cols, :] = joined[p, 0 : z.cols, :]
    for c in range(MARGIN):
        start = base + c * z.tall_pad
        flat[start : start + z.tall, :] = joined[:, z.cols + c, :]
    half = z.packed // 2
    packed[0 : z.packed, :] = flat[:, 0:128].astype(BF16)
    tail = z.cell - 128
    ends = jnp.concatenate([flat[0:half, 128 : z.cell], flat[half:, 128 : z.cell]], axis=1)
    packed[z.packed :, 0 : 2 * tail] = ends.astype(BF16)


def offset(at, step, n):
    return at ^ step if n & (n - 1) == 0 else (at + step) % n


def learn_half(z, grid, where, across, wide_part, stride, bands, outs, partial):
    count = z.rows * stride
    for n, i in enumerate(bands):
        term = jnp.dot(
            across, wide_part[i * stride : i * stride + count, :], preferred_element_type=F32
        )
        partial[:, n * z.band : (n + 1) * z.band] = (term * z.scale).astype(BF16)
    owned = outs[0].shape[0]
    place = Place(where, *grid)
    for step, out in enumerate(outs):
        at = offset(place.col // 2, step, len(outs))
        out[...] = partial[pl.ds(pl.multiple_of(at * owned, owned), owned), :]


def learn_kernel(z, grid, groups, yx_n, where, shared, *rest):
    rows_n, cores_n, _ = groups
    members = rows_n * cores_n
    near, far, outs = rest[:rows_n], rest[rows_n : 2 * rows_n], rest[2 * rows_n :]
    outs, (across, wide_part, partial, flat, whole, codes) = outs[:yx_n], outs[yx_n:]
    stride = members * z.cols
    base = z.tall * z.cols
    half = z.packed // 2
    tail = z.cell - 128
    place = Place(where, *grid)
    mine = place.col % 2

    for x in range(rows_n):
        d = offset(place.row, x, rows_n)
        for k, block in ((mine, near[x]), (1 - mine, far[x])):
            flat[k, d, :, 0:128] = block[0 : z.packed, :].astype(F32)
            ends = block[z.packed :, :].astype(F32)
            flat[k, d, 0:half, 128 : z.cell] = ends[:, 0:tail]
            flat[k, d, half:, 128 : z.cell] = ends[:, tail : 2 * tail]
    for k in range(cores_n):
        for r in range(rows_n):
            d = r * cores_n + k
            for source, low, high, at in (
                (r, 0, z.tall, 0),
                (r - 1, z.rows, z.tall, 0),
                (r + 1, 0, MARGIN, z.rows),
            ):
                if not 0 <= source < rows_n:
                    continue
                n = high - low
                main = flat[k, source, low * z.cols : high * z.cols, :]
                main = main.reshape(n, z.cols, z.lanes)
                side = [
                    flat[k, source, base + c * z.tall_pad + low : base + c * z.tall_pad + high, :]
                    for c in range(MARGIN)
                ]
                if source == r:
                    whole[at : at + n, 0 : z.cols, :] = main
                    for c in range(MARGIN):
                        whole[at : at + n, z.cols + c, :] = side[c]
                else:
                    whole[at : at + n, 0 : z.cols, :] += main
                    for c in range(MARGIN):
                        whole[at : at + n, z.cols + c, :] += side[c]
            windows_of(z, whole, wide_part, d * z.cols, stride)
            for i in range(z.rows):
                codes[i * stride + d * z.cols : i * stride + (d + 1) * z.cols, :] = shared[
                    d, i * z.cols : (i + 1) * z.cols, :
                ]
    across[...] = codes[...].astype(F32).T.astype(BF16)
    learn_half(
        z, grid, where, across[...], wide_part, stride, range(SPAN // 2), outs, partial
    )


def rest_kernel(z, grid, stride, where, across, wide_part, *rest):
    *outs, partial = rest
    learn_half(
        z, grid, where, across[...], wide_part, stride, range(SPAN // 2, SPAN), outs, partial
    )


def finish_kernel(z, yx_n, where, momentum, atoms, *rest):
    *parts, new_dictionary, new_momentum, weights, updated, sems = rest
    width = z.patch // 2
    power = 0.0
    copies = []
    for h in range(2):
        lanes = pl.ds(h * width, width)
        learning = parts[h * yx_n][...].astype(F32)
        for part in parts[h * yx_n + 1 : (h + 1) * yx_n]:
            learning = learning + part[...].astype(F32)
        momentum_out = DECAY * momentum[:, lanes] + learning
        updated[:, lanes] = momentum_out
        copies.append(
            pltpu.make_async_copy(updated.at[:, lanes], new_momentum.at[:, lanes], sems.at[h])
        )
        copies[-1].start()
        weight = atoms[:, lanes].astype(F32) + LEARNING * momentum_out
        weights[:, lanes] = weight
        power = power + jnp.sum(weight * weight, axis=1, keepdims=True)
    norm = lax.rsqrt(power * (1.0 / z.patch) + EPSILON)
    for h in range(2):
        lanes = pl.ds(h * width, width)
        weights[:, lanes] = weights[:, lanes] * norm
        copies.append(
            pltpu.make_async_copy(
                weights.at[:, lanes], new_dictionary.at[:, lanes], sems.at[2 + h]
            )
        )
        copies[-1].start()
    for copy in copies:
        copy.wait()


def kept(x, space=pltpu.VMEM):
    return pltpu.with_memory_space_constraint(x, space)


def call(kernel, outs, inputs, scratch, far=0, leave=VMEM):
    specs = [SMEM] + [HBM] * far + [VMEM] * (len(inputs) - 1 - far)
    where, *others = inputs
    placed = [kept(x, pltpu.HBM) for x in others[:far]] + [kept(x) for x in others[far:]]
    return pl.pallas_call(
        kernel,
        out_shape=outs,
        in_specs=specs,
        out_specs=[leave] * len(outs),
        scratch_shapes=scratch,
        compiler_params=PARAMS,
    )(where, *placed)


def shards(picture, membrane, dictionary, momentum):
    site_rows, site_cols, atom_count = membrane.shape
    z = Sizes(site_rows, site_cols, atom_count, dictionary.shape[1])
    rows_n, yx_n, cores_n = (lax.axis_size(a) for a in ("row", "yx", "core"))
    cols_n = yx_n * cores_n
    owned = momentum.shape[0]
    groups = (rows_n, cores_n, owned)
    members = rows_n * cores_n
    grid = (rows_n, cols_n)
    where = jnp.stack([lax.axis_index("row"), lax.axis_index(("yx", "core"))]).astype(jnp.int32)

    def swapped(axis, n, blocks):
        return [lax.ppermute(b, axis, route) for b, route in zip(blocks, partners(n))]

    def sideways(blocks):
        even, odd = partners(cols_n)
        near_rim = lax.ppermute(blocks[0], ("yx", "core"), even)
        far_rim = lax.ppermute(blocks[1], ("yx", "core"), odd)
        return [near_rim, far_rim]

    own_v = pltpu.VMEM((z.tall, z.wide_pad, z.lanes), F32)
    side_v = pltpu.VMEM((MARGIN, z.tall_pad, z.lanes), BF16)
    end_v = pltpu.VMEM((z.rim, z.lanes), BF16)
    rim_v = pltpu.VMEM((z.rim, z.lanes), F32)
    tall_v = pltpu.VMEM((z.tall * z.cols, z.band), F32)
    wide_v = pltpu.VMEM((z.tall * z.cols, z.band), BF16)
    flat_v = pltpu.VMEM((z.packed, z.lanes), F32)
    site_v = pltpu.VMEM((z.sites, atom_count), F32)
    outs = [own_v, side_v, side_v]

    own, *sides, pixels, dic, potential, atoms = call(
        functools.partial(first_kernel, z, grid),
        outs
        + [
            pltpu.VMEM((z.sites, z.cell), F32),
            pltpu.VMEM(dictionary.shape, BF16),
            site_v,
            pltpu.VMEM(momentum.shape, BF16),
        ],
        (where, membrane.reshape(z.sites, atom_count), picture, dictionary),
        [
            tall_v,
            pltpu.VMEM((3 * picture.shape[2], z.cell), BF16),
            pltpu.VMEM(picture.shape, F32),
            pltpu.SemaphoreType.DMA((SPAN + 2,)),
        ],
        far=3,
    )
    for repeat in range(SWEEPS):
        last = repeat == SWEEPS - 1
        joined, *ends = call(
            functools.partial(side_kernel, z, grid),
            [own_v, end_v, end_v],
            (where, own, *sideways(sides)),
            [rim_v],
        )
        ends = swapped("row", rows_n, ends)
        final = [
            site_v,
            *outs,
            pltpu.VMEM((z.sites, atom_count), BF16),
        ]
        potential, own, *rest = call(
            functools.partial(sweep_kernel, z, grid, last),
            final if last else [site_v] + outs,
            (where, potential, joined, *ends, pixels, dic),
            [tall_v, own_v, wide_v, rim_v],
        )
        sides = rest[:2]
    final_codes = potential.reshape(membrane.shape)
    sides = sideways(sides)
    (shared,) = call(
        functools.partial(sort_kernel, z, groups),
        [pltpu.VMEM((members, z.sites, atom_count // members), BF16)],
        (where, rest[2], sides[0]),
        [],
    )
    shared = lax.all_to_all(shared, ("row", "core"), 0, 0, tiled=True)
    (packed,) = call(
        functools.partial(pack_kernel, z, grid),
        [pltpu.VMEM((z.packed * 3 // 2, 128), BF16)],
        (where, own, *sides),
        [own_v, flat_v],
    )

    def met(block, axis, n, step):
        return lax.ppermute(block, axis, [(i, offset(i, step, n)) for i in range(n)])

    power = rows_n & (rows_n - 1) == 0
    near = [packed] + [
        met(packed, "row", rows_n, x if power else rows_n - x) for x in range(1, rows_n)
    ]
    far = [met(block, "core", 2, 1) for block in near]
    stride = members * z.cols
    group_atoms = atom_count // members
    half_v = pltpu.VMEM((owned, z.patch // 2), BF16)
    partial_v = pltpu.VMEM((group_atoms, z.patch // 2), BF16)
    *first_half, across, wide_part = call(
        functools.partial(learn_kernel, z, grid, groups, yx_n),
        [half_v] * yx_n
        + [
            pltpu.VMEM((group_atoms, members * z.sites), BF16),
            pltpu.VMEM((z.tall * stride, z.band), BF16),
        ],
        (where, shared, *near, *far),
        [
            partial_v,
            pltpu.VMEM((cores_n, rows_n, z.packed, z.lanes), F32),
            own_v,
            pltpu.VMEM((members * z.sites, group_atoms), BF16),
        ],
    )
    other_half = call(
        functools.partial(rest_kernel, z, grid, stride),
        [half_v] * yx_n,
        (where, across, wide_part),
        [partial_v],
    )
    parts = [
        block if step == 0 else met(block, "yx", yx_n, step)
        for half in (first_half, other_half)
        for step, block in enumerate(half)
    ]
    new_dictionary, new_momentum = call(
        functools.partial(finish_kernel, z, yx_n),
        [jax.ShapeDtypeStruct(momentum.shape, F32)] * 2,
        (where, momentum, atoms, *parts),
        [
            pltpu.VMEM(momentum.shape, F32),
            pltpu.VMEM(momentum.shape, F32),
            pltpu.SemaphoreType.DMA((4,)),
        ],
        leave=HBM,
    )
    return (final_codes, new_dictionary, new_momentum)


def solution(mesh):
    rows_n, cols_n = (mesh.shape["row"], mesh.shape["col"])
    split = Mesh(mesh.devices.reshape(rows_n, cols_n // 2, 2), ("row", "yx", "core"))
    col = ("yx", "core")
    return jax.shard_map(
        shards,
        mesh=split,
        in_specs=(P(None, "row", col), P("row", col, None), P(), P(("row",) + col, None)),
        out_specs=(P("row", col, None), P(("row",) + col, None), P(("row",) + col, None)),
        check_vma=False,
    )
```

```python
import functools

import jax
import jax.numpy as jnp
from jax import lax
from jax.experimental import pallas as pl
from jax.experimental.pallas import tpu as pltpu
from jax.sharding import Mesh
from jax.sharding import PartitionSpec as P


PATCH_SIDE = 32
STRIDE = 8
SWEEPS = 2
SPAN = PATCH_SIDE // STRIDE
MARGIN = SPAN - 1

THRESHOLD = 0.25
RELAXATION = 0.1
DECAY = 0.9
LEARNING = 0.25
EPSILON = 1e-05


F32 = jnp.float32
BF16 = jnp.bfloat16
VMEM = pl.BlockSpec(memory_space=pltpu.VMEM)
SMEM = pl.BlockSpec(memory_space=pltpu.SMEM)
HBM = pl.BlockSpec(memory_space=pltpu.HBM)
PARAMS = pltpu.CompilerParams(vmem_limit_bytes=24 * 1024 * 1024)


def up_to(value, step):
    return -(-value // step) * step


def shrink(potential):
    return potential - jnp.clip(potential, -THRESHOLD, THRESHOLD)


class Sizes:
    def __init__(self, site_rows, site_cols, atoms, patch_len):
        self.rows, self.cols, self.atoms, self.patch = site_rows, site_cols, atoms, patch_len
        self.cell = patch_len // (SPAN * SPAN)
        self.band = SPAN * self.cell
        self.sites = site_rows * site_cols
        self.tall = site_rows + MARGIN
        self.wide = site_cols + MARGIN
        self.wide_pad = up_to(self.wide, 8)
        self.tall_pad = up_to(self.tall, 16)
        self.lanes = up_to(self.cell, 128)
        self.rim = up_to(MARGIN * self.wide, 16)
        self.packed = up_to(self.tall * self.cols + MARGIN * self.tall_pad, 32)
        self.scale = patch_len ** (-0.5)


class Place:
    def __init__(self, where, rows_n, cols_n):
        self.row, self.col = where[0], where[1]
        self.rows_n, self.cols_n = rows_n, cols_n
        self.owner = self.row * cols_n + self.col

    def pairs(self, axis):
        at, n = (self.row, self.rows_n) if axis == 0 else (self.col, self.cols_n)
        before, after = at > 0, at < n - 1
        odd = at % 2
        return [
            (odd == 0, ((True, after), (False, before))),
            (odd == 1, ((False, before), (True, after))),
        ]


def partners(n):
    even, odd = {}, {}
    for i in range(n):
        even[i] = i ^ 1 if i ^ 1 < n else i
        other = ((i + 1) ^ 1) - 1
        odd[i] = other if 0 <= other < n else (n - 1 if i == 0 and n % 2 == 0 else i)
    if n % 2 == 0:
        odd[n - 1] = 0
    return [sorted(even.items()), sorted(odd.items())]


def reconstruct(z, place, coding, dic, pixels, tall_sum, own, ready=None):
    tall_sum[z.sites :, :] = jnp.zeros((z.tall * z.cols - z.sites, z.band), F32)
    for i in range(SPAN):
        if ready is not None:
            ready(i)
        placed = jnp.dot(
            coding, dic[:, i * z.band : (i + 1) * z.band], preferred_element_type=F32
        )
        start = i * z.cols
        if i == 0:
            tall_sum[0 : z.sites, :] = placed
        else:
            tall_sum[start : start + z.sites, :] += placed
    own[...] = jnp.zeros((z.tall, z.wide_pad, z.lanes), F32)
    own[0 : z.rows, 0 : z.cols, 0 : z.cell] = pixels[...].reshape(z.rows, z.cols, z.cell)
    for j in range(SPAN):
        part = tall_sum[:, j * z.cell : (j + 1) * z.cell].reshape(z.tall, z.cols, z.cell)
        own[:, j : j + z.cols, 0 : z.cell] -= part * z.scale

    @pl.when(place.row == place.rows_n - 1)
    def _():
        own[z.rows :] = jnp.zeros((MARGIN, z.wide_pad, z.lanes), F32)

    @pl.when(place.col == place.cols_n - 1)
    def _():
        own[:, z.cols :] = jnp.zeros((z.tall, z.wide_pad - z.cols, z.lanes), F32)


def send_sides(z, place, own, sends):
    for mine, halves in place.pairs(1):

        @pl.when(mine)
        def _(halves=halves):
            for send, (onward, _) in zip(sends, halves):
                first = z.cols if onward else 0
                for c in range(MARGIN):
                    send[c, 0 : z.tall, :] = own[:, first + c, :].astype(BF16)


def add_sides(z, place, whole, received):
    for mine, halves in place.pairs(1):
        for rim, (onward, there) in zip(received, halves):

            @pl.when(mine & there)
            def _(rim=rim, first=z.cols if onward else 0):
                for c in range(MARGIN):
                    whole[:, first + c, :] += rim[c].astype(F32)[0 : z.tall]


def is_equal(a, b):
    return (a == b).astype(F32).astype(BF16)


def cells_of(z, picture, pixels, spread):
    channels, height, width = picture.shape
    turned = picture[...].reshape(channels * height, width).T
    high = turned.astype(BF16)
    rest = turned - high.astype(F32)
    middle = rest.astype(BF16)
    spread[0:width, :] = high
    spread[width : 2 * width, :] = middle
    spread[2 * width :, :] = (rest - middle.astype(F32)).astype(BF16)

    def iota(shape, dim):
        return lax.broadcasted_iota(jnp.int32, shape, dim)

    shape = (channels * height, z.cell)
    line, entry = iota(shape, 0), iota(shape, 1)
    channel, image_row = lax.div(line, height), lax.rem(line, height)
    away = (
        (channel * STRIDE + lax.rem(image_row, STRIDE)) * STRIDE
        + lax.div(image_row, STRIDE) * z.cell
        - lax.div(entry, STRIDE) * STRIDE
    )
    shape = (width, z.cell)
    mine = (lax.rem(iota(shape, 0), STRIDE) == lax.rem(iota(shape, 1), STRIDE)).astype(F32)
    for i in range(z.rows):
        moved = jnp.dot(
            spread[...], is_equal(away, i * z.cell), preferred_element_type=F32
        )
        whole = (moved[0:width] + moved[width : 2 * width]) + moved[2 * width :]
        whole = (whole * mine).reshape(z.cols, STRIDE, z.cell)
        pixels[i * z.cols : (i + 1) * z.cols, :] = jnp.sum(whole, axis=1)


def first_kernel(
    z, grid, where, membrane, picture, source, own, *rest
):
    (*sends, pixels, dic, potential, atoms, tall_sum, spread, drawing, sems) = rest
    place = Place(where, *grid)
    early = [
        pltpu.make_async_copy(picture, drawing, sems.at[SPAN]),
        pltpu.make_async_copy(membrane, potential, sems.at[SPAN + 1]),
    ]
    copies = [
        pltpu.make_async_copy(
            source.at[:, i * z.band : (i + 1) * z.band],
            dic.at[:, i * z.band : (i + 1) * z.band],
            sems.at[i],
        )
        for i in range(SPAN)
    ]
    for copy in early + copies:
        copy.start()
    early[0].wait()
    cells_of(z, drawing, pixels, spread)
    early[1].wait()
    coding = shrink(potential[...]).astype(BF16)
    reconstruct(z, place, coding, dic, pixels, tall_sum, own, lambda i: copies[i].wait())
    send_sides(z, place, own, sends)
    owned = atoms.shape[0]
    atoms[...] = dic[pl.ds(pl.multiple_of(place.owner * owned, owned), owned), :]


def side_kernel(z, grid, where, own, from_even, from_odd, joined, even, odd, rim):
    place = Place(where, *grid)
    joined[...] = own[...]
    add_sides(z, place, joined, (from_even, from_odd))
    rim[MARGIN * z.wide :, :] = jnp.zeros((z.rim - MARGIN * z.wide, z.lanes), F32)
    for mine, halves in place.pairs(0):

        @pl.when(mine)
        def _(halves=halves):
            for send, (onward, _) in zip((even, odd), halves):
                first = z.rows if onward else 0
                for r in range(MARGIN):
                    start = MARGIN * z.cols + r * MARGIN
                    rim[r * z.cols : (r + 1) * z.cols, :] = joined[first + r, 0 : z.cols, :]
                    rim[start : start + MARGIN, :] = joined[first + r, z.cols : z.wide, :]
                send[...] = rim[...].astype(BF16)


def add_ends(z, place, whole, received, rim):
    for mine, halves in place.pairs(0):
        for block, (onward, there) in zip(received, halves):

            @pl.when(mine & there)
            def _(block=block, first=z.rows if onward else 0):
                rim[...] = block[...].astype(F32)
                for r in range(MARGIN):
                    start = MARGIN * z.cols + r * MARGIN
                    whole[first + r, 0 : z.cols, :] += rim[r * z.cols : (r + 1) * z.cols, :]
                    whole[first + r, z.cols : z.wide, :] += rim[start : start + MARGIN, :]


def windows_of(z, whole, wide_part, first_row, row_stride):
    for j in range(SPAN):
        part = whole[:, j : j + z.cols, 0 : z.cell].astype(BF16)
        for p in range(z.tall):
            wide_part[
                pl.ds(p * row_stride + first_row, z.cols), j * z.cell : (j + 1) * z.cell
            ] = part[p]


def sweep_kernel(
    z, grid, last, where, potential, joined, from_even, from_odd, pixels, dic, *rest
):
    if last:
        new_potential, own, *sends, codes, tall_sum, whole, wide_part, rim = rest
    else:
        new_potential, own, *sends, tall_sum, whole, wide_part, rim = rest
    place = Place(where, *grid)
    whole[...] = joined[...]
    add_ends(z, place, whole, (from_even, from_odd), rim)
    windows_of(z, whole, wide_part, 0, z.cols)
    drive = None
    for i in range(SPAN):
        term = lax.dot_general(
            wide_part[i * z.cols : i * z.cols + z.sites, :],
            dic[:, i * z.band : (i + 1) * z.band],
            (((1,), (1,)), ((), ())),
            preferred_element_type=F32,
        )
        drive = term if drive is None else drive + term
    old = potential[...]
    updated = old + RELAXATION * (drive * z.scale + shrink(old) - old)
    active = shrink(updated)
    coding = active.astype(BF16)
    if last:
        new_potential[...] = active
        codes[...] = coding
    else:
        new_potential[...] = updated
    reconstruct(z, place, coding, dic, pixels, tall_sum, own)
    send_sides(z, place, own, sends)


def sort_kernel(z, grid, groups, where, codes, _, mine, other):
    rows_n, cores_n, owned = groups
    span = z.atoms // rows_n
    src = lax.broadcasted_iota(jnp.int32, (span, span), 0)
    dst = lax.broadcasted_iota(jnp.int32, (span, span), 1)
    per_core = span // cores_n
    core, rem = lax.div(dst, per_core), lax.rem(dst, per_core)
    wanted = lax.div(rem, owned) * (owned * cores_n) + core * owned + lax.rem(rem, owned)
    order = is_equal(src, wanted)
    place = Place(where, *grid)
    for r in range(rows_n):
        line = jnp.dot(codes[:, r * span : (r + 1) * span], order, preferred_element_type=F32)
        halves = [line[:, k * per_core : (k + 1) * per_core].astype(BF16) for k in range(cores_n)]
        step = place.row ^ r if rows_n & (rows_n - 1) == 0 else (place.row - r) % rows_n
        for k in range(cores_n):

            @pl.when(place.col % 2 == k)
            def _(k=k, halves=halves, step=step):
                mine[step] = halves[k]
                other[step] = halves[1 - k]


def join_kernel(where, mine, other, *joint):
    for step, out in enumerate(joint):
        out[0] = mine[step + 1]
        out[1] = other[step + 1]


def pack_kernel(z, grid, where, own, from_even, from_odd, packed, joined, flat):
    joined[...] = own[...]
    add_sides(z, Place(where, *grid), joined, (from_even, from_odd))
    base = z.tall * z.cols
    flat[base:, :] = jnp.zeros((z.packed - base, z.lanes), F32)
    for p in range(z.tall):
        flat[p * z.cols : (p + 1) * z.cols, :] = joined[p, 0 : z.cols, :]
    for c in range(MARGIN):
        start = base + c * z.tall_pad
        flat[start : start + z.tall, :] = joined[:, z.cols + c, :]
    half = z.packed // 2
    packed[0 : z.packed, :] = flat[:, 0:128].astype(BF16)
    tail = z.cell - 128
    ends = jnp.concatenate([flat[0:half, 128 : z.cell], flat[half:, 128 : z.cell]], axis=1)
    packed[z.packed :, 0 : 2 * tail] = ends.astype(BF16)


def offset(at, step, n):
    return at ^ step if n & (n - 1) == 0 else (at + step) % n


def learn_half(z, grid, where, across, wide_part, stride, bands, outs, partial):
    count = z.rows * stride
    for n, i in enumerate(bands):
        term = jnp.dot(
            across, wide_part[i * stride : i * stride + count, :], preferred_element_type=F32
        )
        partial[:, n * z.band : (n + 1) * z.band] = (term * z.scale).astype(BF16)
    owned = outs[0].shape[0]
    place = Place(where, *grid)
    for step, out in enumerate(outs):
        at = offset(place.col // 2, step, len(outs))
        out[...] = partial[pl.ds(pl.multiple_of(at * owned, owned), owned), :]


def learn_kernel(z, grid, groups, yx_n, where, first_near, first_far, *rest):
    rows_n, cores_n, _ = groups
    members = rows_n * cores_n
    met, rest = rest[: rows_n - 1], rest[rows_n - 1 :]
    near, far, outs = rest[:rows_n], rest[rows_n : 2 * rows_n], rest[2 * rows_n :]
    outs, (across, wide_part, partial, flat, whole, codes) = outs[:yx_n], outs[yx_n:]
    stride = members * z.cols
    base = z.tall * z.cols
    half = z.packed // 2
    tail = z.cell - 128
    place = Place(where, *grid)
    mine = place.col % 2

    for x in range(rows_n):
        d = offset(place.row, x, rows_n)
        for k, block in ((mine, near[x]), (1 - mine, far[x])):
            flat[k, d, :, 0:128] = block[0 : z.packed, :].astype(F32)
            ends = block[z.packed :, :].astype(F32)
            flat[k, d, 0:half, 128 : z.cell] = ends[:, 0:tail]
            flat[k, d, half:, 128 : z.cell] = ends[:, tail : 2 * tail]
            own_core = block is near[x]
            for i in range(z.rows):
                sites = slice(i * z.cols, (i + 1) * z.cols)
                if x == 0:
                    lines = (first_near if own_core else first_far)[0, sites, :]
                else:
                    lines = met[x - 1][0 if own_core else 1, sites, :]
                at = i * stride + (d * cores_n + k) * z.cols
                codes[pl.ds(pl.multiple_of(at, z.cols), z.cols), :] = lines
    for k in range(cores_n):
        for r in range(rows_n):
            d = r * cores_n + k
            for source, low, high, at in (
                (r, 0, z.tall, 0),
                (r - 1, z.rows, z.tall, 0),
                (r + 1, 0, MARGIN, z.rows),
            ):
                if not 0 <= source < rows_n:
                    continue
                n = high - low
                main = flat[k, source, low * z.cols : high * z.cols, :]
                main = main.reshape(n, z.cols, z.lanes)
                side = [
                    flat[k, source, base + c * z.tall_pad + low : base + c * z.tall_pad + high, :]
                    for c in range(MARGIN)
                ]
                if source == r:
                    whole[at : at + n, 0 : z.cols, :] = main
                    for c in range(MARGIN):
                        whole[at : at + n, z.cols + c, :] = side[c]
                else:
                    whole[at : at + n, 0 : z.cols, :] += main
                    for c in range(MARGIN):
                        whole[at : at + n, z.cols + c, :] += side[c]
            windows_of(z, whole, wide_part, d * z.cols, stride)
    across[...] = codes[...].astype(F32).T.astype(BF16)
    learn_half(
        z, grid, where, across[...], wide_part, stride, range(SPAN // 2), outs, partial
    )


def rest_kernel(z, grid, stride, where, across, wide_part, *rest):
    *outs, partial = rest
    learn_half(
        z, grid, where, across[...], wide_part, stride, range(SPAN // 2, SPAN), outs, partial
    )


def finish_kernel(z, yx_n, where, momentum, atoms, *rest):
    *parts, new_dictionary, new_momentum, weights, updated, sems = rest
    width = z.patch // 2
    power = 0.0
    copies = []
    for h in range(2):
        lanes = pl.ds(h * width, width)
        learning = parts[h * yx_n][...].astype(F32)
        for part in parts[h * yx_n + 1 : (h + 1) * yx_n]:
            learning = learning + part[...].astype(F32)
        momentum_out = DECAY * momentum[:, lanes] + learning
        updated[:, lanes] = momentum_out
        copies.append(
            pltpu.make_async_copy(updated.at[:, lanes], new_momentum.at[:, lanes], sems.at[h])
        )
        copies[-1].start()
        weight = atoms[:, lanes].astype(F32) + LEARNING * momentum_out
        weights[:, lanes] = weight
        power = power + jnp.sum(weight * weight, axis=1, keepdims=True)
    norm = lax.rsqrt(power * (1.0 / z.patch) + EPSILON)
    for h in range(2):
        lanes = pl.ds(h * width, width)
        weights[:, lanes] = weights[:, lanes] * norm
        copies.append(
            pltpu.make_async_copy(
                weights.at[:, lanes], new_dictionary.at[:, lanes], sems.at[2 + h]
            )
        )
        copies[-1].start()
    for copy in copies:
        copy.wait()


def kept(x, space=pltpu.VMEM):
    return pltpu.with_memory_space_constraint(x, space)


def call(kernel, outs, inputs, scratch, far=0, leave=VMEM):
    specs = [SMEM] + [HBM] * far + [VMEM] * (len(inputs) - 1 - far)
    where, *others = inputs
    placed = [kept(x, pltpu.HBM) for x in others[:far]] + [kept(x) for x in others[far:]]
    return pl.pallas_call(
        kernel,
        out_shape=outs,
        in_specs=specs,
        out_specs=[leave] * len(outs),
        scratch_shapes=scratch,
        compiler_params=PARAMS,
    )(where, *placed)


def shards(picture, membrane, dictionary, momentum):
    site_rows, site_cols, atom_count = membrane.shape
    z = Sizes(site_rows, site_cols, atom_count, dictionary.shape[1])
    rows_n, yx_n, cores_n = (lax.axis_size(a) for a in ("row", "yx", "core"))
    cols_n = yx_n * cores_n
    owned = momentum.shape[0]
    groups = (rows_n, cores_n, owned)
    members = rows_n * cores_n
    grid = (rows_n, cols_n)
    where = jnp.stack([lax.axis_index("row"), lax.axis_index(("yx", "core"))]).astype(jnp.int32)

    def met(block, axis, n, step):
        return lax.ppermute(block, axis, [(i, offset(i, step, n)) for i in range(n)])

    def swapped(axis, n, blocks):
        return [lax.ppermute(b, axis, route) for b, route in zip(blocks, partners(n))]

    def sideways(blocks):
        even, odd = partners(cols_n)
        near_rim = lax.ppermute(blocks[0], ("yx", "core"), even)
        far_rim = lax.ppermute(blocks[1], ("yx", "core"), odd)
        return [near_rim, far_rim]

    own_v = pltpu.VMEM((z.tall, z.wide_pad, z.lanes), F32)
    side_v = pltpu.VMEM((MARGIN, z.tall_pad, z.lanes), BF16)
    end_v = pltpu.VMEM((z.rim, z.lanes), BF16)
    rim_v = pltpu.VMEM((z.rim, z.lanes), F32)
    tall_v = pltpu.VMEM((z.tall * z.cols, z.band), F32)
    wide_v = pltpu.VMEM((z.tall * z.cols, z.band), BF16)
    flat_v = pltpu.VMEM((z.packed, z.lanes), F32)
    site_v = pltpu.VMEM((z.sites, atom_count), F32)
    outs = [own_v, side_v, side_v]

    own, *sides, pixels, dic, potential, atoms = call(
        functools.partial(first_kernel, z, grid),
        outs
        + [
            pltpu.VMEM((z.sites, z.cell), F32),
            pltpu.VMEM(dictionary.shape, BF16),
            site_v,
            pltpu.VMEM(momentum.shape, BF16),
        ],
        (where, membrane.reshape(z.sites, atom_count), picture, dictionary),
        [
            tall_v,
            pltpu.VMEM((3 * picture.shape[2], z.cell), BF16),
            pltpu.VMEM(picture.shape, F32),
            pltpu.SemaphoreType.DMA((SPAN + 2,)),
        ],
        far=3,
    )
    for repeat in range(SWEEPS):
        last = repeat == SWEEPS - 1
        joined, *ends = call(
            functools.partial(side_kernel, z, grid),
            [own_v, end_v, end_v],
            (where, own, *sideways(sides)),
            [rim_v],
        )
        ends = swapped("row", rows_n, ends)
        final = [
            site_v,
            *outs,
            pltpu.VMEM((z.sites, atom_count), BF16),
        ]
        potential, own, *rest = call(
            functools.partial(sweep_kernel, z, grid, last),
            final if last else [site_v] + outs,
            (where, potential, joined, *ends, pixels, dic),
            [tall_v, own_v, wide_v, rim_v],
        )
        sides = rest[:2]
    final_codes = potential.reshape(membrane.shape)
    sides = sideways(sides)
    codes_v = pltpu.VMEM((rows_n, z.sites, atom_count // members), BF16)
    mine, other = call(
        functools.partial(sort_kernel, z, grid, groups),
        [codes_v, codes_v],
        (where, rest[2], sides[0]),
        [],
    )
    other = met(other, "core", 2, 1)
    joint = call(
        join_kernel,
        [pltpu.VMEM((2,) + codes_v.shape[1:], BF16)] * (rows_n - 1),
        (where, mine, other),
        [],
    )
    power = rows_n & (rows_n - 1) == 0
    joint = [
        met(block, "row", rows_n, x if power else rows_n - x)
        for x, block in enumerate(joint, 1)
    ]
    (packed,) = call(
        functools.partial(pack_kernel, z, grid),
        [pltpu.VMEM((z.packed * 3 // 2, 128), BF16)],
        (where, own, *sides),
        [own_v, flat_v],
    )

    near = [packed] + [
        met(packed, "row", rows_n, x if power else rows_n - x)
        for x in range(1, rows_n)
    ]
    far = [met(block, "core", 2, 1) for block in near]
    stride = members * z.cols
    group_atoms = atom_count // members
    half_v = pltpu.VMEM((owned, z.patch // 2), BF16)
    partial_v = pltpu.VMEM((group_atoms, z.patch // 2), BF16)
    *first_half, across, wide_part = call(
        functools.partial(learn_kernel, z, grid, groups, yx_n),
        [half_v] * yx_n
        + [
            pltpu.VMEM((group_atoms, members * z.sites), BF16),
            pltpu.VMEM((z.tall * stride, z.band), BF16),
        ],
        (where, mine, other, *joint, *near, *far),
        [
            partial_v,
            pltpu.VMEM((cores_n, rows_n, z.packed, z.lanes), F32),
            own_v,
            pltpu.VMEM((members * z.sites, group_atoms), BF16),
        ],
    )
    other_half = call(
        functools.partial(rest_kernel, z, grid, stride),
        [half_v] * yx_n,
        (where, across, wide_part),
        [partial_v],
    )
    parts = [
        block if step == 0 else met(block, "yx", yx_n, step)
        for half in (first_half, other_half)
        for step, block in enumerate(half)
    ]
    new_dictionary, new_momentum = call(
        functools.partial(finish_kernel, z, yx_n),
        [jax.ShapeDtypeStruct(momentum.shape, F32)] * 2,
        (where, momentum, atoms, *parts),
        [
            pltpu.VMEM(momentum.shape, F32),
            pltpu.VMEM(momentum.shape, F32),
            pltpu.SemaphoreType.DMA((4,)),
        ],
        leave=HBM,
    )
    return (final_codes, new_dictionary, new_momentum)


def solution(mesh):
    rows_n, cols_n = (mesh.shape["row"], mesh.shape["col"])
    split = Mesh(mesh.devices.reshape(rows_n, cols_n // 2, 2), ("row", "yx", "core"))
    col = ("yx", "core")
    return jax.shard_map(
        shards,
        mesh=split,
        in_specs=(P(None, "row", col), P("row", col, None), P(), P(("row",) + col, None)),
        out_specs=(P("row", col, None), P(("row",) + col, None), P(("row",) + col, None)),
        check_vma=False,
    )
```

```python
import functools

import jax
import jax.numpy as jnp
from jax import lax
from jax.experimental import pallas as pl
from jax.experimental.pallas import tpu as pltpu
from jax.sharding import Mesh
from jax.sharding import PartitionSpec as P


PATCH_SIDE = 32
STRIDE = 8
SWEEPS = 2
SPAN = PATCH_SIDE // STRIDE
MARGIN = SPAN - 1

THRESHOLD = 0.25
RELAXATION = 0.1
DECAY = 0.9
LEARNING = 0.25
EPSILON = 1e-05


F32 = jnp.float32
BF16 = jnp.bfloat16
VMEM = pl.BlockSpec(memory_space=pltpu.VMEM)
SMEM = pl.BlockSpec(memory_space=pltpu.SMEM)
HBM = pl.BlockSpec(memory_space=pltpu.HBM)
PARAMS = pltpu.CompilerParams(vmem_limit_bytes=24 * 1024 * 1024)


def up_to(value, step):
    return -(-value // step) * step


def shrink(potential):
    return potential - jnp.clip(potential, -THRESHOLD, THRESHOLD)


class Sizes:
    def __init__(self, site_rows, site_cols, atoms, patch_len):
        self.rows, self.cols, self.atoms, self.patch = site_rows, site_cols, atoms, patch_len
        self.cell = patch_len // (SPAN * SPAN)
        self.band = SPAN * self.cell
        self.sites = site_rows * site_cols
        self.tall = site_rows + MARGIN
        self.wide = site_cols + MARGIN
        self.wide_pad = up_to(self.wide, 8)
        self.tall_pad = up_to(self.tall, 16)
        self.lanes = up_to(self.cell, 128)
        self.rim = up_to(MARGIN * self.wide, 16)
        self.packed = up_to(self.tall * self.cols + MARGIN * self.tall_pad, 32)
        self.scale = patch_len ** (-0.5)


class Place:
    def __init__(self, where, rows_n, cols_n):
        self.row, self.col = where[0], where[1]
        self.rows_n, self.cols_n = rows_n, cols_n
        self.owner = self.row * cols_n + self.col

    def pairs(self, axis):
        at, n = (self.row, self.rows_n) if axis == 0 else (self.col, self.cols_n)
        before, after = at > 0, at < n - 1
        odd = at % 2
        return [
            (odd == 0, ((True, after), (False, before))),
            (odd == 1, ((False, before), (True, after))),
        ]


def partners(n):
    even, odd = {}, {}
    for i in range(n):
        even[i] = i ^ 1 if i ^ 1 < n else i
        other = ((i + 1) ^ 1) - 1
        odd[i] = other if 0 <= other < n else (n - 1 if i == 0 and n % 2 == 0 else i)
    if n % 2 == 0:
        odd[n - 1] = 0
    return [sorted(even.items()), sorted(odd.items())]


def reconstruct(z, place, coding, dic, pixels, tall_sum, own, ready=None):
    tall_sum[z.sites :, :] = jnp.zeros((z.tall * z.cols - z.sites, z.band), F32)
    for i in range(SPAN):
        if ready is not None:
            ready(i)
        placed = jnp.dot(
            coding, dic[:, i * z.band : (i + 1) * z.band], preferred_element_type=F32
        )
        start = i * z.cols
        if i == 0:
            tall_sum[0 : z.sites, :] = placed
        else:
            tall_sum[start : start + z.sites, :] += placed
    own[...] = jnp.zeros((z.tall, z.wide_pad, z.lanes), F32)
    own[0 : z.rows, 0 : z.cols, 0 : z.cell] = pixels[...].reshape(z.rows, z.cols, z.cell)
    for j in range(SPAN):
        part = tall_sum[:, j * z.cell : (j + 1) * z.cell].reshape(z.tall, z.cols, z.cell)
        own[:, j : j + z.cols, 0 : z.cell] -= part * z.scale

    @pl.when(place.row == place.rows_n - 1)
    def _():
        own[z.rows :] = jnp.zeros((MARGIN, z.wide_pad, z.lanes), F32)

    @pl.when(place.col == place.cols_n - 1)
    def _():
        own[:, z.cols :] = jnp.zeros((z.tall, z.wide_pad - z.cols, z.lanes), F32)


def send_sides(z, place, own, sends):
    for mine, halves in place.pairs(1):

        @pl.when(mine)
        def _(halves=halves):
            for send, (onward, _) in zip(sends, halves):
                first = z.cols if onward else 0
                for c in range(MARGIN):
                    send[c, 0 : z.tall, :] = own[:, first + c, :].astype(BF16)


def add_sides(z, place, whole, received):
    for mine, halves in place.pairs(1):
        for rim, (onward, there) in zip(received, halves):

            @pl.when(mine & there)
            def _(rim=rim, first=z.cols if onward else 0):
                for c in range(MARGIN):
                    whole[:, first + c, :] += rim[c].astype(F32)[0 : z.tall]


def is_equal(a, b):
    return (a == b).astype(F32).astype(BF16)


def cells_of(z, picture, pixels, spread):
    channels, height, width = picture.shape
    turned = picture[...].reshape(channels * height, width).T
    high = turned.astype(BF16)
    rest = turned - high.astype(F32)
    middle = rest.astype(BF16)
    spread[0:width, :] = high
    spread[width : 2 * width, :] = middle
    spread[2 * width :, :] = (rest - middle.astype(F32)).astype(BF16)

    def iota(shape, dim):
        return lax.broadcasted_iota(jnp.int32, shape, dim)

    shape = (channels * height, z.cell)
    line, entry = iota(shape, 0), iota(shape, 1)
    channel, image_row = lax.div(line, height), lax.rem(line, height)
    away = (
        (channel * STRIDE + lax.rem(image_row, STRIDE)) * STRIDE
        + lax.div(image_row, STRIDE) * z.cell
        - lax.div(entry, STRIDE) * STRIDE
    )
    shape = (width, z.cell)
    mine = (lax.rem(iota(shape, 0), STRIDE) == lax.rem(iota(shape, 1), STRIDE)).astype(F32)
    for i in range(z.rows):
        moved = jnp.dot(
            spread[...], is_equal(away, i * z.cell), preferred_element_type=F32
        )
        whole = (moved[0:width] + moved[width : 2 * width]) + moved[2 * width :]
        whole = (whole * mine).reshape(z.cols, STRIDE, z.cell)
        pixels[i * z.cols : (i + 1) * z.cols, :] = jnp.sum(whole, axis=1)


def first_kernel(
    z, grid, where, membrane, picture, source, own, *rest
):
    (*sends, pixels, dic, potential, atoms, tall_sum, spread, drawing, sems) = rest
    place = Place(where, *grid)
    early = [
        pltpu.make_async_copy(picture, drawing, sems.at[SPAN]),
        pltpu.make_async_copy(membrane, potential, sems.at[SPAN + 1]),
    ]
    copies = [
        pltpu.make_async_copy(
            source.at[:, i * z.band : (i + 1) * z.band],
            dic.at[:, i * z.band : (i + 1) * z.band],
            sems.at[i],
        )
        for i in range(SPAN)
    ]
    for copy in early + copies:
        copy.start()
    early[0].wait()
    cells_of(z, drawing, pixels, spread)
    early[1].wait()
    coding = shrink(potential[...]).astype(BF16)
    reconstruct(z, place, coding, dic, pixels, tall_sum, own, lambda i: copies[i].wait())
    send_sides(z, place, own, sends)
    owned = atoms.shape[0]
    atoms[...] = dic[pl.ds(pl.multiple_of(place.owner * owned, owned), owned), :]


def side_kernel(z, grid, where, own, from_even, from_odd, joined, even, odd, rim):
    place = Place(where, *grid)
    joined[...] = own[...]
    add_sides(z, place, joined, (from_even, from_odd))
    rim[MARGIN * z.wide :, :] = jnp.zeros((z.rim - MARGIN * z.wide, z.lanes), F32)
    for mine, halves in place.pairs(0):

        @pl.when(mine)
        def _(halves=halves):
            for send, (onward, _) in zip((even, odd), halves):
                first = z.rows if onward else 0
                for r in range(MARGIN):
                    start = MARGIN * z.cols + r * MARGIN
                    rim[r * z.cols : (r + 1) * z.cols, :] = joined[first + r, 0 : z.cols, :]
                    rim[start : start + MARGIN, :] = joined[first + r, z.cols : z.wide, :]
                send[...] = rim[...].astype(BF16)


def add_ends(z, place, whole, received, rim):
    for mine, halves in place.pairs(0):
        for block, (onward, there) in zip(received, halves):

            @pl.when(mine & there)
            def _(block=block, first=z.rows if onward else 0):
                rim[...] = block[...].astype(F32)
                for r in range(MARGIN):
                    start = MARGIN * z.cols + r * MARGIN
                    whole[first + r, 0 : z.cols, :] += rim[r * z.cols : (r + 1) * z.cols, :]
                    whole[first + r, z.cols : z.wide, :] += rim[start : start + MARGIN, :]


def windows_of(z, whole, wide_part, first_row, row_stride):
    for j in range(SPAN):
        part = whole[:, j : j + z.cols, 0 : z.cell].astype(BF16)
        for p in range(z.tall):
            wide_part[
                pl.ds(p * row_stride + first_row, z.cols), j * z.cell : (j + 1) * z.cell
            ] = part[p]


def sweep_kernel(
    z, grid, last, where, potential, joined, from_even, from_odd, pixels, dic, *rest
):
    if last:
        new_potential, own, *sends, codes, tall_sum, whole, wide_part, rim = rest
    else:
        new_potential, own, *sends, tall_sum, whole, wide_part, rim = rest
    place = Place(where, *grid)
    whole[...] = joined[...]
    add_ends(z, place, whole, (from_even, from_odd), rim)
    windows_of(z, whole, wide_part, 0, z.cols)
    drive = None
    for i in range(SPAN):
        term = lax.dot_general(
            wide_part[i * z.cols : i * z.cols + z.sites, :],
            dic[:, i * z.band : (i + 1) * z.band],
            (((1,), (1,)), ((), ())),
            preferred_element_type=F32,
        )
        drive = term if drive is None else drive + term
    old = potential[...]
    updated = old + RELAXATION * (drive * z.scale + shrink(old) - old)
    active = shrink(updated)
    coding = active.astype(BF16)
    if last:
        new_potential[...] = active
        codes[...] = coding
    else:
        new_potential[...] = updated
    reconstruct(z, place, coding, dic, pixels, tall_sum, own)
    send_sides(z, place, own, sends)


def sort_kernel(z, grid, groups, where, codes, _, *messages):
    rows_n, cores_n, owned = groups
    span = z.atoms // rows_n
    src = lax.broadcasted_iota(jnp.int32, (span, span), 0)
    dst = lax.broadcasted_iota(jnp.int32, (span, span), 1)
    per_core = span // cores_n
    core, rem = lax.div(dst, per_core), lax.rem(dst, per_core)
    wanted = lax.div(rem, owned) * (owned * cores_n) + core * owned + lax.rem(rem, owned)
    order = is_equal(src, wanted)
    place = Place(where, *grid)
    for x, message in enumerate(messages):
        r = place.row ^ x if rows_n & (rows_n - 1) == 0 else (place.row - x) % rows_n
        block = codes[:, pl.ds(pl.multiple_of(r * span, span), span)]
        line = jnp.dot(block, order, preferred_element_type=F32).astype(BF16)
        for k in range(cores_n):
            message[k] = line[:, k * per_core : (k + 1) * per_core]


def turn_kernel(z, grid, groups, where, *rest):
    rows_n, cores_n, _ = groups
    stride = rows_n * cores_n * z.cols
    near, far, (across, codes) = rest[:rows_n], rest[rows_n : 2 * rows_n], rest[2 * rows_n :]
    place = Place(where, *grid)
    mine = place.col % 2
    for x in range(rows_n):
        d = offset(place.row, x, rows_n)
        for k, message in ((mine, near[x]), (1 - mine, far[x])):
            lines = message[mine]
            for i in range(z.rows):
                at = i * stride + (d * cores_n + k) * z.cols
                codes[pl.ds(pl.multiple_of(at, z.cols), z.cols), :] = lines[
                    i * z.cols : (i + 1) * z.cols, :
                ]
    across[...] = codes[...].astype(F32).T.astype(BF16)


def pack_kernel(z, grid, where, own, from_even, from_odd, packed, joined, flat):
    joined[...] = own[...]
    add_sides(z, Place(where, *grid), joined, (from_even, from_odd))
    base = z.tall * z.cols
    flat[base:, :] = jnp.zeros((z.packed - base, z.lanes), F32)
    for p in range(z.tall):
        flat[p * z.cols : (p + 1) * z.cols, :] = joined[p, 0 : z.cols, :]
    for c in range(MARGIN):
        start = base + c * z.tall_pad
        flat[start : start + z.tall, :] = joined[:, z.cols + c, :]
    half = z.packed // 2
    packed[0 : z.packed, :] = flat[:, 0:128].astype(BF16)
    tail = z.cell - 128
    ends = jnp.concatenate([flat[0:half, 128 : z.cell], flat[half:, 128 : z.cell]], axis=1)
    packed[z.packed :, 0 : 2 * tail] = ends.astype(BF16)


def offset(at, step, n):
    return at ^ step if n & (n - 1) == 0 else (at + step) % n


def learn_half(z, grid, where, across, wide_part, stride, bands, outs, partial):
    count = z.rows * stride
    for n, i in enumerate(bands):
        term = jnp.dot(
            across, wide_part[i * stride : i * stride + count, :], preferred_element_type=F32
        )
        partial[:, n * z.band : (n + 1) * z.band] = (term * z.scale).astype(BF16)
    owned = outs[0].shape[0]
    place = Place(where, *grid)
    for step, out in enumerate(outs):
        at = offset(place.col // 2, step, len(outs))
        out[...] = partial[pl.ds(pl.multiple_of(at * owned, owned), owned), :]


def learn_kernel(z, grid, groups, yx_n, where, across, *rest):
    rows_n, cores_n, _ = groups
    members = rows_n * cores_n
    near, far, outs = rest[:rows_n], rest[rows_n : 2 * rows_n], rest[2 * rows_n :]
    outs, (wide_part, partial, flat, whole) = outs[:yx_n], outs[yx_n:]
    stride = members * z.cols
    base = z.tall * z.cols
    half = z.packed // 2
    tail = z.cell - 128
    place = Place(where, *grid)
    mine = place.col % 2

    for x in range(rows_n):
        d = offset(place.row, x, rows_n)
        for k, block in ((mine, near[x]), (1 - mine, far[x])):
            flat[k, d, :, 0:128] = block[0 : z.packed, :].astype(F32)
            ends = block[z.packed :, :].astype(F32)
            flat[k, d, 0:half, 128 : z.cell] = ends[:, 0:tail]
            flat[k, d, half:, 128 : z.cell] = ends[:, tail : 2 * tail]
    for k in range(cores_n):
        for r in range(rows_n):
            d = r * cores_n + k
            for source, low, high, at in (
                (r, 0, z.tall, 0),
                (r - 1, z.rows, z.tall, 0),
                (r + 1, 0, MARGIN, z.rows),
            ):
                if not 0 <= source < rows_n:
                    continue
                n = high - low
                main = flat[k, source, low * z.cols : high * z.cols, :]
                main = main.reshape(n, z.cols, z.lanes)
                side = [
                    flat[k, source, base + c * z.tall_pad + low : base + c * z.tall_pad + high, :]
                    for c in range(MARGIN)
                ]
                if source == r:
                    whole[at : at + n, 0 : z.cols, :] = main
                    for c in range(MARGIN):
                        whole[at : at + n, z.cols + c, :] = side[c]
                else:
                    whole[at : at + n, 0 : z.cols, :] += main
                    for c in range(MARGIN):
                        whole[at : at + n, z.cols + c, :] += side[c]
            windows_of(z, whole, wide_part, d * z.cols, stride)
    learn_half(
        z, grid, where, across[...], wide_part, stride, range(SPAN // 2), outs, partial
    )


def rest_kernel(z, grid, stride, where, across, wide_part, *rest):
    *outs, partial = rest
    learn_half(
        z, grid, where, across[...], wide_part, stride, range(SPAN // 2, SPAN), outs, partial
    )


def finish_kernel(z, yx_n, where, momentum, atoms, *rest):
    *parts, new_dictionary, new_momentum, weights, updated, sems = rest
    width = z.patch // 2
    power = 0.0
    copies = []
    for h in range(2):
        lanes = pl.ds(h * width, width)
        learning = parts[h * yx_n][...].astype(F32)
        for part in parts[h * yx_n + 1 : (h + 1) * yx_n]:
            learning = learning + part[...].astype(F32)
        momentum_out = DECAY * momentum[:, lanes] + learning
        updated[:, lanes] = momentum_out
        copies.append(
            pltpu.make_async_copy(updated.at[:, lanes], new_momentum.at[:, lanes], sems.at[h])
        )
        copies[-1].start()
        weight = atoms[:, lanes].astype(F32) + LEARNING * momentum_out
        weights[:, lanes] = weight
        power = power + jnp.sum(weight * weight, axis=1, keepdims=True)
    norm = lax.rsqrt(power * (1.0 / z.patch) + EPSILON)
    for h in range(2):
        lanes = pl.ds(h * width, width)
        weights[:, lanes] = weights[:, lanes] * norm
        copies.append(
            pltpu.make_async_copy(
                weights.at[:, lanes], new_dictionary.at[:, lanes], sems.at[2 + h]
            )
        )
        copies[-1].start()
    for copy in copies:
        copy.wait()


def kept(x, space=pltpu.VMEM):
    return pltpu.with_memory_space_constraint(x, space)


def call(kernel, outs, inputs, scratch, far=0, leave=VMEM):
    specs = [SMEM] + [HBM] * far + [VMEM] * (len(inputs) - 1 - far)
    where, *others = inputs
    placed = [kept(x, pltpu.HBM) for x in others[:far]] + [kept(x) for x in others[far:]]
    return pl.pallas_call(
        kernel,
        out_shape=outs,
        in_specs=specs,
        out_specs=[leave] * len(outs),
        scratch_shapes=scratch,
        compiler_params=PARAMS,
    )(where, *placed)


def shards(picture, membrane, dictionary, momentum):
    site_rows, site_cols, atom_count = membrane.shape
    z = Sizes(site_rows, site_cols, atom_count, dictionary.shape[1])
    rows_n, yx_n, cores_n = (lax.axis_size(a) for a in ("row", "yx", "core"))
    cols_n = yx_n * cores_n
    owned = momentum.shape[0]
    groups = (rows_n, cores_n, owned)
    members = rows_n * cores_n
    grid = (rows_n, cols_n)
    where = jnp.stack([lax.axis_index("row"), lax.axis_index(("yx", "core"))]).astype(jnp.int32)

    def met(block, axis, n, step):
        return lax.ppermute(block, axis, [(i, offset(i, step, n)) for i in range(n)])

    def swapped(axis, n, blocks):
        return [lax.ppermute(b, axis, route) for b, route in zip(blocks, partners(n))]

    def sideways(blocks):
        even, odd = partners(cols_n)
        near_rim = lax.ppermute(blocks[0], ("yx", "core"), even)
        far_rim = lax.ppermute(blocks[1], ("yx", "core"), odd)
        return [near_rim, far_rim]

    own_v = pltpu.VMEM((z.tall, z.wide_pad, z.lanes), F32)
    side_v = pltpu.VMEM((MARGIN, z.tall_pad, z.lanes), BF16)
    end_v = pltpu.VMEM((z.rim, z.lanes), BF16)
    rim_v = pltpu.VMEM((z.rim, z.lanes), F32)
    tall_v = pltpu.VMEM((z.tall * z.cols, z.band), F32)
    wide_v = pltpu.VMEM((z.tall * z.cols, z.band), BF16)
    flat_v = pltpu.VMEM((z.packed, z.lanes), F32)
    site_v = pltpu.VMEM((z.sites, atom_count), F32)
    outs = [own_v, side_v, side_v]

    own, *sides, pixels, dic, potential, atoms = call(
        functools.partial(first_kernel, z, grid),
        outs
        + [
            pltpu.VMEM((z.sites, z.cell), F32),
            pltpu.VMEM(dictionary.shape, BF16),
            site_v,
            pltpu.VMEM(momentum.shape, BF16),
        ],
        (where, membrane.reshape(z.sites, atom_count), picture, dictionary),
        [
            tall_v,
            pltpu.VMEM((3 * picture.shape[2], z.cell), BF16),
            pltpu.VMEM(picture.shape, F32),
            pltpu.SemaphoreType.DMA((SPAN + 2,)),
        ],
        far=3,
    )
    for repeat in range(SWEEPS):
        last = repeat == SWEEPS - 1
        joined, *ends = call(
            functools.partial(side_kernel, z, grid),
            [own_v, end_v, end_v],
            (where, own, *sideways(sides)),
            [rim_v],
        )
        ends = swapped("row", rows_n, ends)
        final = [
            site_v,
            *outs,
            pltpu.VMEM((z.sites, atom_count), BF16),
        ]
        potential, own, *rest = call(
            functools.partial(sweep_kernel, z, grid, last),
            final if last else [site_v] + outs,
            (where, potential, joined, *ends, pixels, dic),
            [tall_v, own_v, wide_v, rim_v],
        )
        sides = rest[:2]
    final_codes = potential.reshape(membrane.shape)
    sides = sideways(sides)
    message_v = pltpu.VMEM((2, z.sites, atom_count // members), BF16)
    messages = call(
        functools.partial(sort_kernel, z, grid, groups),
        [message_v] * rows_n,
        (where, rest[2], sides[0]),
        [],
    )
    power = rows_n & (rows_n - 1) == 0

    def along_row(blocks):
        return [blocks[0]] + [
            met(block, "row", rows_n, x if power else rows_n - x)
            for x, block in enumerate(blocks[1:], 1)
        ]

    def across_chip(blocks):
        return [met(block, "core", 2, 1) for block in blocks]

    near_codes = along_row(messages)
    far_codes = across_chip(near_codes)
    (packed,) = call(
        functools.partial(pack_kernel, z, grid),
        [pltpu.VMEM((z.packed * 3 // 2, 128), BF16)],
        (where, own, *sides),
        [own_v, flat_v],
    )

    near = along_row([packed] * rows_n)
    far = across_chip(near)
    stride = members * z.cols
    group_atoms = atom_count // members
    half_v = pltpu.VMEM((owned, z.patch // 2), BF16)
    partial_v = pltpu.VMEM((group_atoms, z.patch // 2), BF16)
    (across,) = call(
        functools.partial(turn_kernel, z, grid, groups),
        [pltpu.VMEM((group_atoms, members * z.sites), BF16)],
        (where, *near_codes, *far_codes),
        [pltpu.VMEM((members * z.sites, group_atoms), BF16)],
    )
    *first_half, wide_part = call(
        functools.partial(learn_kernel, z, grid, groups, yx_n),
        [half_v] * yx_n + [pltpu.VMEM((z.tall * stride, z.band), BF16)],
        (where, across, *near, *far),
        [
            partial_v,
            pltpu.VMEM((cores_n, rows_n, z.packed, z.lanes), F32),
            own_v,
        ],
    )
    other_half = call(
        functools.partial(rest_kernel, z, grid, stride),
        [half_v] * yx_n,
        (where, across, wide_part),
        [partial_v],
    )
    parts = [
        block if step == 0 else met(block, "yx", yx_n, step)
        for half in (first_half, other_half)
        for step, block in enumerate(half)
    ]
    new_dictionary, new_momentum = call(
        functools.partial(finish_kernel, z, yx_n),
        [jax.ShapeDtypeStruct(momentum.shape, F32)] * 2,
        (where, momentum, atoms, *parts),
        [
            pltpu.VMEM(momentum.shape, F32),
            pltpu.VMEM(momentum.shape, F32),
            pltpu.SemaphoreType.DMA((4,)),
        ],
        leave=HBM,
    )
    return (final_codes, new_dictionary, new_momentum)


def solution(mesh):
    rows_n, cols_n = (mesh.shape["row"], mesh.shape["col"])
    split = Mesh(mesh.devices.reshape(rows_n, cols_n // 2, 2), ("row", "yx", "core"))
    col = ("yx", "core")
    return jax.shard_map(
        shards,
        mesh=split,
        in_specs=(P(None, "row", col), P("row", col, None), P(), P(("row",) + col, None)),
        out_specs=(P("row", col, None), P(("row",) + col, None), P(("row",) + col, None)),
        check_vma=False,
    )
```

```python
import functools

import jax
import jax.numpy as jnp
from jax import lax
from jax.experimental import pallas as pl
from jax.experimental.pallas import tpu as pltpu
from jax.sharding import Mesh
from jax.sharding import PartitionSpec as P


PATCH_SIDE = 32
STRIDE = 8
SWEEPS = 2
SPAN = PATCH_SIDE // STRIDE
MARGIN = SPAN - 1

THRESHOLD = 0.25
RELAXATION = 0.1
DECAY = 0.9
LEARNING = 0.25
EPSILON = 1e-05


F32 = jnp.float32
BF16 = jnp.bfloat16
VMEM = pl.BlockSpec(memory_space=pltpu.VMEM)
HBM = pl.BlockSpec(memory_space=pltpu.HBM)
PARAMS = pltpu.CompilerParams(vmem_limit_bytes=24 * 1024 * 1024)


def up_to(value, step):
    return -(-value // step) * step


def shrink(potential):
    return potential - jnp.clip(potential, -THRESHOLD, THRESHOLD)


class Sizes:
    def __init__(self, site_rows, site_cols, atoms, patch_len):
        self.rows, self.cols, self.atoms, self.patch = site_rows, site_cols, atoms, patch_len
        self.cell = patch_len // (SPAN * SPAN)
        self.band = SPAN * self.cell
        self.sites = site_rows * site_cols
        self.tall = site_rows + MARGIN
        self.wide = site_cols + MARGIN
        self.wide_pad = up_to(self.wide, 8)
        self.tall_pad = up_to(self.tall, 16)
        self.lanes = up_to(self.cell, 128)
        self.rim = up_to(MARGIN * self.wide, 16)
        self.packed = up_to(self.tall * self.cols + MARGIN * self.tall_pad, 32)
        self.scale = patch_len ** (-0.5)


class Place:
    def __init__(self, rows_n, cols_n):
        self.row = lax.axis_index("row")
        self.core = lax.axis_index("core")
        self.yx = lax.axis_index("yx")
        self.col = self.yx * 2 + self.core
        self.rows_n, self.cols_n = rows_n, cols_n
        self.owner = self.row * cols_n + self.col

    def pairs(self, axis):
        at, n = (self.row, self.rows_n) if axis == 0 else (self.col, self.cols_n)
        before, after = at > 0, at < n - 1
        odd = at & 1
        return [
            (odd == 0, ((True, after), (False, before))),
            (odd == 1, ((False, before), (True, after))),
        ]


def partners(n):
    even, odd = {}, {}
    for i in range(n):
        even[i] = i ^ 1 if i ^ 1 < n else i
        other = ((i + 1) ^ 1) - 1
        odd[i] = other if 0 <= other < n else (n - 1 if i == 0 and n % 2 == 0 else i)
    if n % 2 == 0:
        odd[n - 1] = 0
    return [sorted(even.items()), sorted(odd.items())]


def reconstruct(z, place, coding, dic, pixels, tall_sum, own, ready=None):
    tall_sum[z.sites :, :] = jnp.zeros((z.tall * z.cols - z.sites, z.band), F32)
    for i in range(SPAN):
        if ready is not None:
            ready(i)
        placed = jnp.dot(
            coding, dic[:, i * z.band : (i + 1) * z.band], preferred_element_type=F32
        )
        start = i * z.cols
        if i == 0:
            tall_sum[0 : z.sites, :] = placed
        else:
            tall_sum[start : start + z.sites, :] += placed
    own[...] = jnp.zeros((z.tall, z.wide_pad, z.lanes), F32)
    own[0 : z.rows, 0 : z.cols, 0 : z.cell] = pixels[...].reshape(z.rows, z.cols, z.cell)
    for j in range(SPAN):
        part = tall_sum[:, j * z.cell : (j + 1) * z.cell].reshape(z.tall, z.cols, z.cell)
        own[:, j : j + z.cols, 0 : z.cell] -= part * z.scale

    @pl.when(place.row == place.rows_n - 1)
    def _():
        own[z.rows :] = jnp.zeros((MARGIN, z.wide_pad, z.lanes), F32)

    @pl.when(place.col == place.cols_n - 1)
    def _():
        own[:, z.cols :] = jnp.zeros((z.tall, z.wide_pad - z.cols, z.lanes), F32)


def send_sides(z, place, own, sends):
    for mine, halves in place.pairs(1):

        @pl.when(mine)
        def _(halves=halves):
            for send, (onward, _) in zip(sends, halves):
                first = z.cols if onward else 0
                for c in range(MARGIN):
                    send[c, 0 : z.tall, :] = own[:, first + c, :].astype(BF16)


def add_sides(z, place, whole, received):
    for mine, halves in place.pairs(1):
        for rim, (onward, there) in zip(received, halves):

            @pl.when(mine & there)
            def _(rim=rim, first=z.cols if onward else 0):
                for c in range(MARGIN):
                    whole[:, first + c, :] += rim[c].astype(F32)[0 : z.tall]


def is_equal(a, b):
    return (a == b).astype(F32).astype(BF16)


def cells_of(z, picture, pixels, spread):
    channels, height, width = picture.shape
    turned = picture[...].reshape(channels * height, width).T
    high = turned.astype(BF16)
    rest = turned - high.astype(F32)
    middle = rest.astype(BF16)
    spread[0:width, :] = high
    spread[width : 2 * width, :] = middle
    spread[2 * width :, :] = (rest - middle.astype(F32)).astype(BF16)

    def iota(shape, dim):
        return lax.broadcasted_iota(jnp.int32, shape, dim)

    shape = (channels * height, z.cell)
    line, entry = iota(shape, 0), iota(shape, 1)
    channel, image_row = lax.div(line, height), lax.rem(line, height)
    away = (
        (channel * STRIDE + lax.rem(image_row, STRIDE)) * STRIDE
        + lax.div(image_row, STRIDE) * z.cell
        - lax.div(entry, STRIDE) * STRIDE
    )
    shape = (width, z.cell)
    mine = (lax.rem(iota(shape, 0), STRIDE) == lax.rem(iota(shape, 1), STRIDE)).astype(F32)
    for i in range(z.rows):
        moved = jnp.dot(
            spread[...], is_equal(away, i * z.cell), preferred_element_type=F32
        )
        whole = (moved[0:width] + moved[width : 2 * width]) + moved[2 * width :]
        whole = (whole * mine).reshape(z.cols, STRIDE, z.cell)
        pixels[i * z.cols : (i + 1) * z.cols, :] = jnp.sum(whole, axis=1)


def first_kernel(
    z, grid, membrane, picture, source, own, *rest
):
    (*sends, pixels, dic, potential, atoms, tall_sum, spread, drawing, sems) = rest
    place = Place(*grid)
    early = [
        pltpu.make_async_copy(picture, drawing, sems.at[SPAN]),
        pltpu.make_async_copy(membrane, potential, sems.at[SPAN + 1]),
    ]
    copies = [
        pltpu.make_async_copy(
            source.at[:, i * z.band : (i + 1) * z.band],
            dic.at[:, i * z.band : (i + 1) * z.band],
            sems.at[i],
        )
        for i in range(SPAN)
    ]
    for copy in early + copies:
        copy.start()
    early[0].wait()
    cells_of(z, drawing, pixels, spread)
    early[1].wait()
    coding = shrink(potential[...]).astype(BF16)
    reconstruct(z, place, coding, dic, pixels, tall_sum, own, lambda i: copies[i].wait())
    send_sides(z, place, own, sends)
    owned = atoms.shape[0]
    atoms[...] = dic[pl.ds(pl.multiple_of(place.owner * owned, owned), owned), :]


def side_kernel(z, grid, own, from_even, from_odd, joined, even, odd, rim):
    place = Place(*grid)
    joined[...] = own[...]
    add_sides(z, place, joined, (from_even, from_odd))
    rim[MARGIN * z.wide :, :] = jnp.zeros((z.rim - MARGIN * z.wide, z.lanes), F32)
    for mine, halves in place.pairs(0):

        @pl.when(mine)
        def _(halves=halves):
            for send, (onward, _) in zip((even, odd), halves):
                first = z.rows if onward else 0
                for r in range(MARGIN):
                    start = MARGIN * z.cols + r * MARGIN
                    rim[r * z.cols : (r + 1) * z.cols, :] = joined[first + r, 0 : z.cols, :]
                    rim[start : start + MARGIN, :] = joined[first + r, z.cols : z.wide, :]
                send[...] = rim[...].astype(BF16)


def add_ends(z, place, whole, received, rim):
    for mine, halves in place.pairs(0):
        for block, (onward, there) in zip(received, halves):

            @pl.when(mine & there)
            def _(block=block, first=z.rows if onward else 0):
                rim[...] = block[...].astype(F32)
                for r in range(MARGIN):
                    start = MARGIN * z.cols + r * MARGIN
                    whole[first + r, 0 : z.cols, :] += rim[r * z.cols : (r + 1) * z.cols, :]
                    whole[first + r, z.cols : z.wide, :] += rim[start : start + MARGIN, :]


def windows_of(z, whole, wide_part, first_row, row_stride):
    for j in range(SPAN):
        part = whole[:, j : j + z.cols, 0 : z.cell].astype(BF16)
        for p in range(z.tall):
            wide_part[
                pl.ds(p * row_stride + first_row, z.cols), j * z.cell : (j + 1) * z.cell
            ] = part[p]


def sweep_kernel(
    z, grid, last, potential, joined, from_even, from_odd, pixels, dic, *rest
):
    if last:
        new_potential, own, *sends, codes, tall_sum, whole, wide_part, rim = rest
    else:
        new_potential, own, *sends, tall_sum, whole, wide_part, rim = rest
    place = Place(*grid)
    whole[...] = joined[...]
    add_ends(z, place, whole, (from_even, from_odd), rim)
    windows_of(z, whole, wide_part, 0, z.cols)
    drive = None
    for i in range(SPAN):
        term = lax.dot_general(
            wide_part[i * z.cols : i * z.cols + z.sites, :],
            dic[:, i * z.band : (i + 1) * z.band],
            (((1,), (1,)), ((), ())),
            preferred_element_type=F32,
        )
        drive = term if drive is None else drive + term
    old = potential[...]
    updated = old + RELAXATION * (drive * z.scale + shrink(old) - old)
    active = shrink(updated)
    coding = active.astype(BF16)
    if last:
        new_potential[...] = active
        codes[...] = coding
    else:
        new_potential[...] = updated
    reconstruct(z, place, coding, dic, pixels, tall_sum, own)
    send_sides(z, place, own, sends)


def sort_kernel(z, grid, groups, codes, _, *messages):
    rows_n, cores_n, owned = groups
    span = z.atoms // rows_n
    src = lax.broadcasted_iota(jnp.int32, (span, span), 0)
    dst = lax.broadcasted_iota(jnp.int32, (span, span), 1)
    per_core = span // cores_n
    core, rem = lax.div(dst, per_core), lax.rem(dst, per_core)
    wanted = lax.div(rem, owned) * (owned * cores_n) + core * owned + lax.rem(rem, owned)
    order = is_equal(src, wanted)
    place = Place(*grid)
    for x, message in enumerate(messages):
        r = place.row ^ x if rows_n & (rows_n - 1) == 0 else (place.row - x) % rows_n
        block = codes[:, pl.ds(pl.multiple_of(r * span, span), span)]
        line = jnp.dot(block, order, preferred_element_type=F32).astype(BF16)
        for k in range(cores_n):
            message[k] = line[:, k * per_core : (k + 1) * per_core]


def turn_kernel(z, grid, groups, *rest):
    rows_n, cores_n, _ = groups
    stride = rows_n * cores_n * z.cols
    near, far, (across, codes) = rest[:rows_n], rest[rows_n : 2 * rows_n], rest[2 * rows_n :]
    place = Place(*grid)
    mine = place.core
    for x in range(rows_n):
        d = offset(place.row, x, rows_n)
        for k, message in ((mine, near[x]), (1 - mine, far[x])):
            lines = message[mine]
            for i in range(z.rows):
                at = i * stride + (d * cores_n + k) * z.cols
                codes[pl.ds(pl.multiple_of(at, z.cols), z.cols), :] = lines[
                    i * z.cols : (i + 1) * z.cols, :
                ]
    across[...] = codes[...].astype(F32).T.astype(BF16)


def pack_kernel(z, grid, own, from_even, from_odd, packed, joined, flat):
    joined[...] = own[...]
    add_sides(z, Place(*grid), joined, (from_even, from_odd))
    base = z.tall * z.cols
    flat[base:, :] = jnp.zeros((z.packed - base, z.lanes), F32)
    for p in range(z.tall):
        flat[p * z.cols : (p + 1) * z.cols, :] = joined[p, 0 : z.cols, :]
    for c in range(MARGIN):
        start = base + c * z.tall_pad
        flat[start : start + z.tall, :] = joined[:, z.cols + c, :]
    half = z.packed // 2
    packed[0 : z.packed, :] = flat[:, 0:128].astype(BF16)
    tail = z.cell - 128
    ends = jnp.concatenate([flat[0:half, 128 : z.cell], flat[half:, 128 : z.cell]], axis=1)
    packed[z.packed :, 0 : 2 * tail] = ends.astype(BF16)


def offset(at, step, n):
    return at ^ step if n & (n - 1) == 0 else (at + step) % n


def learn_half(z, grid, across, wide_part, stride, bands, outs, partial):
    count = z.rows * stride
    for n, i in enumerate(bands):
        term = jnp.dot(
            across, wide_part[i * stride : i * stride + count, :], preferred_element_type=F32
        )
        partial[:, n * z.band : (n + 1) * z.band] = (term * z.scale).astype(BF16)
    owned = outs[0].shape[0]
    place = Place(*grid)
    for step, out in enumerate(outs):
        at = offset(place.yx, step, len(outs))
        out[...] = partial[pl.ds(pl.multiple_of(at * owned, owned), owned), :]


def learn_kernel(z, grid, groups, yx_n, across, *rest):
    rows_n, cores_n, _ = groups
    members = rows_n * cores_n
    near, far, outs = rest[:rows_n], rest[rows_n : 2 * rows_n], rest[2 * rows_n :]
    outs, (wide_part, partial, flat, whole) = outs[:yx_n], outs[yx_n:]
    stride = members * z.cols
    base = z.tall * z.cols
    half = z.packed // 2
    tail = z.cell - 128
    place = Place(*grid)
    mine = place.core

    for x in range(rows_n):
        d = offset(place.row, x, rows_n)
        for k, block in ((mine, near[x]), (1 - mine, far[x])):
            flat[k, d, :, 0:128] = block[0 : z.packed, :].astype(F32)
            ends = block[z.packed :, :].astype(F32)
            flat[k, d, 0:half, 128 : z.cell] = ends[:, 0:tail]
            flat[k, d, half:, 128 : z.cell] = ends[:, tail : 2 * tail]
    for k in range(cores_n):
        for r in range(rows_n):
            d = r * cores_n + k
            for source, low, high, at in (
                (r, 0, z.tall, 0),
                (r - 1, z.rows, z.tall, 0),
                (r + 1, 0, MARGIN, z.rows),
            ):
                if not 0 <= source < rows_n:
                    continue
                n = high - low
                main = flat[k, source, low * z.cols : high * z.cols, :]
                main = main.reshape(n, z.cols, z.lanes)
                side = [
                    flat[k, source, base + c * z.tall_pad + low : base + c * z.tall_pad + high, :]
                    for c in range(MARGIN)
                ]
                if source == r:
                    whole[at : at + n, 0 : z.cols, :] = main
                    for c in range(MARGIN):
                        whole[at : at + n, z.cols + c, :] = side[c]
                else:
                    whole[at : at + n, 0 : z.cols, :] += main
                    for c in range(MARGIN):
                        whole[at : at + n, z.cols + c, :] += side[c]
            windows_of(z, whole, wide_part, d * z.cols, stride)
    learn_half(
        z, grid, across[...], wide_part, stride, range(SPAN // 2), outs, partial
    )


def rest_kernel(z, grid, stride, across, wide_part, *rest):
    *outs, partial = rest
    learn_half(
        z, grid, across[...], wide_part, stride, range(SPAN // 2, SPAN), outs, partial
    )


def half_finished(half, momentum, atoms, parts, updated, weights):
    lanes = pl.ds(half * weights.shape[1], weights.shape[1])
    learning = parts[0][...].astype(F32)
    for part in parts[1:]:
        learning = learning + part[...].astype(F32)
    momentum_out = DECAY * momentum[:, lanes] + learning
    updated[...] = momentum_out
    weight = atoms[:, lanes].astype(F32) + LEARNING * momentum_out
    weights[...] = weight
    return jnp.sum(weight * weight, axis=1, keepdims=True)


def early_kernel(momentum, atoms, *rest):
    *parts, updated, weights, power = rest
    total = half_finished(0, momentum, atoms, parts, updated, weights)
    power[...] = jnp.broadcast_to(total, power.shape)


def finish_kernel(z, first_updated, first_weights, first_power, momentum, atoms, *rest):
    *parts, new_dictionary, new_momentum, updated, weights, scaled, sems = rest
    width = z.patch // 2
    halves = [pl.ds(0, width), pl.ds(width, width)]
    copies = [
        pltpu.make_async_copy(first_updated, new_momentum.at[:, halves[0]], sems.at[0]),
        pltpu.make_async_copy(updated, new_momentum.at[:, halves[1]], sems.at[1]),
        pltpu.make_async_copy(scaled.at[0], new_dictionary.at[:, halves[0]], sems.at[2]),
        pltpu.make_async_copy(scaled.at[1], new_dictionary.at[:, halves[1]], sems.at[3]),
    ]
    copies[0].start()
    power = half_finished(1, momentum, atoms, parts, updated, weights)
    copies[1].start()
    norm = lax.rsqrt((first_power[:, 0:1] + power) * (1.0 / z.patch) + EPSILON)
    for h, source in enumerate((first_weights, weights)):
        scaled[h] = source[...] * norm
        copies[2 + h].start()
    for copy in copies:
        copy.wait()


def kept(x, space=pltpu.VMEM):
    return pltpu.with_memory_space_constraint(x, space)


def call(kernel, outs, inputs, scratch, far=0, leave=VMEM):
    specs = [HBM] * far + [VMEM] * (len(inputs) - far)
    placed = [kept(x, pltpu.HBM) for x in inputs[:far]] + [kept(x) for x in inputs[far:]]
    return pl.pallas_call(
        kernel,
        out_shape=outs,
        in_specs=specs,
        out_specs=[leave] * len(outs),
        scratch_shapes=scratch,
        compiler_params=PARAMS,
    )(*placed)


def shards(picture, membrane, dictionary, momentum):
    site_rows, site_cols, atom_count = membrane.shape
    z = Sizes(site_rows, site_cols, atom_count, dictionary.shape[1])
    rows_n, yx_n, cores_n = (lax.axis_size(a) for a in ("row", "yx", "core"))
    cols_n = yx_n * cores_n
    owned = momentum.shape[0]
    groups = (rows_n, cores_n, owned)
    members = rows_n * cores_n
    grid = (rows_n, cols_n)

    def met(block, axis, n, step):
        return lax.ppermute(block, axis, [(i, offset(i, step, n)) for i in range(n)])

    def swapped(axis, n, blocks):
        return [lax.ppermute(b, axis, route) for b, route in zip(blocks, partners(n))]

    def sideways(blocks):
        even, odd = partners(cols_n)
        near_rim = lax.ppermute(blocks[0], ("yx", "core"), even)
        far_rim = lax.ppermute(blocks[1], ("yx", "core"), odd)
        return [near_rim, far_rim]

    own_v = pltpu.VMEM((z.tall, z.wide_pad, z.lanes), F32)
    side_v = pltpu.VMEM((MARGIN, z.tall_pad, z.lanes), BF16)
    end_v = pltpu.VMEM((z.rim, z.lanes), BF16)
    rim_v = pltpu.VMEM((z.rim, z.lanes), F32)
    tall_v = pltpu.VMEM((z.tall * z.cols, z.band), F32)
    wide_v = pltpu.VMEM((z.tall * z.cols, z.band), BF16)
    flat_v = pltpu.VMEM((z.packed, z.lanes), F32)
    site_v = pltpu.VMEM((z.sites, atom_count), F32)
    outs = [own_v, side_v, side_v]

    own, *sides, pixels, dic, potential, atoms = call(
        functools.partial(first_kernel, z, grid),
        outs
        + [
            pltpu.VMEM((z.sites, z.cell), F32),
            pltpu.VMEM(dictionary.shape, BF16),
            site_v,
            pltpu.VMEM(momentum.shape, BF16),
        ],
        (membrane.reshape(z.sites, atom_count), picture, dictionary),
        [
            tall_v,
            pltpu.VMEM((3 * picture.shape[2], z.cell), BF16),
            pltpu.VMEM(picture.shape, F32),
            pltpu.SemaphoreType.DMA((SPAN + 2,)),
        ],
        far=3,
    )
    for repeat in range(SWEEPS):
        last = repeat == SWEEPS - 1
        joined, *ends = call(
            functools.partial(side_kernel, z, grid),
            [own_v, end_v, end_v],
            (own, *sideways(sides)),
            [rim_v],
        )
        ends = swapped("row", rows_n, ends)
        final = [
            site_v,
            *outs,
            pltpu.VMEM((z.sites, atom_count), BF16),
        ]
        potential, own, *rest = call(
            functools.partial(sweep_kernel, z, grid, last),
            final if last else [site_v] + outs,
            (potential, joined, *ends, pixels, dic),
            [tall_v, own_v, wide_v, rim_v],
        )
        sides = rest[:2]
    final_codes = potential.reshape(membrane.shape)
    sides = sideways(sides)
    message_v = pltpu.VMEM((2, z.sites, atom_count // members), BF16)
    messages = call(
        functools.partial(sort_kernel, z, grid, groups),
        [message_v] * rows_n,
        (rest[2], sides[0]),
        [],
    )
    power = rows_n & (rows_n - 1) == 0

    def along_row(blocks):
        return [blocks[0]] + [
            met(block, "row", rows_n, x if power else rows_n - x)
            for x, block in enumerate(blocks[1:], 1)
        ]

    def across_chip(blocks):
        return [met(block, "core", 2, 1) for block in blocks]

    near_codes = along_row(messages)
    far_codes = across_chip(near_codes)
    (packed,) = call(
        functools.partial(pack_kernel, z, grid),
        [pltpu.VMEM((z.packed * 3 // 2, 128), BF16)],
        (own, *sides),
        [own_v, flat_v],
    )

    near = along_row([packed] * rows_n)
    far = across_chip(near)
    stride = members * z.cols
    group_atoms = atom_count // members
    half_v = pltpu.VMEM((owned, z.patch // 2), BF16)
    partial_v = pltpu.VMEM((group_atoms, z.patch // 2), BF16)
    (across,) = call(
        functools.partial(turn_kernel, z, grid, groups),
        [pltpu.VMEM((group_atoms, members * z.sites), BF16)],
        (*near_codes, *far_codes),
        [pltpu.VMEM((members * z.sites, group_atoms), BF16)],
    )
    *first_half, wide_part = call(
        functools.partial(learn_kernel, z, grid, groups, yx_n),
        [half_v] * yx_n + [pltpu.VMEM((z.tall * stride, z.band), BF16)],
        (across, *near, *far),
        [
            partial_v,
            pltpu.VMEM((cores_n, rows_n, z.packed, z.lanes), F32),
            own_v,
        ],
    )
    other_half = call(
        functools.partial(rest_kernel, z, grid, stride),
        [half_v] * yx_n,
        (across, wide_part),
        [partial_v],
    )
    parts = [
        [block if step == 0 else met(block, "yx", yx_n, step) for step, block in enumerate(half)]
        for half in (first_half, other_half)
    ]
    wide_half = (owned, z.patch // 2)
    early = call(
        early_kernel,
        [pltpu.VMEM(s, F32) for s in (wide_half, wide_half, (owned, 128))],
        (momentum, atoms, *parts[0]),
        [],
    )
    new_dictionary, new_momentum = call(
        functools.partial(finish_kernel, z),
        [jax.ShapeDtypeStruct(momentum.shape, F32)] * 2,
        (*early, momentum, atoms, *parts[1]),
        [
            pltpu.VMEM(wide_half, F32),
            pltpu.VMEM(wide_half, F32),
            pltpu.VMEM((2,) + wide_half, F32),
            pltpu.SemaphoreType.DMA((4,)),
        ],
        leave=HBM,
    )
    return (final_codes, new_dictionary, new_momentum)


def solution(mesh):
    rows_n, cols_n = (mesh.shape["row"], mesh.shape["col"])
    split = Mesh(mesh.devices.reshape(rows_n, cols_n // 2, 2), ("row", "yx", "core"))
    col = ("yx", "core")
    return jax.shard_map(
        shards,
        mesh=split,
        in_specs=(P(None, "row", col), P("row", col, None), P(), P(("row",) + col, None)),
        out_specs=(P("row", col, None), P(("row",) + col, None), P(("row",) + col, None)),
        check_vma=False,
    )
```

```python
import functools

import jax
import jax.numpy as jnp
from jax import lax
from jax.experimental import pallas as pl
from jax.experimental.pallas import tpu as pltpu
from jax.sharding import Mesh
from jax.sharding import PartitionSpec as P


PATCH_SIDE = 32
STRIDE = 8
SWEEPS = 2
SPAN = PATCH_SIDE // STRIDE
MARGIN = SPAN - 1

THRESHOLD = 0.25
RELAXATION = 0.1
DECAY = 0.9
LEARNING = 0.25
EPSILON = 1e-05


F32 = jnp.float32
BF16 = jnp.bfloat16
VMEM = pl.BlockSpec(memory_space=pltpu.VMEM)
HBM = pl.BlockSpec(memory_space=pltpu.HBM)
PARAMS = pltpu.CompilerParams(vmem_limit_bytes=24 * 1024 * 1024)


def up_to(value, step):
    return -(-value // step) * step


def shrink(potential):
    return potential - jnp.clip(potential, -THRESHOLD, THRESHOLD)


class Sizes:
    def __init__(self, site_rows, site_cols, atoms, patch_len):
        self.rows, self.cols, self.atoms, self.patch = site_rows, site_cols, atoms, patch_len
        self.cell = patch_len // (SPAN * SPAN)
        self.band = SPAN * self.cell
        self.sites = site_rows * site_cols
        self.tall = site_rows + MARGIN
        self.wide = site_cols + MARGIN
        self.wide_pad = up_to(self.wide, 8)
        self.tall_pad = up_to(self.tall, 16)
        self.lanes = up_to(self.cell, 128)
        self.rim = up_to(MARGIN * self.wide, 16)
        self.packed = up_to(self.tall * self.cols + MARGIN * self.tall_pad, 32)
        self.scale = patch_len ** (-0.5)


class Place:
    def __init__(self, rows_n, cols_n):
        self.row = lax.axis_index("row")
        self.core = lax.axis_index("core")
        self.yx = lax.axis_index("yx")
        self.col = self.yx * 2 + self.core
        self.rows_n, self.cols_n = rows_n, cols_n
        self.owner = self.row * cols_n + self.col

    def pairs(self, axis):
        at, n = (self.row, self.rows_n) if axis == 0 else (self.col, self.cols_n)
        before, after = at > 0, at < n - 1
        odd = at & 1
        return [
            (odd == 0, ((True, after), (False, before))),
            (odd == 1, ((False, before), (True, after))),
        ]


def partners(n):
    even, odd = {}, {}
    for i in range(n):
        even[i] = i ^ 1 if i ^ 1 < n else i
        other = ((i + 1) ^ 1) - 1
        odd[i] = other if 0 <= other < n else (n - 1 if i == 0 and n % 2 == 0 else i)
    if n % 2 == 0:
        odd[n - 1] = 0
    return [sorted(even.items()), sorted(odd.items())]


def reconstruct(z, place, coding, dic, pixels, tall_sum, own, ready=None):
    tall_sum[z.sites :, :] = jnp.zeros((z.tall * z.cols - z.sites, z.band), F32)
    for pair in range(0, SPAN, 2):
        if ready is not None:
            ready(pair)
            ready(pair + 1)
        placed = jnp.dot(
            coding, dic[:, pair * z.band : (pair + 2) * z.band], preferred_element_type=F32
        )
        for i in (pair, pair + 1):
            part = placed[:, (i - pair) * z.band : (i - pair + 1) * z.band]
            start = i * z.cols
            if i == 0:
                tall_sum[0 : z.sites, :] = part
            else:
                tall_sum[start : start + z.sites, :] += part
    own[...] = jnp.zeros((z.tall, z.wide_pad, z.lanes), F32)
    own[0 : z.rows, 0 : z.cols, 0 : z.cell] = pixels[...].reshape(z.rows, z.cols, z.cell)
    for j in range(SPAN):
        part = tall_sum[:, j * z.cell : (j + 1) * z.cell].reshape(z.tall, z.cols, z.cell)
        own[:, j : j + z.cols, 0 : z.cell] -= part * z.scale

    @pl.when(place.row == place.rows_n - 1)
    def _():
        own[z.rows :] = jnp.zeros((MARGIN, z.wide_pad, z.lanes), F32)

    @pl.when(place.col == place.cols_n - 1)
    def _():
        own[:, z.cols :] = jnp.zeros((z.tall, z.wide_pad - z.cols, z.lanes), F32)


def send_sides(z, place, own, sends):
    for mine, halves in place.pairs(1):

        @pl.when(mine)
        def _(halves=halves):
            for send, (onward, _) in zip(sends, halves):
                first = z.cols if onward else 0
                for c in range(MARGIN):
                    send[c, 0 : z.tall, :] = own[:, first + c, :].astype(BF16)


def add_sides(z, place, whole, received):
    for mine, halves in place.pairs(1):
        for rim, (onward, there) in zip(received, halves):

            @pl.when(mine & there)
            def _(rim=rim, first=z.cols if onward else 0):
                for c in range(MARGIN):
                    whole[:, first + c, :] += rim[c].astype(F32)[0 : z.tall]


def is_equal(a, b):
    return (a == b).astype(F32).astype(BF16)


def cells_of(z, picture, pixels, spread, picks, ready):
    channels, height, width = picture.shape

    def iota(shape, dim):
        return lax.broadcasted_iota(jnp.int32, shape, dim)

    shape = (channels * height, z.cell)
    line, entry = iota(shape, 0), iota(shape, 1)
    channel, image_row = lax.div(line, height), lax.rem(line, height)
    away = (
        (channel * STRIDE + lax.rem(image_row, STRIDE)) * STRIDE
        + lax.div(image_row, STRIDE) * z.cell
        - lax.div(entry, STRIDE) * STRIDE
    )
    for i in range(z.rows):
        picks[i] = is_equal(away, i * z.cell)
    shape = (width, z.cell)
    mine = (lax.rem(iota(shape, 0), STRIDE) == lax.rem(iota(shape, 1), STRIDE)).astype(F32)
    ready()
    turned = picture[...].reshape(channels * height, width).T
    high = turned.astype(BF16)
    rest = turned - high.astype(F32)
    middle = rest.astype(BF16)
    spread[0:width, :] = high
    spread[width : 2 * width, :] = middle
    spread[2 * width :, :] = (rest - middle.astype(F32)).astype(BF16)
    for i in range(z.rows):
        moved = jnp.dot(
            spread[...], picks[i], preferred_element_type=F32
        )
        whole = (moved[0:width] + moved[width : 2 * width]) + moved[2 * width :]
        whole = (whole * mine).reshape(z.cols, STRIDE, z.cell)
        pixels[i * z.cols : (i + 1) * z.cols, :] = jnp.sum(whole, axis=1)


def first_kernel(
    z, grid, membrane, picture, source, own, *rest
):
    (*sends, pixels, dic, potential, atoms, tall_sum, spread, picks, drawing, sems) = rest
    place = Place(*grid)
    early = [
        pltpu.make_async_copy(picture, drawing, sems.at[SPAN]),
        pltpu.make_async_copy(membrane, potential, sems.at[SPAN + 1]),
    ]
    copies = [
        pltpu.make_async_copy(
            source.at[:, i * z.band : (i + 1) * z.band],
            dic.at[:, i * z.band : (i + 1) * z.band],
            sems.at[i],
        )
        for i in range(SPAN)
    ]
    for copy in early + copies:
        copy.start()
    cells_of(z, drawing, pixels, spread, picks, early[0].wait)
    early[1].wait()
    coding = shrink(potential[...]).astype(BF16)
    reconstruct(z, place, coding, dic, pixels, tall_sum, own, lambda i: copies[i].wait())
    send_sides(z, place, own, sends)
    owned = atoms.shape[0]
    atoms[...] = dic[pl.ds(pl.multiple_of(place.owner * owned, owned), owned), :]


def flip_kernel(z, dic, turned):
    size = 256
    shape = (size, size)
    same = is_equal(lax.broadcasted_iota(jnp.int32, shape, 0), lax.broadcasted_iota(jnp.int32, shape, 1))
    for i in range(0, z.patch, size):
        turned[i : i + size, :] = lax.dot_general(
            same, dic[:, i : i + size], (((1,), (1,)), ((), ())), preferred_element_type=F32
        ).astype(BF16)


def side_kernel(z, grid, own, from_even, from_odd, joined, even, odd, rim):
    place = Place(*grid)
    joined[...] = own[...]
    add_sides(z, place, joined, (from_even, from_odd))
    rim[MARGIN * z.wide :, :] = jnp.zeros((z.rim - MARGIN * z.wide, z.lanes), F32)
    for mine, halves in place.pairs(0):

        @pl.when(mine)
        def _(halves=halves):
            for send, (onward, _) in zip((even, odd), halves):
                first = z.rows if onward else 0
                for r in range(MARGIN):
                    start = MARGIN * z.cols + r * MARGIN
                    rim[r * z.cols : (r + 1) * z.cols, :] = joined[first + r, 0 : z.cols, :]
                    rim[start : start + MARGIN, :] = joined[first + r, z.cols : z.wide, :]
                send[...] = rim[...].astype(BF16)


def add_ends(z, place, whole, received, rim):
    for mine, halves in place.pairs(0):
        for block, (onward, there) in zip(received, halves):

            @pl.when(mine & there)
            def _(block=block, first=z.rows if onward else 0):
                rim[...] = block[...].astype(F32)
                for r in range(MARGIN):
                    start = MARGIN * z.cols + r * MARGIN
                    whole[first + r, 0 : z.cols, :] += rim[r * z.cols : (r + 1) * z.cols, :]
                    whole[first + r, z.cols : z.wide, :] += rim[start : start + MARGIN, :]


def windows_of(z, whole, wide_part, first_row, row_stride):
    for j in range(SPAN):
        part = whole[:, j : j + z.cols, 0 : z.cell].astype(BF16)
        for p in range(z.tall):
            wide_part[
                pl.ds(p * row_stride + first_row, z.cols), j * z.cell : (j + 1) * z.cell
            ] = part[p]


def sweep_kernel(
    z, grid, last, potential, joined, from_even, from_odd, pixels, dic, turned, *rest
):
    if last:
        new_potential, own, *sends, codes, tall_sum, whole, wide_part, rim = rest
    else:
        new_potential, own, *sends, tall_sum, whole, wide_part, rim = rest
    place = Place(*grid)
    whole[...] = joined[...]
    add_ends(z, place, whole, (from_even, from_odd), rim)
    windows_of(z, whole, wide_part, 0, z.cols)
    drive = None
    for i in range(SPAN):
        term = lax.dot_general(
            wide_part[i * z.cols : i * z.cols + z.sites, :],
            turned[i * z.band : (i + 1) * z.band, :],
            (((1,), (0,)), ((), ())),
            preferred_element_type=F32,
        )
        drive = term if drive is None else drive + term
    old = potential[...]
    updated = old + RELAXATION * (drive * z.scale + shrink(old) - old)
    active = shrink(updated)
    coding = active.astype(BF16)
    if last:
        new_potential[...] = active
        codes[...] = coding
    else:
        new_potential[...] = updated
    reconstruct(z, place, coding, dic, pixels, tall_sum, own)
    send_sides(z, place, own, sends)


def sort_kernel(z, grid, groups, codes, _, *messages):
    rows_n, cores_n, owned = groups
    span = z.atoms // rows_n
    src = lax.broadcasted_iota(jnp.int32, (span, span), 0)
    dst = lax.broadcasted_iota(jnp.int32, (span, span), 1)
    per_core = span // cores_n
    core, rem = lax.div(dst, per_core), lax.rem(dst, per_core)
    wanted = lax.div(rem, owned) * (owned * cores_n) + core * owned + lax.rem(rem, owned)
    order = is_equal(src, wanted)
    place = Place(*grid)
    for x, message in enumerate(messages):
        r = place.row ^ x if rows_n & (rows_n - 1) == 0 else (place.row - x) % rows_n
        block = codes[:, pl.ds(pl.multiple_of(r * span, span), span)]
        line = jnp.dot(block, order, preferred_element_type=F32).astype(BF16)
        for k in range(cores_n):
            message[k] = line[:, k * per_core : (k + 1) * per_core]


def turn_kernel(z, grid, groups, *rest):
    rows_n, cores_n, _ = groups
    stride = rows_n * cores_n * z.cols
    near, far, (across, codes) = rest[:rows_n], rest[rows_n : 2 * rows_n], rest[2 * rows_n :]
    place = Place(*grid)
    mine = place.core
    for x in range(rows_n):
        d = offset(place.row, x, rows_n)
        for k, message in ((mine, near[x]), (1 - mine, far[x])):
            lines = message[mine]
            for i in range(z.rows):
                at = i * stride + (d * cores_n + k) * z.cols
                codes[pl.ds(pl.multiple_of(at, z.cols), z.cols), :] = lines[
                    i * z.cols : (i + 1) * z.cols, :
                ]
    across[...] = codes[...].astype(F32).T.astype(BF16)


def pack_kernel(z, grid, own, from_even, from_odd, packed, joined, flat):
    joined[...] = own[...]
    add_sides(z, Place(*grid), joined, (from_even, from_odd))
    base = z.tall * z.cols
    flat[base:, :] = jnp.zeros((z.packed - base, z.lanes), F32)
    for p in range(z.tall):
        flat[p * z.cols : (p + 1) * z.cols, :] = joined[p, 0 : z.cols, :]
    for c in range(MARGIN):
        start = base + c * z.tall_pad
        flat[start : start + z.tall, :] = joined[:, z.cols + c, :]
    half = z.packed // 2
    packed[0 : z.packed, :] = flat[:, 0:128].astype(BF16)
    tail = z.cell - 128
    ends = jnp.concatenate([flat[0:half, 128 : z.cell], flat[half:, 128 : z.cell]], axis=1)
    packed[z.packed :, 0 : 2 * tail] = ends.astype(BF16)


def offset(at, step, n):
    return at ^ step if n & (n - 1) == 0 else (at + step) % n


def learn_half(z, grid, across, wide_part, stride, bands, outs, partial):
    count = z.rows * stride
    for n, i in enumerate(bands):
        term = jnp.dot(
            across, wide_part[i * stride : i * stride + count, :], preferred_element_type=F32
        )
        partial[:, n * z.band : (n + 1) * z.band] = (term * z.scale).astype(BF16)
    owned = outs[0].shape[0]
    place = Place(*grid)
    for step, out in enumerate(outs):
        at = offset(place.yx, step, len(outs))
        out[...] = partial[pl.ds(pl.multiple_of(at * owned, owned), owned), :]


def learn_kernel(z, grid, groups, yx_n, across, *rest):
    rows_n, cores_n, _ = groups
    members = rows_n * cores_n
    near, far, outs = rest[:rows_n], rest[rows_n : 2 * rows_n], rest[2 * rows_n :]
    outs, (wide_part, partial, flat, whole) = outs[:yx_n], outs[yx_n:]
    stride = members * z.cols
    base = z.tall * z.cols
    half = z.packed // 2
    tail = z.cell - 128
    place = Place(*grid)
    mine = place.core

    for x in range(rows_n):
        d = offset(place.row, x, rows_n)
        for k, block in ((mine, near[x]), (1 - mine, far[x])):
            flat[k, d, :, 0:128] = block[0 : z.packed, :].astype(F32)
            ends = block[z.packed :, :].astype(F32)
            flat[k, d, 0:half, 128 : z.cell] = ends[:, 0:tail]
            flat[k, d, half:, 128 : z.cell] = ends[:, tail : 2 * tail]
    for k in range(cores_n):
        for r in range(rows_n):
            d = r * cores_n + k
            for source, low, high, at in (
                (r, 0, z.tall, 0),
                (r - 1, z.rows, z.tall, 0),
                (r + 1, 0, MARGIN, z.rows),
            ):
                if not 0 <= source < rows_n:
                    continue
                n = high - low
                main = flat[k, source, low * z.cols : high * z.cols, :]
                main = main.reshape(n, z.cols, z.lanes)
                side = [
                    flat[k, source, base + c * z.tall_pad + low : base + c * z.tall_pad + high, :]
                    for c in range(MARGIN)
                ]
                if source == r:
                    whole[at : at + n, 0 : z.cols, :] = main
                    for c in range(MARGIN):
                        whole[at : at + n, z.cols + c, :] = side[c]
                else:
                    whole[at : at + n, 0 : z.cols, :] += main
                    for c in range(MARGIN):
                        whole[at : at + n, z.cols + c, :] += side[c]
            windows_of(z, whole, wide_part, d * z.cols, stride)
    learn_half(
        z, grid, across[...], wide_part, stride, range(SPAN // 2), outs, partial
    )


def rest_kernel(z, grid, stride, across, wide_part, *rest):
    *outs, partial = rest
    learn_half(
        z, grid, across[...], wide_part, stride, range(SPAN // 2, SPAN), outs, partial
    )


def half_finished(half, momentum, atoms, parts, updated, weights):
    lanes = pl.ds(half * weights.shape[1], weights.shape[1])
    learning = parts[0][...].astype(F32)
    for part in parts[1:]:
        learning = learning + part[...].astype(F32)
    momentum_out = DECAY * momentum[:, lanes] + learning
    updated[...] = momentum_out
    weight = atoms[:, lanes].astype(F32) + LEARNING * momentum_out
    weights[...] = weight
    return jnp.sum(weight * weight, axis=1, keepdims=True)


def early_kernel(momentum, atoms, *rest):
    *parts, updated, weights, power = rest
    total = half_finished(0, momentum, atoms, parts, updated, weights)
    power[...] = jnp.broadcast_to(total, power.shape)


def finish_kernel(z, first_updated, first_weights, first_power, momentum, atoms, *rest):
    *parts, new_dictionary, new_momentum, updated, weights, scaled, sems = rest
    width = z.patch // 2
    halves = [pl.ds(0, width), pl.ds(width, width)]
    copies = [
        pltpu.make_async_copy(first_updated, new_momentum.at[:, halves[0]], sems.at[0]),
        pltpu.make_async_copy(updated, new_momentum.at[:, halves[1]], sems.at[1]),
        pltpu.make_async_copy(scaled.at[0], new_dictionary.at[:, halves[0]], sems.at[2]),
        pltpu.make_async_copy(scaled.at[1], new_dictionary.at[:, halves[1]], sems.at[3]),
    ]
    copies[0].start()
    power = half_finished(1, momentum, atoms, parts, updated, weights)
    copies[1].start()
    norm = lax.rsqrt((first_power[:, 0:1] + power) * (1.0 / z.patch) + EPSILON)
    for h, source in enumerate((first_weights, weights)):
        scaled[h] = source[...] * norm
        copies[2 + h].start()
    for copy in copies:
        copy.wait()


def kept(x, space=pltpu.VMEM):
    return pltpu.with_memory_space_constraint(x, space)


def call(kernel, outs, inputs, scratch, far=0, leave=VMEM):
    specs = [HBM] * far + [VMEM] * (len(inputs) - far)
    placed = [kept(x, pltpu.HBM) for x in inputs[:far]] + [kept(x) for x in inputs[far:]]
    return pl.pallas_call(
        kernel,
        out_shape=outs,
        in_specs=specs,
        out_specs=[leave] * len(outs),
        scratch_shapes=scratch,
        compiler_params=PARAMS,
    )(*placed)


def shards(picture, membrane, dictionary, momentum):
    site_rows, site_cols, atom_count = membrane.shape
    z = Sizes(site_rows, site_cols, atom_count, dictionary.shape[1])
    rows_n, yx_n, cores_n = (lax.axis_size(a) for a in ("row", "yx", "core"))
    cols_n = yx_n * cores_n
    owned = momentum.shape[0]
    groups = (rows_n, cores_n, owned)
    members = rows_n * cores_n
    grid = (rows_n, cols_n)

    def met(block, axis, n, step):
        return lax.ppermute(block, axis, [(i, offset(i, step, n)) for i in range(n)])

    def swapped(axis, n, blocks):
        return [lax.ppermute(b, axis, route) for b, route in zip(blocks, partners(n))]

    def sideways(blocks):
        even, odd = partners(cols_n)
        near_rim = lax.ppermute(blocks[0], ("yx", "core"), even)
        far_rim = lax.ppermute(blocks[1], ("yx", "core"), odd)
        return [near_rim, far_rim]

    own_v = pltpu.VMEM((z.tall, z.wide_pad, z.lanes), F32)
    side_v = pltpu.VMEM((MARGIN, z.tall_pad, z.lanes), BF16)
    end_v = pltpu.VMEM((z.rim, z.lanes), BF16)
    rim_v = pltpu.VMEM((z.rim, z.lanes), F32)
    tall_v = pltpu.VMEM((z.tall * z.cols, z.band), F32)
    wide_v = pltpu.VMEM((z.tall * z.cols, z.band), BF16)
    flat_v = pltpu.VMEM((z.packed, z.lanes), F32)
    site_v = pltpu.VMEM((z.sites, atom_count), F32)
    outs = [own_v, side_v, side_v]

    own, *sides, pixels, dic, potential, atoms = call(
        functools.partial(first_kernel, z, grid),
        outs
        + [
            pltpu.VMEM((z.sites, z.cell), F32),
            pltpu.VMEM(dictionary.shape, BF16),
            site_v,
            pltpu.VMEM(momentum.shape, BF16),
        ],
        (membrane.reshape(z.sites, atom_count), picture, dictionary),
        [
            tall_v,
            pltpu.VMEM((3 * picture.shape[2], z.cell), BF16),
            pltpu.VMEM((z.rows, picture.shape[0] * picture.shape[1], z.cell), BF16),
            pltpu.VMEM(picture.shape, F32),
            pltpu.SemaphoreType.DMA((SPAN + 2,)),
        ],
        far=3,
    )
    for repeat in range(SWEEPS):
        last = repeat == SWEEPS - 1
        sides = sideways(sides)
        if repeat == 0:
            (turned,) = call(
                functools.partial(flip_kernel, z),
                [pltpu.VMEM((z.patch, atom_count), BF16)],
                (dic,),
                [],
            )
        joined, *ends = call(
            functools.partial(side_kernel, z, grid), [own_v, end_v, end_v], (own, *sides), [rim_v]
        )
        ends = swapped("row", rows_n, ends)
        final = [
            site_v,
            *outs,
            pltpu.VMEM((z.sites, atom_count), BF16),
        ]
        potential, own, *rest = call(
            functools.partial(sweep_kernel, z, grid, last),
            final if last else [site_v] + outs,
            (potential, joined, *ends, pixels, dic, turned),
            [tall_v, own_v, wide_v, rim_v],
        )
        sides = rest[:2]
    final_codes = potential.reshape(membrane.shape)
    sides = sideways(sides)
    message_v = pltpu.VMEM((2, z.sites, atom_count // members), BF16)
    messages = call(
        functools.partial(sort_kernel, z, grid, groups),
        [message_v] * rows_n,
        (rest[2], sides[0]),
        [],
    )
    power = rows_n & (rows_n - 1) == 0

    def along_row(blocks):
        return [blocks[0]] + [
            met(block, "row", rows_n, x if power else rows_n - x)
            for x, block in enumerate(blocks[1:], 1)
        ]

    def across_chip(blocks):
        return [met(block, "core", 2, 1) for block in blocks]

    near_codes = along_row(messages)
    far_codes = across_chip(near_codes)
    (packed,) = call(
        functools.partial(pack_kernel, z, grid),
        [pltpu.VMEM((z.packed * 3 // 2, 128), BF16)],
        (own, *sides),
        [own_v, flat_v],
    )

    near = along_row([packed] * rows_n)
    far = across_chip(near)
    stride = members * z.cols
    group_atoms = atom_count // members
    half_v = pltpu.VMEM((owned, z.patch // 2), BF16)
    partial_v = pltpu.VMEM((group_atoms, z.patch // 2), BF16)
    (across,) = call(
        functools.partial(turn_kernel, z, grid, groups),
        [pltpu.VMEM((group_atoms, members * z.sites), BF16)],
        (*near_codes, *far_codes),
        [pltpu.VMEM((members * z.sites, group_atoms), BF16)],
    )
    *first_half, wide_part = call(
        functools.partial(learn_kernel, z, grid, groups, yx_n),
        [half_v] * yx_n + [pltpu.VMEM((z.tall * stride, z.band), BF16)],
        (across, *near, *far),
        [
            partial_v,
            pltpu.VMEM((cores_n, rows_n, z.packed, z.lanes), F32),
            own_v,
        ],
    )
    other_half = call(
        functools.partial(rest_kernel, z, grid, stride),
        [half_v] * yx_n,
        (across, wide_part),
        [partial_v],
    )
    parts = [
        [block if step == 0 else met(block, "yx", yx_n, step) for step, block in enumerate(half)]
        for half in (first_half, other_half)
    ]
    wide_half = (owned, z.patch // 2)
    early = call(
        early_kernel,
        [pltpu.VMEM(s, F32) for s in (wide_half, wide_half, (owned, 128))],
        (momentum, atoms, *parts[0]),
        [],
    )
    new_dictionary, new_momentum = call(
        functools.partial(finish_kernel, z),
        [jax.ShapeDtypeStruct(momentum.shape, F32)] * 2,
        (*early, momentum, atoms, *parts[1]),
        [
            pltpu.VMEM(wide_half, F32),
            pltpu.VMEM(wide_half, F32),
            pltpu.VMEM((2,) + wide_half, F32),
            pltpu.SemaphoreType.DMA((4,)),
        ],
        leave=HBM,
    )
    return (final_codes, new_dictionary, new_momentum)


def solution(mesh):
    rows_n, cols_n = (mesh.shape["row"], mesh.shape["col"])
    split = Mesh(mesh.devices.reshape(rows_n, cols_n // 2, 2), ("row", "yx", "core"))
    col = ("yx", "core")
    return jax.shard_map(
        shards,
        mesh=split,
        in_specs=(P(None, "row", col), P("row", col, None), P(), P(("row",) + col, None)),
        out_specs=(P("row", col, None), P(("row",) + col, None), P(("row",) + col, None)),
        check_vma=False,
    )
```

```python
import functools

import jax
import jax.numpy as jnp
from jax import lax
from jax.experimental import pallas as pl
from jax.experimental.pallas import tpu as pltpu
from jax.sharding import Mesh
from jax.sharding import PartitionSpec as P


PATCH_SIDE = 32
STRIDE = 8
SWEEPS = 2
SPAN = PATCH_SIDE // STRIDE
MARGIN = SPAN - 1

THRESHOLD = 0.25
RELAXATION = 0.1
DECAY = 0.9
LEARNING = 0.25
EPSILON = 1e-05


F32 = jnp.float32
BF16 = jnp.bfloat16
VMEM = pl.BlockSpec(memory_space=pltpu.VMEM)
HBM = pl.BlockSpec(memory_space=pltpu.HBM)
PARAMS = pltpu.CompilerParams(vmem_limit_bytes=24 * 1024 * 1024)


def up_to(value, step):
    return -(-value // step) * step


def shrink(potential):
    return potential - jnp.clip(potential, -THRESHOLD, THRESHOLD)


class Sizes:
    def __init__(self, site_rows, site_cols, atoms, patch_len):
        self.rows, self.cols, self.atoms, self.patch = site_rows, site_cols, atoms, patch_len
        self.cell = patch_len // (SPAN * SPAN)
        self.band = SPAN * self.cell
        self.sites = site_rows * site_cols
        self.tall = site_rows + MARGIN
        self.wide = site_cols + MARGIN
        self.wide_pad = up_to(self.wide, 8)
        self.tall_pad = up_to(self.tall, 16)
        self.lanes = up_to(self.cell, 128)
        self.rim = up_to(MARGIN * self.wide, 16)
        self.packed = up_to(self.tall * self.cols + MARGIN * self.tall_pad, 32)
        self.scale = patch_len ** (-0.5)
        self.block = 512 if patch_len % 512 == 0 else self.band


class Place:
    def __init__(self, rows_n, cols_n):
        self.row = lax.axis_index("row")
        self.core = lax.axis_index("core")
        self.yx = lax.axis_index("yx")
        self.col = self.yx * 2 + self.core
        self.rows_n, self.cols_n = rows_n, cols_n
        self.owner = self.row * cols_n + self.col

    def pairs(self, axis):
        at, n = (self.row, self.rows_n) if axis == 0 else (self.col, self.cols_n)
        before, after = at > 0, at < n - 1
        odd = at & 1
        return [
            (odd == 0, ((True, after), (False, before))),
            (odd == 1, ((False, before), (True, after))),
        ]


def partners(n):
    even, odd = {}, {}
    for i in range(n):
        even[i] = i ^ 1 if i ^ 1 < n else i
        other = ((i + 1) ^ 1) - 1
        odd[i] = other if 0 <= other < n else (n - 1 if i == 0 and n % 2 == 0 else i)
    if n % 2 == 0:
        odd[n - 1] = 0
    return [sorted(even.items()), sorted(odd.items())]


def reconstruct(z, place, coding, dic, pixels, tall_sum, own, step, ready=None):
    tall_sum[z.sites :, :] = jnp.zeros((z.tall * z.cols - z.sites, z.band), F32)
    for n, low in enumerate(range(0, z.patch, step)):
        high = low + step
        if ready is not None:
            ready(n)
        placed = jnp.dot(coding, dic[:, low:high], preferred_element_type=F32)
        for i in range(low // z.band, (high - 1) // z.band + 1):
            left, right = max(low, i * z.band), min(high, (i + 1) * z.band)
            part = placed[:, left - low : right - low]
            lanes = slice(left - i * z.band, right - i * z.band)
            if i == 0:
                tall_sum[0 : z.sites, lanes] = part
            else:
                tall_sum[i * z.cols : i * z.cols + z.sites, lanes] += part
    own[...] = jnp.zeros((z.tall, z.wide_pad, z.lanes), F32)
    own[0 : z.rows, 0 : z.cols, 0 : z.cell] = pixels[...].reshape(z.rows, z.cols, z.cell)
    for j in range(SPAN):
        part = tall_sum[:, j * z.cell : (j + 1) * z.cell].reshape(z.tall, z.cols, z.cell)
        own[:, j : j + z.cols, 0 : z.cell] -= part * z.scale

    @pl.when(place.row == place.rows_n - 1)
    def _():
        own[z.rows :] = jnp.zeros((MARGIN, z.wide_pad, z.lanes), F32)

    @pl.when(place.col == place.cols_n - 1)
    def _():
        own[:, z.cols :] = jnp.zeros((z.tall, z.wide_pad - z.cols, z.lanes), F32)


def send_sides(z, place, own, sends):
    for mine, halves in place.pairs(1):

        @pl.when(mine)
        def _(halves=halves):
            for send, (onward, _) in zip(sends, halves):
                first = z.cols if onward else 0
                for c in range(MARGIN):
                    send[c, 0 : z.tall, :] = own[:, first + c, :].astype(BF16)


def add_sides(z, place, whole, received):
    for mine, halves in place.pairs(1):
        for rim, (onward, there) in zip(received, halves):

            @pl.when(mine & there)
            def _(rim=rim, first=z.cols if onward else 0):
                for c in range(MARGIN):
                    whole[:, first + c, :] += rim[c].astype(F32)[0 : z.tall]


def is_equal(a, b):
    return (a == b).astype(F32).astype(BF16)


def cells_of(z, picture, pixels, spread, picks, ready):
    channels, height, width = picture.shape

    def iota(shape, dim):
        return lax.broadcasted_iota(jnp.int32, shape, dim)

    shape = (channels * height, z.cell)
    line, entry = iota(shape, 0), iota(shape, 1)
    channel, image_row = lax.div(line, height), lax.rem(line, height)
    away = (
        (channel * STRIDE + lax.rem(image_row, STRIDE)) * STRIDE
        + lax.div(image_row, STRIDE) * z.cell
        - lax.div(entry, STRIDE) * STRIDE
    )
    for i in range(z.rows):
        picks[i] = is_equal(away, i * z.cell)
    shape = (width, z.cell)
    mine = (lax.rem(iota(shape, 0), STRIDE) == lax.rem(iota(shape, 1), STRIDE)).astype(F32)
    ready()
    turned = picture[...].reshape(channels * height, width).T
    high = turned.astype(BF16)
    rest = turned - high.astype(F32)
    middle = rest.astype(BF16)
    spread[0:width, :] = high
    spread[width : 2 * width, :] = middle
    spread[2 * width :, :] = (rest - middle.astype(F32)).astype(BF16)
    for i in range(z.rows):
        moved = jnp.dot(
            spread[...], picks[i], preferred_element_type=F32
        )
        whole = (moved[0:width] + moved[width : 2 * width]) + moved[2 * width :]
        whole = (whole * mine).reshape(z.cols, STRIDE, z.cell)
        pixels[i * z.cols : (i + 1) * z.cols, :] = jnp.sum(whole, axis=1)


def first_kernel(
    z, grid, membrane, picture, source, own, *rest
):
    (*sends, pixels, dic, potential, atoms, tall_sum, spread, picks, drawing, sems) = rest
    place = Place(*grid)
    early = [
        pltpu.make_async_copy(picture, drawing, sems.at[0]),
        pltpu.make_async_copy(membrane, potential, sems.at[1]),
    ]
    step = z.block
    copies = [
        pltpu.make_async_copy(
            source.at[:, low : low + step], dic.at[:, low : low + step], sems.at[2 + n]
        )
        for n, low in enumerate(range(0, z.patch, step))
    ]
    for copy in early + copies:
        copy.start()
    cells_of(z, drawing, pixels, spread, picks, early[0].wait)
    early[1].wait()
    coding = shrink(potential[...]).astype(BF16)
    reconstruct(z, place, coding, dic, pixels, tall_sum, own, step, lambda i: copies[i].wait())
    send_sides(z, place, own, sends)
    owned = atoms.shape[0]
    atoms[...] = dic[pl.ds(pl.multiple_of(place.owner * owned, owned), owned), :]


def flip_kernel(z, dic, turned):
    size = 256
    shape = (size, size)
    same = is_equal(lax.broadcasted_iota(jnp.int32, shape, 0), lax.broadcasted_iota(jnp.int32, shape, 1))
    for i in range(0, z.patch, size):
        turned[i : i + size, :] = lax.dot_general(
            same, dic[:, i : i + size], (((1,), (1,)), ((), ())), preferred_element_type=F32
        ).astype(BF16)


def side_kernel(z, grid, own, from_even, from_odd, joined, even, odd, rim):
    place = Place(*grid)
    joined[...] = own[...]
    add_sides(z, place, joined, (from_even, from_odd))
    rim[MARGIN * z.wide :, :] = jnp.zeros((z.rim - MARGIN * z.wide, z.lanes), F32)
    for mine, halves in place.pairs(0):

        @pl.when(mine)
        def _(halves=halves):
            for send, (onward, _) in zip((even, odd), halves):
                first = z.rows if onward else 0
                for r in range(MARGIN):
                    start = MARGIN * z.cols + r * MARGIN
                    rim[r * z.cols : (r + 1) * z.cols, :] = joined[first + r, 0 : z.cols, :]
                    rim[start : start + MARGIN, :] = joined[first + r, z.cols : z.wide, :]
                send[...] = rim[...].astype(BF16)


def add_ends(z, place, whole, received, rim):
    for mine, halves in place.pairs(0):
        for block, (onward, there) in zip(received, halves):

            @pl.when(mine & there)
            def _(block=block, first=z.rows if onward else 0):
                rim[...] = block[...].astype(F32)
                for r in range(MARGIN):
                    start = MARGIN * z.cols + r * MARGIN
                    whole[first + r, 0 : z.cols, :] += rim[r * z.cols : (r + 1) * z.cols, :]
                    whole[first + r, z.cols : z.wide, :] += rim[start : start + MARGIN, :]


def windows_of(z, whole, wide_part, first_row, row_stride):
    for j in range(SPAN):
        part = whole[:, j : j + z.cols, 0 : z.cell].astype(BF16)
        for p in range(z.tall):
            wide_part[
                pl.ds(p * row_stride + first_row, z.cols), j * z.cell : (j + 1) * z.cell
            ] = part[p]


def sweep_kernel(
    z, grid, last, potential, joined, from_even, from_odd, pixels, dic, turned, *rest
):
    if last:
        new_potential, own, *sends, codes, tall_sum, whole, wide_part, rim = rest
    else:
        new_potential, own, *sends, tall_sum, whole, wide_part, rim = rest
    place = Place(*grid)
    whole[...] = joined[...]
    add_ends(z, place, whole, (from_even, from_odd), rim)
    windows_of(z, whole, wide_part, 0, z.cols)
    drive = None
    for i in range(SPAN):
        term = lax.dot_general(
            wide_part[i * z.cols : i * z.cols + z.sites, :],
            turned[i * z.band : (i + 1) * z.band, :],
            (((1,), (0,)), ((), ())),
            preferred_element_type=F32,
        )
        drive = term if drive is None else drive + term
    old = potential[...]
    updated = old + RELAXATION * (drive * z.scale + shrink(old) - old)
    active = shrink(updated)
    coding = active.astype(BF16)
    if last:
        new_potential[...] = active
        codes[...] = coding
    else:
        new_potential[...] = updated
    reconstruct(z, place, coding, dic, pixels, tall_sum, own, 2 * z.band)
    send_sides(z, place, own, sends)


def sort_kernel(z, grid, groups, codes, _, *messages):
    rows_n, cores_n, owned = groups
    span = z.atoms // rows_n
    src = lax.broadcasted_iota(jnp.int32, (span, span), 0)
    dst = lax.broadcasted_iota(jnp.int32, (span, span), 1)
    per_core = span // cores_n
    core, rem = lax.div(dst, per_core), lax.rem(dst, per_core)
    wanted = lax.div(rem, owned) * (owned * cores_n) + core * owned + lax.rem(rem, owned)
    order = is_equal(src, wanted)
    place = Place(*grid)
    for x, message in enumerate(messages):
        r = place.row ^ x if rows_n & (rows_n - 1) == 0 else (place.row - x) % rows_n
        block = codes[:, pl.ds(pl.multiple_of(r * span, span), span)]
        line = jnp.dot(block, order, preferred_element_type=F32).astype(BF16)
        for k in range(cores_n):
            message[k] = line[:, k * per_core : (k + 1) * per_core]


def turn_kernel(z, grid, groups, *rest):
    rows_n, cores_n, _ = groups
    stride = rows_n * cores_n * z.cols
    near, far, (across, codes) = rest[:rows_n], rest[rows_n : 2 * rows_n], rest[2 * rows_n :]
    place = Place(*grid)
    mine = place.core
    for x in range(rows_n):
        d = offset(place.row, x, rows_n)
        for k, message in ((mine, near[x]), (1 - mine, far[x])):
            lines = message[mine]
            for i in range(z.rows):
                at = i * stride + (d * cores_n + k) * z.cols
                codes[pl.ds(pl.multiple_of(at, z.cols), z.cols), :] = lines[
                    i * z.cols : (i + 1) * z.cols, :
                ]
    across[...] = codes[...].astype(F32).T.astype(BF16)


def pack_kernel(z, grid, own, from_even, from_odd, packed, joined, flat):
    joined[...] = own[...]
    add_sides(z, Place(*grid), joined, (from_even, from_odd))
    base = z.tall * z.cols
    flat[base:, :] = jnp.zeros((z.packed - base, z.lanes), F32)
    for p in range(z.tall):
        flat[p * z.cols : (p + 1) * z.cols, :] = joined[p, 0 : z.cols, :]
    for c in range(MARGIN):
        start = base + c * z.tall_pad
        flat[start : start + z.tall, :] = joined[:, z.cols + c, :]
    half = z.packed // 2
    packed[0 : z.packed, :] = flat[:, 0:128].astype(BF16)
    tail = z.cell - 128
    ends = jnp.concatenate([flat[0:half, 128 : z.cell], flat[half:, 128 : z.cell]], axis=1)
    packed[z.packed :, 0 : 2 * tail] = ends.astype(BF16)


def offset(at, step, n):
    return at ^ step if n & (n - 1) == 0 else (at + step) % n


def learn_half(z, grid, across, wide_part, stride, bands, outs, partial):
    count = z.rows * stride
    for n, i in enumerate(bands):
        term = jnp.dot(
            across, wide_part[i * stride : i * stride + count, :], preferred_element_type=F32
        )
        partial[:, n * z.band : (n + 1) * z.band] = (term * z.scale).astype(BF16)
    owned = outs[0].shape[0]
    place = Place(*grid)
    for step, out in enumerate(outs):
        at = offset(place.yx, step, len(outs))
        out[...] = partial[pl.ds(pl.multiple_of(at * owned, owned), owned), :]


def learn_kernel(z, grid, groups, yx_n, across, *rest):
    rows_n, cores_n, _ = groups
    members = rows_n * cores_n
    near, far, outs = rest[:rows_n], rest[rows_n : 2 * rows_n], rest[2 * rows_n :]
    outs, (wide_part, partial, flat, whole) = outs[:yx_n], outs[yx_n:]
    stride = members * z.cols
    base = z.tall * z.cols
    half = z.packed // 2
    tail = z.cell - 128
    place = Place(*grid)
    mine = place.core

    for x in range(rows_n):
        d = offset(place.row, x, rows_n)
        for k, block in ((mine, near[x]), (1 - mine, far[x])):
            flat[k, d, :, 0:128] = block[0 : z.packed, :].astype(F32)
            ends = block[z.packed :, :].astype(F32)
            flat[k, d, 0:half, 128 : z.cell] = ends[:, 0:tail]
            flat[k, d, half:, 128 : z.cell] = ends[:, tail : 2 * tail]
    for k in range(cores_n):
        for r in range(rows_n):
            d = r * cores_n + k
            for source, low, high, at in (
                (r, 0, z.tall, 0),
                (r - 1, z.rows, z.tall, 0),
                (r + 1, 0, MARGIN, z.rows),
            ):
                if not 0 <= source < rows_n:
                    continue
                n = high - low
                main = flat[k, source, low * z.cols : high * z.cols, :]
                main = main.reshape(n, z.cols, z.lanes)
                side = [
                    flat[k, source, base + c * z.tall_pad + low : base + c * z.tall_pad + high, :]
                    for c in range(MARGIN)
                ]
                if source == r:
                    whole[at : at + n, 0 : z.cols, :] = main
                    for c in range(MARGIN):
                        whole[at : at + n, z.cols + c, :] = side[c]
                else:
                    whole[at : at + n, 0 : z.cols, :] += main
                    for c in range(MARGIN):
                        whole[at : at + n, z.cols + c, :] += side[c]
            windows_of(z, whole, wide_part, d * z.cols, stride)
    learn_half(
        z, grid, across[...], wide_part, stride, range(SPAN // 2), outs, partial
    )


def rest_kernel(z, grid, stride, across, wide_part, *rest):
    *outs, partial = rest
    learn_half(
        z, grid, across[...], wide_part, stride, range(SPAN // 2, SPAN), outs, partial
    )


def half_finished(half, momentum, atoms, parts, updated, weights):
    lanes = pl.ds(half * weights.shape[1], weights.shape[1])
    learning = parts[0][...].astype(F32)
    for part in parts[1:]:
        learning = learning + part[...].astype(F32)
    momentum_out = DECAY * momentum[:, lanes] + learning
    updated[...] = momentum_out
    weight = atoms[:, lanes].astype(F32) + LEARNING * momentum_out
    weights[...] = weight
    return jnp.sum(weight * weight, axis=1, keepdims=True)


def early_kernel(momentum, atoms, *rest):
    *parts, updated, weights, power = rest
    total = half_finished(0, momentum, atoms, parts, updated, weights)
    power[...] = jnp.broadcast_to(total, power.shape)


def finish_kernel(z, first_updated, first_weights, first_power, momentum, atoms, *rest):
    *parts, new_dictionary, new_momentum, updated, weights, scaled, sems = rest
    width = z.patch // 2
    halves = [pl.ds(0, width), pl.ds(width, width)]
    copies = [
        pltpu.make_async_copy(first_updated, new_momentum.at[:, halves[0]], sems.at[0]),
        pltpu.make_async_copy(updated, new_momentum.at[:, halves[1]], sems.at[1]),
        pltpu.make_async_copy(scaled.at[0], new_dictionary.at[:, halves[0]], sems.at[2]),
        pltpu.make_async_copy(scaled.at[1], new_dictionary.at[:, halves[1]], sems.at[3]),
    ]
    copies[0].start()
    power = half_finished(1, momentum, atoms, parts, updated, weights)
    copies[1].start()
    norm = lax.rsqrt((first_power[:, 0:1] + power) * (1.0 / z.patch) + EPSILON)
    for h, source in enumerate((first_weights, weights)):
        scaled[h] = source[...] * norm
        copies[2 + h].start()
    for copy in copies:
        copy.wait()


def kept(x, space=pltpu.VMEM):
    return pltpu.with_memory_space_constraint(x, space)


def call(kernel, outs, inputs, scratch, far=0, leave=VMEM):
    specs = [HBM] * far + [VMEM] * (len(inputs) - far)
    placed = [kept(x, pltpu.HBM) for x in inputs[:far]] + [kept(x) for x in inputs[far:]]
    return pl.pallas_call(
        kernel,
        out_shape=outs,
        in_specs=specs,
        out_specs=[leave] * len(outs),
        scratch_shapes=scratch,
        compiler_params=PARAMS,
    )(*placed)


def shards(picture, membrane, dictionary, momentum):
    site_rows, site_cols, atom_count = membrane.shape
    z = Sizes(site_rows, site_cols, atom_count, dictionary.shape[1])
    rows_n, yx_n, cores_n = (lax.axis_size(a) for a in ("row", "yx", "core"))
    cols_n = yx_n * cores_n
    owned = momentum.shape[0]
    groups = (rows_n, cores_n, owned)
    members = rows_n * cores_n
    grid = (rows_n, cols_n)

    def met(block, axis, n, step):
        return lax.ppermute(block, axis, [(i, offset(i, step, n)) for i in range(n)])

    def swapped(axis, n, blocks):
        return [lax.ppermute(b, axis, route) for b, route in zip(blocks, partners(n))]

    def sideways(blocks):
        even, odd = partners(cols_n)
        near_rim = lax.ppermute(blocks[0], ("yx", "core"), even)
        far_rim = lax.ppermute(blocks[1], ("yx", "core"), odd)
        return [near_rim, far_rim]

    own_v = pltpu.VMEM((z.tall, z.wide_pad, z.lanes), F32)
    side_v = pltpu.VMEM((MARGIN, z.tall_pad, z.lanes), BF16)
    end_v = pltpu.VMEM((z.rim, z.lanes), BF16)
    rim_v = pltpu.VMEM((z.rim, z.lanes), F32)
    tall_v = pltpu.VMEM((z.tall * z.cols, z.band), F32)
    wide_v = pltpu.VMEM((z.tall * z.cols, z.band), BF16)
    flat_v = pltpu.VMEM((z.packed, z.lanes), F32)
    site_v = pltpu.VMEM((z.sites, atom_count), F32)
    outs = [own_v, side_v, side_v]

    own, *sides, pixels, dic, potential, atoms = call(
        functools.partial(first_kernel, z, grid),
        outs
        + [
            pltpu.VMEM((z.sites, z.cell), F32),
            pltpu.VMEM(dictionary.shape, BF16),
            site_v,
            pltpu.VMEM(momentum.shape, BF16),
        ],
        (membrane.reshape(z.sites, atom_count), picture, dictionary),
        [
            tall_v,
            pltpu.VMEM((3 * picture.shape[2], z.cell), BF16),
            pltpu.VMEM((z.rows, picture.shape[0] * picture.shape[1], z.cell), BF16),
            pltpu.VMEM(picture.shape, F32),
            pltpu.SemaphoreType.DMA((2 + z.patch // z.block,)),
        ],
        far=3,
    )
    for repeat in range(SWEEPS):
        last = repeat == SWEEPS - 1
        sides = sideways(sides)
        if repeat == 0:
            (turned,) = call(
                functools.partial(flip_kernel, z),
                [pltpu.VMEM((z.patch, atom_count), BF16)],
                (dic,),
                [],
            )
        joined, *ends = call(
            functools.partial(side_kernel, z, grid), [own_v, end_v, end_v], (own, *sides), [rim_v]
        )
        ends = swapped("row", rows_n, ends)
        final = [
            site_v,
            *outs,
            pltpu.VMEM((z.sites, atom_count), BF16),
        ]
        potential, own, *rest = call(
            functools.partial(sweep_kernel, z, grid, last),
            final if last else [site_v] + outs,
            (potential, joined, *ends, pixels, dic, turned),
            [tall_v, own_v, wide_v, rim_v],
        )
        sides = rest[:2]
    final_codes = potential.reshape(membrane.shape)
    sides = sideways(sides)
    message_v = pltpu.VMEM((2, z.sites, atom_count // members), BF16)
    messages = call(
        functools.partial(sort_kernel, z, grid, groups),
        [message_v] * rows_n,
        (rest[2], sides[0]),
        [],
    )
    power = rows_n & (rows_n - 1) == 0

    def along_row(blocks):
        return [blocks[0]] + [
            met(block, "row", rows_n, x if power else rows_n - x)
            for x, block in enumerate(blocks[1:], 1)
        ]

    def across_chip(blocks):
        return [met(block, "core", 2, 1) for block in blocks]

    near_codes = along_row(messages)
    far_codes = across_chip(near_codes)
    (packed,) = call(
        functools.partial(pack_kernel, z, grid),
        [pltpu.VMEM((z.packed * 3 // 2, 128), BF16)],
        (own, *sides),
        [own_v, flat_v],
    )

    near = along_row([packed] * rows_n)
    far = across_chip(near)
    stride = members * z.cols
    group_atoms = atom_count // members
    half_v = pltpu.VMEM((owned, z.patch // 2), BF16)
    partial_v = pltpu.VMEM((group_atoms, z.patch // 2), BF16)
    (across,) = call(
        functools.partial(turn_kernel, z, grid, groups),
        [pltpu.VMEM((group_atoms, members * z.sites), BF16)],
        (*near_codes, *far_codes),
        [pltpu.VMEM((members * z.sites, group_atoms), BF16)],
    )
    *first_half, wide_part = call(
        functools.partial(learn_kernel, z, grid, groups, yx_n),
        [half_v] * yx_n + [pltpu.VMEM((z.tall * stride, z.band), BF16)],
        (across, *near, *far),
        [
            partial_v,
            pltpu.VMEM((cores_n, rows_n, z.packed, z.lanes), F32),
            own_v,
        ],
    )
    other_half = call(
        functools.partial(rest_kernel, z, grid, stride),
        [half_v] * yx_n,
        (across, wide_part),
        [partial_v],
    )
    parts = [
        [block if step == 0 else met(block, "yx", yx_n, step) for step, block in enumerate(half)]
        for half in (first_half, other_half)
    ]
    wide_half = (owned, z.patch // 2)
    early = call(
        early_kernel,
        [pltpu.VMEM(s, F32) for s in (wide_half, wide_half, (owned, 128))],
        (momentum, atoms, *parts[0]),
        [],
    )
    new_dictionary, new_momentum = call(
        functools.partial(finish_kernel, z),
        [jax.ShapeDtypeStruct(momentum.shape, F32)] * 2,
        (*early, momentum, atoms, *parts[1]),
        [
            pltpu.VMEM(wide_half, F32),
            pltpu.VMEM(wide_half, F32),
            pltpu.VMEM((2,) + wide_half, F32),
            pltpu.SemaphoreType.DMA((4,)),
        ],
        leave=HBM,
    )
    return (final_codes, new_dictionary, new_momentum)


def solution(mesh):
    rows_n, cols_n = (mesh.shape["row"], mesh.shape["col"])
    split = Mesh(mesh.devices.reshape(rows_n, cols_n // 2, 2), ("row", "yx", "core"))
    col = ("yx", "core")
    return jax.shard_map(
        shards,
        mesh=split,
        in_specs=(P(None, "row", col), P("row", col, None), P(), P(("row",) + col, None)),
        out_specs=(P("row", col, None), P(("row",) + col, None), P(("row",) + col, None)),
        check_vma=False,
    )
```

```python
import functools

import jax
import jax.numpy as jnp
from jax import lax
from jax.experimental import pallas as pl
from jax.experimental.pallas import tpu as pltpu
from jax.sharding import Mesh
from jax.sharding import PartitionSpec as P


PATCH_SIDE = 32
STRIDE = 8
SWEEPS = 2
SPAN = PATCH_SIDE // STRIDE
MARGIN = SPAN - 1

THRESHOLD = 0.25
RELAXATION = 0.1
DECAY = 0.9
LEARNING = 0.25
EPSILON = 1e-05


F32 = jnp.float32
BF16 = jnp.bfloat16
VMEM = pl.BlockSpec(memory_space=pltpu.VMEM)
HBM = pl.BlockSpec(memory_space=pltpu.HBM)
PARAMS = pltpu.CompilerParams(vmem_limit_bytes=24 * 1024 * 1024)


def up_to(value, step):
    return -(-value // step) * step


def shrink(potential):
    return potential - jnp.clip(potential, -THRESHOLD, THRESHOLD)


class Sizes:
    def __init__(self, site_rows, site_cols, atoms, patch_len):
        self.rows, self.cols, self.atoms, self.patch = site_rows, site_cols, atoms, patch_len
        self.cell = patch_len // (SPAN * SPAN)
        self.band = SPAN * self.cell
        self.sites = site_rows * site_cols
        self.tall = site_rows + MARGIN
        self.wide = site_cols + MARGIN
        self.wide_pad = up_to(self.wide, 8)
        self.tall_pad = up_to(self.tall, 16)
        self.lanes = up_to(self.cell, 128)
        self.rim = up_to(MARGIN * self.wide, 16)
        self.packed = up_to(self.tall * self.cols + MARGIN * self.tall_pad, 32)
        self.scale = patch_len ** (-0.5)
        self.block = self.band


class Place:
    def __init__(self, rows_n, cols_n):
        self.row = lax.axis_index("row")
        self.core = lax.axis_index("core")
        self.yx = lax.axis_index("yx")
        self.col = self.yx * 2 + self.core
        self.rows_n, self.cols_n = rows_n, cols_n
        self.owner = self.row * cols_n + self.col

    def pairs(self, axis):
        at, n = (self.row, self.rows_n) if axis == 0 else (self.col, self.cols_n)
        before, after = at > 0, at < n - 1
        odd = at & 1
        return [
            (odd == 0, ((True, after), (False, before))),
            (odd == 1, ((False, before), (True, after))),
        ]


def partners(n):
    even, odd = {}, {}
    for i in range(n):
        even[i] = i ^ 1 if i ^ 1 < n else i
        other = ((i + 1) ^ 1) - 1
        odd[i] = other if 0 <= other < n else (n - 1 if i == 0 and n % 2 == 0 else i)
    if n % 2 == 0:
        odd[n - 1] = 0
    return [sorted(even.items()), sorted(odd.items())]


def reconstruct(z, place, coding, dic, pixels, tall_sum, own, step, ready=None):
    tall_sum[z.sites :, :] = jnp.zeros((z.tall * z.cols - z.sites, z.band), F32)
    for n, low in enumerate(range(0, z.patch, step)):
        high = low + step
        if ready is not None:
            ready(n)
        placed = jnp.dot(coding, dic[:, low:high], preferred_element_type=F32)
        for i in range(low // z.band, (high - 1) // z.band + 1):
            left, right = max(low, i * z.band), min(high, (i + 1) * z.band)
            part = placed[:, left - low : right - low]
            lanes = slice(left - i * z.band, right - i * z.band)
            if i == 0:
                tall_sum[0 : z.sites, lanes] = part
            else:
                tall_sum[i * z.cols : i * z.cols + z.sites, lanes] += part
    own[...] = jnp.zeros((z.tall, z.wide_pad, z.lanes), F32)
    own[0 : z.rows, 0 : z.cols, 0 : z.cell] = pixels[...].reshape(z.rows, z.cols, z.cell)
    for j in range(SPAN):
        part = tall_sum[:, j * z.cell : (j + 1) * z.cell].reshape(z.tall, z.cols, z.cell)
        own[:, j : j + z.cols, 0 : z.cell] -= part * z.scale

    @pl.when(place.row == place.rows_n - 1)
    def _():
        own[z.rows :] = jnp.zeros((MARGIN, z.wide_pad, z.lanes), F32)

    @pl.when(place.col == place.cols_n - 1)
    def _():
        own[:, z.cols :] = jnp.zeros((z.tall, z.wide_pad - z.cols, z.lanes), F32)


def send_sides(z, place, own, sends):
    for mine, halves in place.pairs(1):

        @pl.when(mine)
        def _(halves=halves):
            for send, (onward, _) in zip(sends, halves):
                first = z.cols if onward else 0
                for c in range(MARGIN):
                    send[c, 0 : z.tall, :] = own[:, first + c, :].astype(BF16)


def add_sides(z, place, whole, received):
    for mine, halves in place.pairs(1):
        for rim, (onward, there) in zip(received, halves):

            @pl.when(mine & there)
            def _(rim=rim, first=z.cols if onward else 0):
                for c in range(MARGIN):
                    whole[:, first + c, :] += rim[c].astype(F32)[0 : z.tall]


def is_equal(a, b):
    return (a == b).astype(F32).astype(BF16)


def cells_of(z, picture, pixels, spread, ready):
    channels, height, width = picture.shape

    def iota(shape, dim):
        return lax.broadcasted_iota(jnp.int32, shape, dim)

    shape = (channels * height, z.cell)
    line, entry = iota(shape, 0), iota(shape, 1)
    channel, image_row = lax.div(line, height), lax.rem(line, height)
    away = (
        (channel * STRIDE + lax.rem(image_row, STRIDE)) * STRIDE
        + lax.div(image_row, STRIDE) * z.cell
        - lax.div(entry, STRIDE) * STRIDE
    )
    shape = (width, z.cell)
    mine = (lax.rem(iota(shape, 0), STRIDE) == lax.rem(iota(shape, 1), STRIDE)).astype(F32)
    ready()
    turned = picture[...].reshape(channels * height, width).T
    high = turned.astype(BF16)
    rest = turned - high.astype(F32)
    middle = rest.astype(BF16)
    spread[0:width, :] = high
    spread[width : 2 * width, :] = middle
    spread[2 * width :, :] = (rest - middle.astype(F32)).astype(BF16)
    for i in range(z.rows):
        moved = jnp.dot(
            spread[...], is_equal(away, i * z.cell), preferred_element_type=F32
        )
        whole = (moved[0:width] + moved[width : 2 * width]) + moved[2 * width :]
        whole = (whole * mine).reshape(z.cols, STRIDE, z.cell)
        pixels[i * z.cols : (i + 1) * z.cols, :] = jnp.sum(whole, axis=1)


def first_kernel(
    z, grid, membrane, picture, source, own, *rest
):
    (*sends, pixels, dic, potential, atoms, tall_sum, spread, drawing, sems) = rest
    place = Place(*grid)
    early = [
        pltpu.make_async_copy(picture, drawing, sems.at[0]),
        pltpu.make_async_copy(membrane, potential, sems.at[1]),
    ]
    step = z.block
    copies = [
        pltpu.make_async_copy(
            source.at[:, low : low + step], dic.at[:, low : low + step], sems.at[2 + n]
        )
        for n, low in enumerate(range(0, z.patch, step))
    ]
    for copy in early + copies:
        copy.start()
    cells_of(z, drawing, pixels, spread, early[0].wait)
    early[1].wait()
    coding = shrink(potential[...]).astype(BF16)
    reconstruct(z, place, coding, dic, pixels, tall_sum, own, step, lambda i: copies[i].wait())
    send_sides(z, place, own, sends)
    owned = atoms.shape[0]
    atoms[...] = dic[pl.ds(pl.multiple_of(place.owner * owned, owned), owned), :]


def flip_kernel(z, dic, turned):
    size = 256
    shape = (size, size)
    same = is_equal(lax.broadcasted_iota(jnp.int32, shape, 0), lax.broadcasted_iota(jnp.int32, shape, 1))
    for i in range(0, z.patch, size):
        turned[i : i + size, :] = lax.dot_general(
            same, dic[:, i : i + size], (((1,), (1,)), ((), ())), preferred_element_type=F32
        ).astype(BF16)


def side_kernel(z, grid, own, from_even, from_odd, joined, even, odd, rim):
    place = Place(*grid)
    joined[...] = own[...]
    add_sides(z, place, joined, (from_even, from_odd))
    rim[MARGIN * z.wide :, :] = jnp.zeros((z.rim - MARGIN * z.wide, z.lanes), F32)
    for mine, halves in place.pairs(0):

        @pl.when(mine)
        def _(halves=halves):
            for send, (onward, _) in zip((even, odd), halves):
                first = z.rows if onward else 0
                for r in range(MARGIN):
                    start = MARGIN * z.cols + r * MARGIN
                    rim[r * z.cols : (r + 1) * z.cols, :] = joined[first + r, 0 : z.cols, :]
                    rim[start : start + MARGIN, :] = joined[first + r, z.cols : z.wide, :]
                send[...] = rim[...].astype(BF16)


def add_ends(z, place, whole, received, rim):
    for mine, halves in place.pairs(0):
        for block, (onward, there) in zip(received, halves):

            @pl.when(mine & there)
            def _(block=block, first=z.rows if onward else 0):
                rim[...] = block[...].astype(F32)
                for r in range(MARGIN):
                    start = MARGIN * z.cols + r * MARGIN
                    whole[first + r, 0 : z.cols, :] += rim[r * z.cols : (r + 1) * z.cols, :]
                    whole[first + r, z.cols : z.wide, :] += rim[start : start + MARGIN, :]


def windows_of(z, whole, wide_part, first_row, row_stride):
    for j in range(SPAN):
        part = whole[:, j : j + z.cols, 0 : z.cell].astype(BF16)
        for p in range(z.tall):
            wide_part[
                pl.ds(p * row_stride + first_row, z.cols), j * z.cell : (j + 1) * z.cell
            ] = part[p]


def sweep_kernel(
    z, grid, last, potential, joined, from_even, from_odd, pixels, dic, turned, *rest
):
    if last:
        new_potential, own, *sends, codes, tall_sum, whole, wide_part, rim = rest
    else:
        new_potential, own, *sends, tall_sum, whole, wide_part, rim = rest
    place = Place(*grid)
    whole[...] = joined[...]
    add_ends(z, place, whole, (from_even, from_odd), rim)
    windows_of(z, whole, wide_part, 0, z.cols)
    drive = None
    for i in range(SPAN):
        term = lax.dot_general(
            wide_part[i * z.cols : i * z.cols + z.sites, :],
            turned[i * z.band : (i + 1) * z.band, :],
            (((1,), (0,)), ((), ())),
            preferred_element_type=F32,
        )
        drive = term if drive is None else drive + term
    old = potential[...]
    updated = old + RELAXATION * (drive * z.scale + shrink(old) - old)
    active = shrink(updated)
    coding = active.astype(BF16)
    if last:
        new_potential[...] = active
        codes[...] = coding
    else:
        new_potential[...] = updated
    reconstruct(z, place, coding, dic, pixels, tall_sum, own, 2 * z.band)
    send_sides(z, place, own, sends)


def sort_kernel(z, grid, groups, codes, _, *messages):
    rows_n, cores_n, owned = groups
    span = z.atoms // rows_n
    src = lax.broadcasted_iota(jnp.int32, (span, span), 0)
    dst = lax.broadcasted_iota(jnp.int32, (span, span), 1)
    per_core = span // cores_n
    core, rem = lax.div(dst, per_core), lax.rem(dst, per_core)
    wanted = lax.div(rem, owned) * (owned * cores_n) + core * owned + lax.rem(rem, owned)
    order = is_equal(src, wanted)
    place = Place(*grid)
    for x, message in enumerate(messages):
        r = place.row ^ x if rows_n & (rows_n - 1) == 0 else (place.row - x) % rows_n
        block = codes[:, pl.ds(pl.multiple_of(r * span, span), span)]
        line = jnp.dot(block, order, preferred_element_type=F32).astype(BF16)
        for k in range(cores_n):
            message[k] = line[:, k * per_core : (k + 1) * per_core]


def turn_kernel(z, grid, groups, *rest):
    rows_n, cores_n, _ = groups
    stride = rows_n * cores_n * z.cols
    near, far, (across, codes) = rest[:rows_n], rest[rows_n : 2 * rows_n], rest[2 * rows_n :]
    place = Place(*grid)
    mine = place.core
    for x in range(rows_n):
        d = offset(place.row, x, rows_n)
        for k, message in ((mine, near[x]), (1 - mine, far[x])):
            lines = message[mine]
            for i in range(z.rows):
                at = i * stride + (d * cores_n + k) * z.cols
                codes[pl.ds(pl.multiple_of(at, z.cols), z.cols), :] = lines[
                    i * z.cols : (i + 1) * z.cols, :
                ]
    across[...] = codes[...].astype(F32).T.astype(BF16)


def pack_kernel(z, grid, own, from_even, from_odd, packed, joined, flat):
    joined[...] = own[...]
    add_sides(z, Place(*grid), joined, (from_even, from_odd))
    base = z.tall * z.cols
    flat[base:, :] = jnp.zeros((z.packed - base, z.lanes), F32)
    for p in range(z.tall):
        flat[p * z.cols : (p + 1) * z.cols, :] = joined[p, 0 : z.cols, :]
    for c in range(MARGIN):
        start = base + c * z.tall_pad
        flat[start : start + z.tall, :] = joined[:, z.cols + c, :]
    half = z.packed // 2
    packed[0 : z.packed, :] = flat[:, 0:128].astype(BF16)
    tail = z.cell - 128
    ends = jnp.concatenate([flat[0:half, 128 : z.cell], flat[half:, 128 : z.cell]], axis=1)
    packed[z.packed :, 0 : 2 * tail] = ends.astype(BF16)


def offset(at, step, n):
    return at ^ step if n & (n - 1) == 0 else (at + step) % n


def learn_half(z, grid, across, wide_part, stride, bands, outs, partial):
    count = z.rows * stride
    for n, i in enumerate(bands):
        term = jnp.dot(
            across, wide_part[i * stride : i * stride + count, :], preferred_element_type=F32
        )
        partial[:, n * z.band : (n + 1) * z.band] = (term * z.scale).astype(BF16)
    owned = outs[0].shape[0]
    place = Place(*grid)
    for step, out in enumerate(outs):
        at = offset(place.yx, step, len(outs))
        out[...] = partial[pl.ds(pl.multiple_of(at * owned, owned), owned), :]


def learn_kernel(z, grid, groups, yx_n, across, *rest):
    rows_n, cores_n, _ = groups
    members = rows_n * cores_n
    near, far, outs = rest[:rows_n], rest[rows_n : 2 * rows_n], rest[2 * rows_n :]
    outs, (wide_part, partial, flat, whole) = outs[:yx_n], outs[yx_n:]
    stride = members * z.cols
    base = z.tall * z.cols
    half = z.packed // 2
    tail = z.cell - 128
    place = Place(*grid)
    mine = place.core

    for x in range(rows_n):
        d = offset(place.row, x, rows_n)
        for k, block in ((mine, near[x]), (1 - mine, far[x])):
            flat[k, d, :, 0:128] = block[0 : z.packed, :].astype(F32)
            ends = block[z.packed :, :].astype(F32)
            flat[k, d, 0:half, 128 : z.cell] = ends[:, 0:tail]
            flat[k, d, half:, 128 : z.cell] = ends[:, tail : 2 * tail]
    for k in range(cores_n):
        for r in range(rows_n):
            d = r * cores_n + k
            for source, low, high, at in (
                (r, 0, z.tall, 0),
                (r - 1, z.rows, z.tall, 0),
                (r + 1, 0, MARGIN, z.rows),
            ):
                if not 0 <= source < rows_n:
                    continue
                n = high - low
                main = flat[k, source, low * z.cols : high * z.cols, :]
                main = main.reshape(n, z.cols, z.lanes)
                side = [
                    flat[k, source, base + c * z.tall_pad + low : base + c * z.tall_pad + high, :]
                    for c in range(MARGIN)
                ]
                if source == r:
                    whole[at : at + n, 0 : z.cols, :] = main
                    for c in range(MARGIN):
                        whole[at : at + n, z.cols + c, :] = side[c]
                else:
                    whole[at : at + n, 0 : z.cols, :] += main
                    for c in range(MARGIN):
                        whole[at : at + n, z.cols + c, :] += side[c]
            windows_of(z, whole, wide_part, d * z.cols, stride)
    learn_half(
        z, grid, across[...], wide_part, stride, range(SPAN // 2), outs, partial
    )


def rest_kernel(z, grid, stride, across, wide_part, *rest):
    *outs, partial = rest
    learn_half(
        z, grid, across[...], wide_part, stride, range(SPAN // 2, SPAN), outs, partial
    )


def half_finished(half, momentum, atoms, parts, updated, weights):
    lanes = pl.ds(half * weights.shape[1], weights.shape[1])
    learning = parts[0][...].astype(F32)
    for part in parts[1:]:
        learning = learning + part[...].astype(F32)
    momentum_out = DECAY * momentum[:, lanes] + learning
    updated[...] = momentum_out
    weight = atoms[:, lanes].astype(F32) + LEARNING * momentum_out
    weights[...] = weight
    return jnp.sum(weight * weight, axis=1, keepdims=True)


def early_kernel(momentum, atoms, *rest):
    *parts, updated, weights, power = rest
    total = half_finished(0, momentum, atoms, parts, updated, weights)
    power[...] = jnp.broadcast_to(total, power.shape)


def finish_kernel(z, first_updated, first_weights, first_power, momentum, atoms, *rest):
    *parts, new_dictionary, new_momentum, updated, weights, scaled, sems = rest
    width = z.patch // 2
    halves = [pl.ds(0, width), pl.ds(width, width)]
    copies = [
        pltpu.make_async_copy(first_updated, new_momentum.at[:, halves[0]], sems.at[0]),
        pltpu.make_async_copy(updated, new_momentum.at[:, halves[1]], sems.at[1]),
        pltpu.make_async_copy(scaled.at[0], new_dictionary.at[:, halves[0]], sems.at[2]),
        pltpu.make_async_copy(scaled.at[1], new_dictionary.at[:, halves[1]], sems.at[3]),
    ]
    copies[0].start()
    power = half_finished(1, momentum, atoms, parts, updated, weights)
    copies[1].start()
    norm = lax.rsqrt((first_power[:, 0:1] + power) * (1.0 / z.patch) + EPSILON)
    for h, source in enumerate((first_weights, weights)):
        scaled[h] = source[...] * norm
        copies[2 + h].start()
    for copy in copies:
        copy.wait()


def kept(x, space=pltpu.VMEM):
    return pltpu.with_memory_space_constraint(x, space)


def call(kernel, outs, inputs, scratch, far=0, leave=VMEM):
    specs = [HBM] * far + [VMEM] * (len(inputs) - far)
    placed = [kept(x, pltpu.HBM) for x in inputs[:far]] + [kept(x) for x in inputs[far:]]
    return pl.pallas_call(
        kernel,
        out_shape=outs,
        in_specs=specs,
        out_specs=[leave] * len(outs),
        scratch_shapes=scratch,
        compiler_params=PARAMS,
    )(*placed)


def shards(picture, membrane, dictionary, momentum):
    site_rows, site_cols, atom_count = membrane.shape
    z = Sizes(site_rows, site_cols, atom_count, dictionary.shape[1])
    rows_n, yx_n, cores_n = (lax.axis_size(a) for a in ("row", "yx", "core"))
    cols_n = yx_n * cores_n
    owned = momentum.shape[0]
    groups = (rows_n, cores_n, owned)
    members = rows_n * cores_n
    grid = (rows_n, cols_n)

    def met(block, axis, n, step):
        return lax.ppermute(block, axis, [(i, offset(i, step, n)) for i in range(n)])

    def swapped(axis, n, blocks):
        return [lax.ppermute(b, axis, route) for b, route in zip(blocks, partners(n))]

    def sideways(blocks):
        even, odd = partners(cols_n)
        near_rim = lax.ppermute(blocks[0], ("yx", "core"), even)
        far_rim = lax.ppermute(blocks[1], ("yx", "core"), odd)
        return [near_rim, far_rim]

    own_v = pltpu.VMEM((z.tall, z.wide_pad, z.lanes), F32)
    side_v = pltpu.VMEM((MARGIN, z.tall_pad, z.lanes), BF16)
    end_v = pltpu.VMEM((z.rim, z.lanes), BF16)
    rim_v = pltpu.VMEM((z.rim, z.lanes), F32)
    tall_v = pltpu.VMEM((z.tall * z.cols, z.band), F32)
    wide_v = pltpu.VMEM((z.tall * z.cols, z.band), BF16)
    flat_v = pltpu.VMEM((z.packed, z.lanes), F32)
    site_v = pltpu.VMEM((z.sites, atom_count), F32)
    outs = [own_v, side_v, side_v]

    own, *sides, pixels, dic, potential, atoms = call(
        functools.partial(first_kernel, z, grid),
        outs
        + [
            pltpu.VMEM((z.sites, z.cell), F32),
            pltpu.VMEM(dictionary.shape, BF16),
            site_v,
            pltpu.VMEM(momentum.shape, BF16),
        ],
        (membrane.reshape(z.sites, atom_count), picture, dictionary),
        [
            tall_v,
            pltpu.VMEM((3 * picture.shape[2], z.cell), BF16),
            pltpu.VMEM(picture.shape, F32),
            pltpu.SemaphoreType.DMA((2 + z.patch // z.block,)),
        ],
        far=3,
    )
    for repeat in range(SWEEPS):
        last = repeat == SWEEPS - 1
        sides = sideways(sides)
        if repeat == 0:
            (turned,) = call(
                functools.partial(flip_kernel, z),
                [pltpu.VMEM((z.patch, atom_count), BF16)],
                (dic,),
                [],
            )
        joined, *ends = call(
            functools.partial(side_kernel, z, grid), [own_v, end_v, end_v], (own, *sides), [rim_v]
        )
        ends = swapped("row", rows_n, ends)
        final = [
            site_v,
            *outs,
            pltpu.VMEM((z.sites, atom_count), BF16),
        ]
        potential, own, *rest = call(
            functools.partial(sweep_kernel, z, grid, last),
            final if last else [site_v] + outs,
            (potential, joined, *ends, pixels, dic, turned),
            [tall_v, own_v, wide_v, rim_v],
        )
        sides = rest[:2]
    final_codes = potential.reshape(membrane.shape)
    sides = sideways(sides)
    message_v = pltpu.VMEM((2, z.sites, atom_count // members), BF16)
    messages = call(
        functools.partial(sort_kernel, z, grid, groups),
        [message_v] * rows_n,
        (rest[2], sides[0]),
        [],
    )
    power = rows_n & (rows_n - 1) == 0

    def along_row(blocks):
        return [blocks[0]] + [
            met(block, "row", rows_n, x if power else rows_n - x)
            for x, block in enumerate(blocks[1:], 1)
        ]

    def across_chip(blocks):
        return [met(block, "core", 2, 1) for block in blocks]

    near_codes = along_row(messages)
    far_codes = across_chip(near_codes)
    (packed,) = call(
        functools.partial(pack_kernel, z, grid),
        [pltpu.VMEM((z.packed * 3 // 2, 128), BF16)],
        (own, *sides),
        [own_v, flat_v],
    )

    near = [packed]
    for x in range(1, rows_n):
        low = x & -x
        if power:
            near.append(met(near[x - low], "row", rows_n, low))
        else:
            near.append(met(packed, "row", rows_n, rows_n - x))
    far = across_chip(near)
    stride = members * z.cols
    group_atoms = atom_count // members
    half_v = pltpu.VMEM((owned, z.patch // 2), BF16)
    partial_v = pltpu.VMEM((group_atoms, z.patch // 2), BF16)
    (across,) = call(
        functools.partial(turn_kernel, z, grid, groups),
        [pltpu.VMEM((group_atoms, members * z.sites), BF16)],
        (*near_codes, *far_codes),
        [pltpu.VMEM((members * z.sites, group_atoms), BF16)],
    )
    *first_half, wide_part = call(
        functools.partial(learn_kernel, z, grid, groups, yx_n),
        [half_v] * yx_n + [pltpu.VMEM((z.tall * stride, z.band), BF16)],
        (across, *near, *far),
        [
            partial_v,
            pltpu.VMEM((cores_n, rows_n, z.packed, z.lanes), F32),
            own_v,
        ],
    )
    other_half = call(
        functools.partial(rest_kernel, z, grid, stride),
        [half_v] * yx_n,
        (across, wide_part),
        [partial_v],
    )
    parts = [
        [block if step == 0 else met(block, "yx", yx_n, step) for step, block in enumerate(half)]
        for half in (first_half, other_half)
    ]
    wide_half = (owned, z.patch // 2)
    early = call(
        early_kernel,
        [pltpu.VMEM(s, F32) for s in (wide_half, wide_half, (owned, 128))],
        (momentum, atoms, *parts[0]),
        [],
    )
    new_dictionary, new_momentum = call(
        functools.partial(finish_kernel, z),
        [jax.ShapeDtypeStruct(momentum.shape, F32)] * 2,
        (*early, momentum, atoms, *parts[1]),
        [
            pltpu.VMEM(wide_half, F32),
            pltpu.VMEM(wide_half, F32),
            pltpu.VMEM((2,) + wide_half, F32),
            pltpu.SemaphoreType.DMA((4,)),
        ],
        leave=HBM,
    )
    return (final_codes, new_dictionary, new_momentum)


def solution(mesh):
    rows_n, cols_n = (mesh.shape["row"], mesh.shape["col"])
    split = Mesh(mesh.devices.reshape(rows_n, cols_n // 2, 2), ("row", "yx", "core"))
    col = ("yx", "core")
    return jax.shard_map(
        shards,
        mesh=split,
        in_specs=(P(None, "row", col), P("row", col, None), P(), P(("row",) + col, None)),
        out_specs=(P("row", col, None), P(("row",) + col, None), P(("row",) + col, None)),
        check_vma=False,
    )
```

```python
import functools

import jax
import jax.numpy as jnp
from jax import lax
from jax.experimental import pallas as pl
from jax.experimental.pallas import tpu as pltpu
from jax.sharding import Mesh
from jax.sharding import PartitionSpec as P


PATCH_SIDE = 32
STRIDE = 8
SWEEPS = 2
SPAN = PATCH_SIDE // STRIDE
MARGIN = SPAN - 1

THRESHOLD = 0.25
RELAXATION = 0.1
DECAY = 0.9
LEARNING = 0.25
EPSILON = 1e-05


F32 = jnp.float32
BF16 = jnp.bfloat16
VMEM = pl.BlockSpec(memory_space=pltpu.VMEM)
HBM = pl.BlockSpec(memory_space=pltpu.HBM)
PARAMS = pltpu.CompilerParams(vmem_limit_bytes=24 * 1024 * 1024)


def up_to(value, step):
    return -(-value // step) * step


def shrink(potential):
    return potential - jnp.clip(potential, -THRESHOLD, THRESHOLD)


class Sizes:
    def __init__(self, site_rows, site_cols, atoms, patch_len):
        self.rows, self.cols, self.atoms, self.patch = site_rows, site_cols, atoms, patch_len
        self.cell = patch_len // (SPAN * SPAN)
        self.band = SPAN * self.cell
        self.sites = site_rows * site_cols
        self.tall = site_rows + MARGIN
        self.wide = site_cols + MARGIN
        self.wide_pad = up_to(self.wide, 8)
        self.tall_pad = up_to(self.tall, 16)
        self.lanes = up_to(self.cell, 128)
        self.rim = up_to(MARGIN * self.wide, 16)
        self.packed = up_to(self.tall * self.cols + MARGIN * self.tall_pad, 32)
        self.scale = patch_len ** (-0.5)
        self.block = self.band


class Place:
    def __init__(self, rows_n, cols_n):
        self.row = lax.axis_index("row")
        self.core = lax.axis_index("core")
        self.yx = lax.axis_index("yx")
        self.col = self.yx * 2 + self.core
        self.rows_n, self.cols_n = rows_n, cols_n
        self.owner = self.row * cols_n + self.col

    def pairs(self, axis):
        at, n = (self.row, self.rows_n) if axis == 0 else (self.col, self.cols_n)
        before, after = at > 0, at < n - 1
        odd = at & 1
        return [
            (odd == 0, ((True, after), (False, before))),
            (odd == 1, ((False, before), (True, after))),
        ]


def partners(n):
    even, odd = {}, {}
    for i in range(n):
        even[i] = i ^ 1 if i ^ 1 < n else i
        other = ((i + 1) ^ 1) - 1
        odd[i] = other if 0 <= other < n else (n - 1 if i == 0 and n % 2 == 0 else i)
    if n % 2 == 0:
        odd[n - 1] = 0
    return [sorted(even.items()), sorted(odd.items())]


def reconstruct(z, place, coding, dic, pixels, tall_sum, own, step, ready=None):
    tall_sum[z.sites :, :] = jnp.zeros((z.tall * z.cols - z.sites, z.band), F32)
    for n, low in enumerate(range(0, z.patch, step)):
        high = low + step
        if ready is not None:
            ready(n)
        placed = jnp.dot(coding, dic[:, low:high], preferred_element_type=F32)
        for i in range(low // z.band, (high - 1) // z.band + 1):
            left, right = max(low, i * z.band), min(high, (i + 1) * z.band)
            part = placed[:, left - low : right - low]
            lanes = slice(left - i * z.band, right - i * z.band)
            if i == 0:
                tall_sum[0 : z.sites, lanes] = part
            else:
                tall_sum[i * z.cols : i * z.cols + z.sites, lanes] += part
    own[...] = jnp.zeros((z.tall, z.wide_pad, z.lanes), F32)
    own[0 : z.rows, 0 : z.cols, 0 : z.cell] = pixels[...].reshape(z.rows, z.cols, z.cell)
    for j in range(SPAN):
        part = tall_sum[:, j * z.cell : (j + 1) * z.cell].reshape(z.tall, z.cols, z.cell)
        own[:, j : j + z.cols, 0 : z.cell] -= part * z.scale

    @pl.when(place.row == place.rows_n - 1)
    def _():
        own[z.rows :] = jnp.zeros((MARGIN, z.wide_pad, z.lanes), F32)

    @pl.when(place.col == place.cols_n - 1)
    def _():
        own[:, z.cols :] = jnp.zeros((z.tall, z.wide_pad - z.cols, z.lanes), F32)


def send_sides(z, place, own, sends):
    for mine, halves in place.pairs(1):

        @pl.when(mine)
        def _(halves=halves):
            for send, (onward, _) in zip(sends, halves):
                first = z.cols if onward else 0
                for c in range(MARGIN):
                    send[c, 0 : z.tall, :] = own[:, first + c, :].astype(BF16)


def add_sides(z, place, whole, received):
    for mine, halves in place.pairs(1):
        for rim, (onward, there) in zip(received, halves):

            @pl.when(mine & there)
            def _(rim=rim, first=z.cols if onward else 0):
                for c in range(MARGIN):
                    whole[:, first + c, :] += rim[c].astype(F32)[0 : z.tall]


def is_equal(a, b):
    return (a == b).astype(F32).astype(BF16)


def cells_of(z, picture, pixels, spread, ready):
    channels, height, width = picture.shape

    def iota(shape, dim):
        return lax.broadcasted_iota(jnp.int32, shape, dim)

    shape = (channels * height, z.cell)
    line, entry = iota(shape, 0), iota(shape, 1)
    channel, image_row = lax.div(line, height), lax.rem(line, height)
    away = (
        (channel * STRIDE + lax.rem(image_row, STRIDE)) * STRIDE
        + lax.div(image_row, STRIDE) * z.cell
        - lax.div(entry, STRIDE) * STRIDE
    )
    shape = (width, z.cell)
    mine = (lax.rem(iota(shape, 0), STRIDE) == lax.rem(iota(shape, 1), STRIDE)).astype(F32)
    ready()
    turned = picture[...].reshape(channels * height, width).T
    high = turned.astype(BF16)
    rest = turned - high.astype(F32)
    middle = rest.astype(BF16)
    spread[0:width, :] = high
    spread[width : 2 * width, :] = middle
    spread[2 * width :, :] = (rest - middle.astype(F32)).astype(BF16)
    for i in range(z.rows):
        moved = jnp.dot(
            spread[...], is_equal(away, i * z.cell), preferred_element_type=F32
        )
        whole = (moved[0:width] + moved[width : 2 * width]) + moved[2 * width :]
        whole = (whole * mine).reshape(z.cols, STRIDE, z.cell)
        pixels[i * z.cols : (i + 1) * z.cols, :] = jnp.sum(whole, axis=1)


def first_kernel(
    z, grid, membrane, picture, source, own, *rest
):
    (*sends, pixels, dic, potential, atoms, tall_sum, spread, drawing, sems) = rest
    place = Place(*grid)
    early = [
        pltpu.make_async_copy(picture, drawing, sems.at[0]),
        pltpu.make_async_copy(membrane, potential, sems.at[1]),
    ]
    step = z.block
    copies = [
        pltpu.make_async_copy(
            source.at[:, low : low + step], dic.at[:, low : low + step], sems.at[2 + n]
        )
        for n, low in enumerate(range(0, z.patch, step))
    ]
    for copy in early + copies:
        copy.start()
    cells_of(z, drawing, pixels, spread, early[0].wait)
    early[1].wait()
    coding = shrink(potential[...]).astype(BF16)
    reconstruct(z, place, coding, dic, pixels, tall_sum, own, step, lambda i: copies[i].wait())
    send_sides(z, place, own, sends)
    owned = atoms.shape[0]
    atoms[...] = dic[pl.ds(pl.multiple_of(place.owner * owned, owned), owned), :]


def flip_kernel(z, dic, turned):
    size = 256
    shape = (size, size)
    same = is_equal(lax.broadcasted_iota(jnp.int32, shape, 0), lax.broadcasted_iota(jnp.int32, shape, 1))
    for i in range(0, z.patch, size):
        turned[i : i + size, :] = lax.dot_general(
            same, dic[:, i : i + size], (((1,), (1,)), ((), ())), preferred_element_type=F32
        ).astype(BF16)


def side_kernel(z, grid, own, from_even, from_odd, joined, even, odd, rim):
    place = Place(*grid)
    joined[...] = own[...]
    add_sides(z, place, joined, (from_even, from_odd))
    rim[MARGIN * z.wide :, :] = jnp.zeros((z.rim - MARGIN * z.wide, z.lanes), F32)
    for mine, halves in place.pairs(0):

        @pl.when(mine)
        def _(halves=halves):
            for send, (onward, _) in zip((even, odd), halves):
                first = z.rows if onward else 0
                for r in range(MARGIN):
                    start = MARGIN * z.cols + r * MARGIN
                    rim[r * z.cols : (r + 1) * z.cols, :] = joined[first + r, 0 : z.cols, :]
                    rim[start : start + MARGIN, :] = joined[first + r, z.cols : z.wide, :]
                send[...] = rim[...].astype(BF16)


def add_ends(z, place, whole, received, rim):
    for mine, halves in place.pairs(0):
        for block, (onward, there) in zip(received, halves):

            @pl.when(mine & there)
            def _(block=block, first=z.rows if onward else 0):
                rim[...] = block[...].astype(F32)
                for r in range(MARGIN):
                    start = MARGIN * z.cols + r * MARGIN
                    whole[first + r, 0 : z.cols, :] += rim[r * z.cols : (r + 1) * z.cols, :]
                    whole[first + r, z.cols : z.wide, :] += rim[start : start + MARGIN, :]


def windows_of(z, whole, wide_part, first_row, row_stride):
    for j in range(SPAN):
        part = whole[:, j : j + z.cols, 0 : z.cell].astype(BF16)
        for p in range(z.tall):
            wide_part[
                pl.ds(p * row_stride + first_row, z.cols), j * z.cell : (j + 1) * z.cell
            ] = part[p]


def sweep_kernel(
    z, grid, last, potential, joined, from_even, from_odd, pixels, dic, turned, *rest
):
    if last:
        new_potential, own, *sends, codes, tall_sum, whole, wide_part, rim = rest
    else:
        new_potential, own, *sends, tall_sum, whole, wide_part, rim = rest
    place = Place(*grid)
    whole[...] = joined[...]
    add_ends(z, place, whole, (from_even, from_odd), rim)
    windows_of(z, whole, wide_part, 0, z.cols)
    drive = None
    for i in range(SPAN):
        term = lax.dot_general(
            wide_part[i * z.cols : i * z.cols + z.sites, :],
            turned[i * z.band : (i + 1) * z.band, :],
            (((1,), (0,)), ((), ())),
            preferred_element_type=F32,
        )
        drive = term if drive is None else drive + term
    old = potential[...]
    updated = old + RELAXATION * (drive * z.scale + shrink(old) - old)
    active = shrink(updated)
    coding = active.astype(BF16)
    if last:
        new_potential[...] = active
        codes[...] = coding
    else:
        new_potential[...] = updated
    reconstruct(z, place, coding, dic, pixels, tall_sum, own, 2 * z.band)
    send_sides(z, place, own, sends)


def sort_kernel(z, grid, groups, codes, _, *messages):
    rows_n, cores_n, owned = groups
    span = z.atoms // rows_n
    src = lax.broadcasted_iota(jnp.int32, (span, span), 0)
    dst = lax.broadcasted_iota(jnp.int32, (span, span), 1)
    per_core = span // cores_n
    core, rem = lax.div(dst, per_core), lax.rem(dst, per_core)
    wanted = lax.div(rem, owned) * (owned * cores_n) + core * owned + lax.rem(rem, owned)
    order = is_equal(src, wanted)
    place = Place(*grid)
    for x, message in enumerate(messages):
        r = place.row ^ x if rows_n & (rows_n - 1) == 0 else (place.row - x) % rows_n
        block = codes[:, pl.ds(pl.multiple_of(r * span, span), span)]
        line = jnp.dot(block, order, preferred_element_type=F32).astype(BF16)
        for k in range(cores_n):
            message[k] = line[:, k * per_core : (k + 1) * per_core]


def turn_kernel(z, grid, groups, *rest):
    rows_n, cores_n, _ = groups
    stride = rows_n * cores_n * z.cols
    near, far, (across, codes) = rest[:rows_n], rest[rows_n : 2 * rows_n], rest[2 * rows_n :]
    place = Place(*grid)
    mine = place.core
    for x in range(rows_n):
        d = offset(place.row, x, rows_n)
        for k, message in ((mine, near[x]), (1 - mine, far[x])):
            lines = message[mine]
            for i in range(z.rows):
                at = i * stride + (d * cores_n + k) * z.cols
                codes[pl.ds(pl.multiple_of(at, z.cols), z.cols), :] = lines[
                    i * z.cols : (i + 1) * z.cols, :
                ]
    across[...] = codes[...].astype(F32).T.astype(BF16)


def pack_kernel(z, grid, own, from_even, from_odd, packed, joined, flat):
    joined[...] = own[...]
    add_sides(z, Place(*grid), joined, (from_even, from_odd))
    base = z.tall * z.cols
    flat[base:, :] = jnp.zeros((z.packed - base, z.lanes), F32)
    for p in range(z.tall):
        flat[p * z.cols : (p + 1) * z.cols, :] = joined[p, 0 : z.cols, :]
    for c in range(MARGIN):
        start = base + c * z.tall_pad
        flat[start : start + z.tall, :] = joined[:, z.cols + c, :]
    half = z.packed // 2
    packed[0 : z.packed, :] = flat[:, 0:128].astype(BF16)
    tail = z.cell - 128
    ends = jnp.concatenate([flat[0:half, 128 : z.cell], flat[half:, 128 : z.cell]], axis=1)
    packed[z.packed :, 0 : 2 * tail] = ends.astype(BF16)


def offset(at, step, n):
    return at ^ step if n & (n - 1) == 0 else (at + step) % n


def learn_half(z, grid, across, wide_part, stride, bands, outs, partial):
    count = z.rows * stride
    for n, i in enumerate(bands):
        term = jnp.dot(
            across, wide_part[i * stride : i * stride + count, :], preferred_element_type=F32
        )
        partial[:, n * z.band : (n + 1) * z.band] = (term * z.scale).astype(BF16)
    owned = outs[0].shape[0]
    place = Place(*grid)
    for step, out in enumerate(outs):
        at = offset(place.yx, step, len(outs))
        out[...] = partial[pl.ds(pl.multiple_of(at * owned, owned), owned), :]


def learn_kernel(z, grid, groups, yx_n, across, *rest):
    rows_n, cores_n, _ = groups
    members = rows_n * cores_n
    near, far, outs = rest[:rows_n], rest[rows_n : 2 * rows_n], rest[2 * rows_n :]
    outs, (wide_part, partial, flat, whole) = outs[:yx_n], outs[yx_n:]
    stride = members * z.cols
    base = z.tall * z.cols
    half = z.packed // 2
    tail = z.cell - 128
    place = Place(*grid)
    mine = place.core

    for x in range(rows_n):
        d = offset(place.row, x, rows_n)
        for k, block in ((mine, near[x]), (1 - mine, far[x])):
            flat[k, d, :, 0:128] = block[0 : z.packed, :].astype(F32)
            ends = block[z.packed :, :].astype(F32)
            flat[k, d, 0:half, 128 : z.cell] = ends[:, 0:tail]
            flat[k, d, half:, 128 : z.cell] = ends[:, tail : 2 * tail]
    for k in range(cores_n):
        for r in range(rows_n):
            d = r * cores_n + k
            for source, low, high, at in (
                (r, 0, z.tall, 0),
                (r - 1, z.rows, z.tall, 0),
                (r + 1, 0, MARGIN, z.rows),
            ):
                if not 0 <= source < rows_n:
                    continue
                n = high - low
                main = flat[k, source, low * z.cols : high * z.cols, :]
                main = main.reshape(n, z.cols, z.lanes)
                side = [
                    flat[k, source, base + c * z.tall_pad + low : base + c * z.tall_pad + high, :]
                    for c in range(MARGIN)
                ]
                if source == r:
                    whole[at : at + n, 0 : z.cols, :] = main
                    for c in range(MARGIN):
                        whole[at : at + n, z.cols + c, :] = side[c]
                else:
                    whole[at : at + n, 0 : z.cols, :] += main
                    for c in range(MARGIN):
                        whole[at : at + n, z.cols + c, :] += side[c]
            windows_of(z, whole, wide_part, d * z.cols, stride)
    learn_half(
        z, grid, across[...], wide_part, stride, range(SPAN // 2), outs, partial
    )


def rest_kernel(z, grid, stride, across, wide_part, *rest):
    *outs, partial = rest
    learn_half(
        z, grid, across[...], wide_part, stride, range(SPAN // 2, SPAN), outs, partial
    )


def half_finished(half, momentum, atoms, parts, updated, weights):
    lanes = pl.ds(half * weights.shape[1], weights.shape[1])
    learning = parts[0][...].astype(F32)
    for part in parts[1:]:
        learning = learning + part[...].astype(F32)
    momentum_out = DECAY * momentum[:, lanes] + learning
    updated[...] = momentum_out
    weight = atoms[:, lanes].astype(F32) + LEARNING * momentum_out
    weights[...] = weight
    return jnp.sum(weight * weight, axis=1, keepdims=True)


def early_kernel(momentum, atoms, *rest):
    *parts, updated, weights, power = rest
    total = half_finished(0, momentum, atoms, parts, updated, weights)
    power[...] = jnp.broadcast_to(total, power.shape)


def finish_kernel(z, first_updated, first_weights, first_power, momentum, atoms, *rest):
    *parts, new_dictionary, new_momentum, updated, weights, scaled, sems = rest
    width = z.patch // 2
    halves = [pl.ds(0, width), pl.ds(width, width)]
    copies = [
        pltpu.make_async_copy(first_updated, new_momentum.at[:, halves[0]], sems.at[0]),
        pltpu.make_async_copy(updated, new_momentum.at[:, halves[1]], sems.at[1]),
        pltpu.make_async_copy(scaled.at[0], new_dictionary.at[:, halves[0]], sems.at[2]),
        pltpu.make_async_copy(scaled.at[1], new_dictionary.at[:, halves[1]], sems.at[3]),
    ]
    copies[0].start()
    power = half_finished(1, momentum, atoms, parts, updated, weights)
    copies[1].start()
    norm = lax.rsqrt((first_power[:, 0:1] + power) * (1.0 / z.patch) + EPSILON)
    for h, source in enumerate((first_weights, weights)):
        scaled[h] = source[...] * norm
        copies[2 + h].start()
    for copy in copies:
        copy.wait()


def kept(x, space=pltpu.VMEM):
    return pltpu.with_memory_space_constraint(x, space)


def call(kernel, outs, inputs, scratch, far=0, leave=VMEM):
    specs = [HBM] * far + [VMEM] * (len(inputs) - far)
    placed = [kept(x, pltpu.HBM) for x in inputs[:far]] + [kept(x) for x in inputs[far:]]
    return pl.pallas_call(
        kernel,
        out_shape=outs,
        in_specs=specs,
        out_specs=[leave] * len(outs),
        scratch_shapes=scratch,
        compiler_params=PARAMS,
    )(*placed)


def shards(picture, membrane, dictionary, momentum):
    site_rows, site_cols, atom_count = membrane.shape
    z = Sizes(site_rows, site_cols, atom_count, dictionary.shape[1])
    rows_n, yx_n, cores_n = (lax.axis_size(a) for a in ("row", "yx", "core"))
    cols_n = yx_n * cores_n
    owned = momentum.shape[0]
    groups = (rows_n, cores_n, owned)
    members = rows_n * cores_n
    grid = (rows_n, cols_n)

    def met(block, axis, n, step):
        return lax.ppermute(block, axis, [(i, offset(i, step, n)) for i in range(n)])

    def swapped(axis, n, blocks):
        return [lax.ppermute(b, axis, route) for b, route in zip(blocks, partners(n))]

    def sideways(blocks):
        even, odd = partners(cols_n)
        near_rim = lax.ppermute(blocks[0], ("yx", "core"), even)
        far_rim = lax.ppermute(blocks[1], ("yx", "core"), odd)
        return [near_rim, far_rim]

    own_v = pltpu.VMEM((z.tall, z.wide_pad, z.lanes), F32)
    side_v = pltpu.VMEM((MARGIN, z.tall_pad, z.lanes), BF16)
    end_v = pltpu.VMEM((z.rim, z.lanes), BF16)
    rim_v = pltpu.VMEM((z.rim, z.lanes), F32)
    tall_v = pltpu.VMEM((z.tall * z.cols, z.band), F32)
    wide_v = pltpu.VMEM((z.tall * z.cols, z.band), BF16)
    flat_v = pltpu.VMEM((z.packed, z.lanes), F32)
    site_v = pltpu.VMEM((z.sites, atom_count), F32)
    outs = [own_v, side_v, side_v]

    own, *sides, pixels, dic, potential, atoms = call(
        functools.partial(first_kernel, z, grid),
        outs
        + [
            pltpu.VMEM((z.sites, z.cell), F32),
            pltpu.VMEM(dictionary.shape, BF16),
            site_v,
            pltpu.VMEM(momentum.shape, BF16),
        ],
        (membrane.reshape(z.sites, atom_count), picture, dictionary),
        [
            tall_v,
            pltpu.VMEM((3 * picture.shape[2], z.cell), BF16),
            pltpu.VMEM(picture.shape, F32),
            pltpu.SemaphoreType.DMA((2 + z.patch // z.block,)),
        ],
        far=3,
    )
    for repeat in range(SWEEPS):
        last = repeat == SWEEPS - 1
        sides = sideways(sides)
        if repeat == 0:
            (turned,) = call(
                functools.partial(flip_kernel, z),
                [pltpu.VMEM((z.patch, atom_count), BF16)],
                (dic,),
                [],
            )
        joined, *ends = call(
            functools.partial(side_kernel, z, grid), [own_v, end_v, end_v], (own, *sides), [rim_v]
        )
        ends = swapped("row", rows_n, ends)
        final = [
            site_v,
            *outs,
            pltpu.VMEM((z.sites, atom_count), BF16),
        ]
        potential, own, *rest = call(
            functools.partial(sweep_kernel, z, grid, last),
            final if last else [site_v] + outs,
            (potential, joined, *ends, pixels, dic, turned),
            [tall_v, own_v, wide_v, rim_v],
        )
        sides = rest[:2]
    final_codes = potential.reshape(membrane.shape)
    sides = sideways(sides)
    message_v = pltpu.VMEM((2, z.sites, atom_count // members), BF16)
    messages = call(
        functools.partial(sort_kernel, z, grid, groups),
        [message_v] * rows_n,
        (rest[2], sides[0]),
        [],
    )
    power = rows_n & (rows_n - 1) == 0

    def along_row(blocks):
        return [blocks[0]] + [
            met(block, "row", rows_n, x if power else rows_n - x)
            for x, block in enumerate(blocks[1:], 1)
        ]

    def across_chip(blocks):
        return [met(block, "core", 2, 1) for block in blocks]

    near_codes = along_row(messages)
    far_codes = across_chip(near_codes)
    (packed,) = call(
        functools.partial(pack_kernel, z, grid),
        [pltpu.VMEM((z.packed * 3 // 2, 128), BF16)],
        (own, *sides),
        [own_v, flat_v],
    )

    near = along_row([packed] * rows_n)
    far = across_chip(near)
    stride = members * z.cols
    group_atoms = atom_count // members
    half_v = pltpu.VMEM((owned, z.patch // 2), BF16)
    partial_v = pltpu.VMEM((group_atoms, z.patch // 2), BF16)
    (across,) = call(
        functools.partial(turn_kernel, z, grid, groups),
        [pltpu.VMEM((group_atoms, members * z.sites), BF16)],
        (*near_codes, *far_codes),
        [pltpu.VMEM((members * z.sites, group_atoms), BF16)],
    )
    *first_half, wide_part = call(
        functools.partial(learn_kernel, z, grid, groups, yx_n),
        [half_v] * yx_n + [pltpu.VMEM((z.tall * stride, z.band), BF16)],
        (across, *near, *far),
        [
            partial_v,
            pltpu.VMEM((cores_n, rows_n, z.packed, z.lanes), F32),
            own_v,
        ],
    )
    other_half = call(
        functools.partial(rest_kernel, z, grid, stride),
        [half_v] * yx_n,
        (across, wide_part),
        [partial_v],
    )
    parts = [
        [block if step == 0 else met(block, "yx", yx_n, step) for step, block in enumerate(half)]
        for half in (first_half, other_half)
    ]
    wide_half = (owned, z.patch // 2)
    early = call(
        early_kernel,
        [pltpu.VMEM(s, F32) for s in (wide_half, wide_half, (owned, 128))],
        (momentum, atoms, *parts[0]),
        [],
    )
    new_dictionary, new_momentum = call(
        functools.partial(finish_kernel, z),
        [jax.ShapeDtypeStruct(momentum.shape, F32)] * 2,
        (*early, momentum, atoms, *parts[1]),
        [
            pltpu.VMEM(wide_half, F32),
            pltpu.VMEM(wide_half, F32),
            pltpu.VMEM((2,) + wide_half, F32),
            pltpu.SemaphoreType.DMA((4,)),
        ],
        leave=HBM,
    )
    return (final_codes, new_dictionary, new_momentum)


def solution(mesh):
    rows_n, cols_n = (mesh.shape["row"], mesh.shape["col"])
    split = Mesh(mesh.devices.reshape(rows_n, cols_n // 2, 2), ("row", "yx", "core"))
    col = ("yx", "core")
    return jax.shard_map(
        shards,
        mesh=split,
        in_specs=(P(None, "row", col), P("row", col, None), P(), P(("row",) + col, None)),
        out_specs=(P("row", col, None), P(("row",) + col, None), P(("row",) + col, None)),
        check_vma=False,
    )
```
